32 devices in a mesh: fsdp: 16 (over z, y, core), seq: 2 (over x).
Axes of the slice: x: 2, y: 2, z: 4, core: 2. Of those that a mesh axis runs over, the one named last changes fastest.
Arguments:
- block_input: bfloat16 [2, 16, 1024, 1024], P(None, 'fsdp', 'seq'), may hold values from -6 to 6
- output_grad: bfloat16 [2, 16, 1024, 1024], P(None, 'fsdp', 'seq'), may hold values from -6 to 6
- adapter_ids: int32 [2, 16], P(None, 'fsdp'), may hold values from 0 to 7
- in_weight: bfloat16 [1024, 3072], P('fsdp'), may hold values from -0.1875 to 0.1875
- out_weight: bfloat16 [1024, 1024], P('fsdp'), may hold values from -0.1875 to 0.1875
- gate_weight: bfloat16 [1024, 4608], P('fsdp'), may hold values from -0.1875 to 0.1875
- up_weight: bfloat16 [1024, 4608], P('fsdp'), may hold values from -0.1875 to 0.1875
- down_weight: bfloat16 [4608, 1024], P('fsdp'), may hold values from -0.09375 to 0.09375
- conv_weight: bfloat16 [3, 1024], replicated, may hold values from -3.5 to 3.5
- first_gain: bfloat16 [1024], replicated, may hold values from 0.099609375 to 1.8984375
- second_gain: bfloat16 [1024], replicated, may hold values from 0.099609375 to 1.8984375
- infirst_adapter: bfloat16 [1024, 128], replicated, may hold values from -0.1875 to 0.1875
- insecond_adapter: bfloat16 [128, 3072], replicated, may hold values from -1.5 to 1.5
- outfirst_adapter: bfloat16 [1024, 128], replicated, may hold values from -0.1875 to 0.1875
- outsecond_adapter: bfloat16 [128, 1024], replicated, may hold values from -1.5 to 1.5
- gatefirst_adapter: bfloat16 [1024, 128], replicated, may hold values from -0.1875 to 0.1875
- gatesecond_adapter: bfloat16 [128, 4608], replicated, may hold values from -1.5 to 1.5
- upfirst_adapter: bfloat16 [1024, 128], replicated, may hold values from -0.1875 to 0.1875
- upsecond_adapter: bfloat16 [128, 4608], replicated, may hold values from -1.5 to 1.5
- downfirst_adapter: bfloat16 [4608, 128], replicated, may hold values from -0.09375 to 0.09375
- downsecond_adapter: bfloat16 [128, 1024], replicated, may hold values from -1.5 to 1.5
Outputs:
- block_output: bfloat16 [2, 16, 1024, 1024], P(None, 'fsdp', 'seq')
- input_grad: bfloat16 [2, 16, 1024, 1024], P(None, 'fsdp', 'seq')
- infirst_grad: float32 [1024, 128], replicated
- insecond_grad: float32 [128, 3072], replicated
- outfirst_grad: float32 [1024, 128], replicated
- outsecond_grad: float32 [128, 1024], replicated
- gatefirst_grad: float32 [1024, 128], replicated
- gatesecond_grad: float32 [128, 4608], replicated
- upfirst_grad: float32 [1024, 128], replicated
- upsecond_grad: float32 [128, 4608], replicated
- downfirst_grad: float32 [4608, 128], replicated
- downsecond_grad: float32 [128, 1024], replicated
The draws below stay inside these ranges and needn't reach their ends.
All inputs are finite; a program needn't handle non-finite values.
Results may differ from the reference program's by a relative error of at most 0.012.
The reference program's roundings to bfloat16 on the way count: a program that leaves them out, or rounds other values in their place, can miss the bound.
Values may be sent and summed in bfloat16 or wider, within the bound.
A program may use at most 256 MiB of HBM per device.

```python
import jax
import jax.numpy as jnp
from jax import lax

D = 1024
FF = 4608
KERNEL = 3
NA = 8
R = 16
LENGTH = 1024
MICRO = 2
SEQS = 16


def set_ends(array, key, smallest, high):
    spot = [jax.random.randint(jax.random.fold_in(key, axis), (), 0, length) for axis, length in enumerate(array.shape)]
    longest = array.shape.index(max(array.shape))
    next_to = spot[:longest] + [(spot[longest] + 1) % array.shape[longest]] + spot[longest + 1:]
    return array.at[tuple(spot)].set(smallest).at[tuple(next_to)].set(high)


def spiked(entries, key, source, target, parts, factor):
    def block_of(dim):
        return (jnp.arange(entries.shape[dim]) // (entries.shape[dim] // parts)).reshape((-1,) + (1,) * (entries.ndim - 1 - dim))

    near = jax.random.permutation(key, parts)[block_of(target)]
    far = (block_of(target) + parts // 2) % parts
    return jnp.where((block_of(source) == near) | (block_of(source) == far), factor * entries, entries)


def block_levels(own_key, extent, split, smallest, high):
    gain, own = 1.0, jax.random.fold_in(own_key, 6)
    for axis_at, parts in split:
        draws = jnp.exp(jax.random.uniform(jax.random.fold_in(own, axis_at), (parts,), jnp.float32, smallest / len(split), high / len(split)))
        gain = gain * jnp.repeat(draws, extent[axis_at] // parts).reshape([-1 if axis == axis_at else 1 for axis in range(len(extent))])
    return gain


def scatter_about(key, shape, deviation, bound, pieces=(), held_as=jnp.bfloat16):
    gain = block_levels(key, shape, pieces, -0.22, 0.18) if pieces else 1.0
    array = jax.random.normal(key, shape, jnp.float32) * deviation * gain
    return jnp.minimum(jnp.maximum(array, -bound), bound).astype(held_as)


def heavy_noise(own_key, extent, deviation, most, cuts, heavy, kind=jnp.bfloat16):
    entries = deviation * jax.random.normal(own_key, extent, jnp.float32)
    if cuts:
        entries = entries * block_levels(own_key, extent, cuts, -0.22, 0.18)
    return jnp.clip(spiked(entries, jax.random.fold_in(own_key, 3), *heavy), -most, most).astype(kind)


def setup_inputs(seed: int = 0) -> dict:
    key_list = jax.random.split(jax.random.key(seed), 22)
    return {
        "block_input": scatter_about(key_list[0], (MICRO, SEQS, LENGTH, D), 1.0, 6.0, ((1, 16), (2, 2))),
        "output_grad": heavy_noise(key_list[1], (MICRO, SEQS, LENGTH, D), 1.0, 6.0, ((1, 16), (2, 2)), (1, 3, 16, 2.0)),
        "adapter_ids": set_ends(jax.random.randint(key_list[2], (MICRO, SEQS), 0, NA), jax.random.fold_in(key_list[2], 1), 0, NA - 1).astype(jnp.int32),
        "in_weight": scatter_about(key_list[3], (D, 3 * D), D ** -0.5, 0.1875, ((0, 16),)),
        "out_weight": scatter_about(key_list[4], (D, D), D ** -0.5, 0.1875, ((0, 16),)),
        "gate_weight": scatter_about(key_list[5], (D, FF), D ** -0.5, 0.1875, ((0, 16),)),
        "up_weight": scatter_about(key_list[6], (D, FF), D ** -0.5, 0.1875, ((0, 16),)),
        "down_weight": scatter_about(key_list[7], (FF, D), FF ** -0.5, 0.09375, ((0, 16),)),
        "conv_weight": scatter_about(key_list[8], (KERNEL, D), KERNEL ** -0.5, 3.5),
        "first_gain": jnp.clip(1.0 + 0.18 * jax.random.normal(key_list[9], (D,), jnp.float32), 0.099609375, 1.8984375).astype(jnp.bfloat16),
        "second_gain": jnp.clip(1.0 + 0.18 * jax.random.normal(key_list[10], (D,), jnp.float32), 0.099609375, 1.8984375).astype(jnp.bfloat16),
        "infirst_adapter": scatter_about(key_list[11], (D, NA * R), D ** -0.5, 0.1875),
        "insecond_adapter": scatter_about(key_list[12], (NA * R, 3 * D), R ** -0.5, 1.5),
        "outfirst_adapter": scatter_about(key_list[13], (D, NA * R), D ** -0.5, 0.1875),
        "outsecond_adapter": scatter_about(key_list[14], (NA * R, D), R ** -0.5, 1.5),
        "gatefirst_adapter": scatter_about(key_list[15], (D, NA * R), D ** -0.5, 0.1875),
        "gatesecond_adapter": scatter_about(key_list[16], (NA * R, FF), R ** -0.5, 1.5),
        "upfirst_adapter": scatter_about(key_list[17], (D, NA * R), D ** -0.5, 0.1875),
        "upsecond_adapter": scatter_about(key_list[18], (NA * R, FF), R ** -0.5, 1.5),
        "downfirst_adapter": scatter_about(key_list[19], (FF, NA * R), FF ** -0.5, 0.09375),
        "downsecond_adapter": scatter_about(key_list[20], (NA * R, D), R ** -0.5, 1.5),
    }


EPSILON = 1e-05
ADAPTER_SCALE = 0.5

@jax.custom_vjp
def low(v):
    return lax.optimization_barrier(v.astype(jnp.bfloat16)).astype(jnp.float32)

@jax.custom_vjp
def low_back(v):
    return v

def low_keep(v):
    return (low(v), None)

def low_pass(kept, grad):
    return (grad,)

def back_keep(v):
    return (v, None)

def back_low(kept, grad):
    return (low(grad),)
low.defvjp(low_keep, low_pass)
low_back.defvjp(back_keep, back_low)

def matmul(left_side, right_side):
    return jnp.dot(left_side, right_side, preferred_element_type=jnp.float32, precision=lax.Precision.HIGHEST)

def rms_scale(values, gain_vector):
    inverse = lax.rsqrt(lax.optimization_barrier(jnp.mean(values * values, axis=-1, keepdims=True)) + EPSILON)
    return values * inverse * gain_vector

def project(inputs, weight, first_map, second_map, select):
    reduced = low(low_back(matmul(inputs, first_map))) * select
    return low_back(matmul(inputs, weight) + ADAPTER_SCALE * matmul(reduced, second_map))

def causal_conv(values, kernel):
    count_rows = values.shape[0]
    padded = jnp.concatenate([jnp.zeros((2, values.shape[1]), jnp.float32), values], axis=0)
    return kernel[0] * padded[:count_rows] + kernel[1] * padded[1:count_rows + 1] + kernel[2] * padded[2:]

def forward(frozen, adapters, inputs, select):
    weight_in, weight_out, weight_gate, weight_up, weight_down, kernel, gain_first, gain_second = frozen
    normed = low(rms_scale(inputs, gain_first))
    mixed_in = project(normed, weight_in, adapters[0], adapters[1], select)
    gated_values = mixed_in[:, :D] * mixed_in[:, 2 * D:]
    mixer_out = low(mixed_in[:, D:2 * D] * causal_conv(gated_values, kernel))
    after_mixer = inputs + project(mixer_out, weight_out, adapters[2], adapters[3], select)
    second = low(rms_scale(after_mixer, gain_second))
    gate_value = project(second, weight_gate, adapters[4], adapters[5], select)
    up_value = project(second, weight_up, adapters[6], adapters[7], select)
    hidden = low(jax.nn.silu(gate_value) * up_value)
    return after_mixer + project(hidden, weight_down, adapters[8], adapters[9], select)

def reference(block_input, output_grad, adapter_ids, in_weight, out_weight, gate_weight, up_weight, down_weight, conv_weight, first_gain, second_gain, infirst_adapter, insecond_adapter, outfirst_adapter, outsecond_adapter, gatefirst_adapter, gatesecond_adapter, upfirst_adapter, upsecond_adapter, downfirst_adapter, downsecond_adapter):
    frozen = tuple((member.astype(jnp.float32) for member in (in_weight, out_weight, gate_weight, up_weight, down_weight, conv_weight, first_gain, second_gain)))
    adapters = tuple((member.astype(jnp.float32) for member in (infirst_adapter, insecond_adapter, outfirst_adapter, outsecond_adapter, gatefirst_adapter, gatesecond_adapter, upfirst_adapter, upsecond_adapter, downfirst_adapter, downsecond_adapter)))
    inputs = block_input.astype(jnp.float32).reshape(MICRO * SEQS, LENGTH, D)
    cotangents = output_grad.astype(jnp.float32).reshape(MICRO * SEQS, LENGTH, D)
    identities = adapter_ids.reshape(MICRO * SEQS).astype(jnp.int32)
    columns = jnp.arange(NA * R, dtype=jnp.int32) // R

    def one_sequence(totals, sliced):
        values, cotangent, identity = sliced
        select = (columns == identity).astype(jnp.float32)[None, :]

        def wrapped(points, params):
            return forward(frozen, params, points, select)
        outcome, pullback = jax.vjp(wrapped, values, adapters)
        grad_values, grad_params = pullback(cotangent)
        return (jax.tree.map(jnp.add, totals, grad_params), (outcome.astype(jnp.bfloat16), grad_values.astype(jnp.bfloat16)))
    initial = jax.tree.map(jnp.zeros_like, adapters)
    totals, (outcomes, input_grads) = lax.scan(one_sequence, initial, (inputs, cotangents, identities))
    block_output = outcomes.reshape(MICRO, SEQS, LENGTH, D)
    input_grad = input_grads.reshape(MICRO, SEQS, LENGTH, D)
    return (block_output, input_grad, totals[0], totals[1], totals[2], totals[3], totals[4], totals[5], totals[6], totals[7], totals[8], totals[9])
```

```python
import functools

import jax
import jax.numpy as jnp
from jax import lax
from jax.experimental import pallas as pl
from jax.experimental.pallas import tpu as pltpu
from jax.sharding import PartitionSpec as P

R = 16


EPSILON = 1e-05
ADAPTER_SCALE = 0.5
MESH = pl.DeviceIdType.MESH
BF16 = jnp.bfloat16
F32 = jnp.float32


class Ring:
    def __init__(self, fsdp_size):
        self.count = fsdp_size // 2
        self.me = lax.axis_index("fsdp")
        self.core = lax.rem(self.me, 2)
        chip = self.me // 2
        if fsdp_size == 16:
            z, y = chip // 2, lax.rem(chip, 2)
            self.place = y * z + (1 - y) * (7 - z)
        else:
            self.place = chip
        self.grid = fsdp_size == 16
        x = lax.axis_index("seq")
        self.role = lax.rem(x, 2)
        self.to_next = {"fsdp": self.device(lax.rem(self.place + 1, self.count))}
        self.to_prev = {"fsdp": self.device(lax.rem(self.place + self.count - 1, self.count))}
        self.to_core = {"fsdp": self.me + 1 - 2 * self.core}
        self.to_seq = {"seq": x + 1 - 2 * self.role}

    def device(self, place):
        if self.grid:
            y = 1 - place // 4
            z = y * place + (1 - y) * (7 - place)
            return (z * 2 + y) * 2 + self.core
        return place * 2 + self.core

    def at_step(self, direction, step):
        if direction == 0:
            return self.device(lax.rem(self.place + self.count - step, self.count))
        return self.device(lax.rem(self.place + step, self.count))

    def greet(self):
        barrier = pltpu.get_barrier_semaphore()
        for device in (self.to_next, self.to_prev, self.to_core, self.to_seq):
            pl.semaphore_signal(barrier, inc=1, device_id=device, device_id_type=MESH)
        pl.semaphore_wait(barrier, 4)


class Unit:
    def __init__(self, ring, number, spot, sems):
        self.ring, self.number, self.spot = ring, number, spot
        self.send, self.ring_sem, self.seq_sem, self.core_sem = sems
        half = ring.count // 2
        self.reach = (half, ring.count - 1 - half) if number % 2 == 0 else (ring.count - 1 - half, half)
        self.steps = max(self.reach)
        self.sent = []

    def push(self, spot, sem, device):
        copy = pltpu.make_async_remote_copy(
            src_ref=spot, dst_ref=spot, send_sem=self.send.at[self.number, len(self.sent)],
            recv_sem=sem, device_id=device, device_id_type=MESH,
        )
        copy.start()
        self.sent.append(copy)

    def arrived(self, spot, sem):
        pltpu.make_async_remote_copy(
            src_ref=spot, dst_ref=spot, send_sem=self.send.at[self.number, 0],
            recv_sem=sem, device_id=self.ring.to_next, device_id_type=MESH,
        ).wait_recv()

    def own(self):
        ring, n = self.ring, self.number
        for slot, third in ((0, ring.role), (1, 2)):
            spot = self.spot(third, ring.me)
            self.push(spot, self.ring_sem.at[n, slot, 0], ring.to_next)
            self.push(spot, self.ring_sem.at[n, slot, ring.count - 2], ring.to_prev)
        for third in (ring.role, 1 - ring.role, 2):
            self.push(self.spot(third, ring.me), self.core_sem.at[n, third, 0], ring.to_core)

    def legs(self, step):
        for direction, reach in enumerate(self.reach):
            if step <= reach:
                lane = step - 1 if direction == 0 else self.ring.count - 1 - step
                yield direction, reach, lane, self.ring.at_step(direction, step)

    def relay(self, step):
        ring, n = self.ring, self.number
        for direction, reach, lane, owner in self.legs(step):
            for slot, third in ((0, ring.role), (1, 2)):
                spot = self.spot(third, owner)
                self.arrived(spot, self.ring_sem.at[n, slot, lane])
                if step < reach:
                    onward = lane + 1 - 2 * direction
                    self.push(spot, self.ring_sem.at[n, slot, onward], (ring.to_next, ring.to_prev)[direction])
                if slot == 0:
                    self.push(spot, self.seq_sem.at[n, lane], ring.to_seq)
                self.push(spot, self.core_sem.at[n, third, 1 + lane], ring.to_core)

    def relay_seq(self, step):
        ring, n = self.ring, self.number
        third = 1 - ring.role
        for _, _, lane, owner in self.legs(step):
            spot = self.spot(third, owner)
            self.arrived(spot, self.seq_sem.at[n, lane])
            self.push(spot, self.core_sem.at[n, third, 1 + lane], ring.to_core)

    def collect(self):
        ring, n = self.ring, self.number
        for third in range(3):
            for lane in range(ring.count):
                self.arrived(self.spot(third, ring.me), self.core_sem.at[n, third, lane])

    def drain(self):
        for copy in self.sent:
            copy.wait_send()


def timeline(units, lag=2):
    entries = []
    for k, unit in enumerate(units):
        entries.append((k, 0, unit.own))
        for step in range(1, unit.steps + 1):
            entries.append((k + step, 1, functools.partial(unit.relay, step)))
            entries.append((k + step + lag, 2, functools.partial(unit.relay_seq, step)))
    return [entry[2] for entry in sorted(entries, key=lambda entry: entry[:2])]


def sem_shapes(units, count):
    sends = 4 + 3 + 2 * (count - 1) * 2 + (count - 1) * 2
    return [
        pltpu.SemaphoreType.DMA((units, sends)),
        pltpu.SemaphoreType.DMA((units, 2, count - 1)),
        pltpu.SemaphoreType.DMA((units, count - 1)),
        pltpu.SemaphoreType.DMA((units, 3, count)),
    ]


GU_UNITS = 3


def spots(in_all, out_all, gu_all, down_all, fsdp_size):
    rows = in_all.shape[0] // fsdp_size
    down_rows = down_all.shape[0] // fsdp_size
    part = in_all.shape[1] // 3
    out_x = 3 * out_all.shape[1] // 8

    def in_spot(third, owner):
        return in_all.at[pl.ds(owner * rows, rows), pl.ds(pl.multiple_of(third * part, 128), part)]

    def out_spot(third, owner):
        width = out_x if not isinstance(third, int) or third < 2 else out_all.shape[1] - 2 * out_x
        return out_all.at[pl.ds(owner * rows, rows), pl.ds(pl.multiple_of(third * out_x, 128), width)]

    def down_spot(third, owner):
        size = down_rows // 3
        return down_all.at[pl.ds(owner * down_rows + third * size, size), :]

    def gu_spot(chunk, third, owner):
        size = gu_all.shape[2] // GU_UNITS // 3
        start = pl.multiple_of((chunk * 3 + third) * size, 128)
        return gu_all.at[:, pl.ds(owner * rows, rows), pl.ds(start, size)]

    return [in_spot, out_spot, down_spot] + [functools.partial(gu_spot, k) for k in range(GU_UNITS)]


def gather_kernel(fsdp_size, *refs):
    in_own, out_own, gate_own, up_own, down_own, in_all, out_all, gu_all, down_all = refs[:9]
    sems, local_sem, held = refs[9:13], refs[13], refs[14:]
    ring = Ring(fsdp_size)
    rows, down_rows = in_own.shape[0], down_own.shape[0]
    mine = pl.ds(ring.me * rows, rows)
    moves = [
        (in_own, held[0], in_all.at[mine, :]),
        (out_own, held[1], out_all.at[mine, :]),
        (gate_own, held[2], gu_all.at[0, mine, :]),
        (up_own, held[3], gu_all.at[1, mine, :]),
        (down_own, held[4], down_all.at[pl.ds(ring.me * down_rows, down_rows), :]),
    ]
    inward = [pltpu.make_async_copy(a, b, local_sem.at[0, k]) for k, (a, b, _) in enumerate(moves)]
    outward = [pltpu.make_async_copy(b, c, local_sem.at[1, k]) for k, (_, b, c) in enumerate(moves)]
    for copy in inward:
        copy.start()
    ring.greet()
    for first, second in zip(inward, outward):
        first.wait()
        second.start()
    for copy in outward:
        copy.wait()
    units = [
        Unit(ring, k, spot, sems)
        for k, spot in enumerate(spots(in_all, out_all, gu_all, down_all, fsdp_size))
    ]
    for action in timeline(units):
        action()
    for unit in units:
        unit.collect()
    for unit in units:
        unit.drain()


def gather_all(fsdp_size, in_weight, out_weight, gate_weight, up_weight, down_weight):
    anywhere = pl.BlockSpec(memory_space=pl.ANY)
    rows, features = fsdp_size * in_weight.shape[0], out_weight.shape[1]
    own = (in_weight, out_weight, gate_weight, up_weight, down_weight)
    return pl.pallas_call(
        functools.partial(gather_kernel, fsdp_size),
        out_shape=(
            jax.ShapeDtypeStruct((rows, in_weight.shape[1]), BF16),
            jax.ShapeDtypeStruct((rows, features), BF16),
            jax.ShapeDtypeStruct((2, rows, gate_weight.shape[1]), BF16),
            jax.ShapeDtypeStruct((fsdp_size * down_weight.shape[0], features), BF16),
        ),
        in_specs=[anywhere] * 5,
        out_specs=(anywhere,) * 4,
        scratch_shapes=sem_shapes(3 + GU_UNITS, fsdp_size // 2)
        + [pltpu.SemaphoreType.DMA((2, 5))]
        + [pltpu.VMEM(member.shape, BF16) for member in own],
        compiler_params=pltpu.CompilerParams(collective_id=0, has_side_effects=True),
    )(*own)


def from_behind(block, axis, distance):
    devices = range(lax.axis_size(axis))
    route = [(i - distance, i) for i in devices if i - distance in devices]
    return lax.ppermute(block, axis, route)


def forward_dot(left_side, right_side):
    return jnp.dot(left_side, right_side, preferred_element_type=jnp.float32)


def against_dot(left_side, right_side):
    return lax.dot_general(
        left_side, right_side, (((1,), (1,)), ((), ())), preferred_element_type=jnp.float32
    )


def outer_dot(left_side, right_side):
    return lax.dot_general(
        left_side, right_side, (((0,), (0,)), ((), ())), preferred_element_type=jnp.float32
    )


def adapted(inputs, weight, first_map, second_map, select):
    reduced = forward_dot(inputs, first_map).astype(jnp.bfloat16) * select
    result = forward_dot(inputs, weight) + ADAPTER_SCALE * forward_dot(reduced, second_map)
    return (result, reduced)


def adapted_back(grad_low, inputs, reduced, weight, first_map, second_map, select):
    grad_second = ADAPTER_SCALE * outer_dot(reduced, grad_low)
    grad_reduced = (ADAPTER_SCALE * against_dot(grad_low, second_map) * select).astype(jnp.bfloat16)
    grad_first = outer_dot(inputs, grad_reduced)
    grad_inputs = against_dot(grad_low, weight) + against_dot(grad_reduced, first_map)
    return (grad_inputs, grad_first, grad_second)


def rms_parts(values):
    inverse = lax.rsqrt(jnp.mean(values * values, axis=-1, keepdims=True) + EPSILON)
    return (inverse, values * inverse)


def rms_back(grad_normed, gain_vector, inverse, unit_rows):
    scaled = grad_normed * gain_vector
    return inverse * (scaled - unit_rows * jnp.mean(scaled * unit_rows, axis=-1, keepdims=True))


def per_device(
    block_input,
    output_grad,
    adapter_ids,
    in_weight,
    out_weight,
    gate_weight,
    up_weight,
    down_weight,
    conv_weight,
    first_gain,
    second_gain,
    infirst_adapter,
    insecond_adapter,
    outfirst_adapter,
    outsecond_adapter,
    gatefirst_adapter,
    gatesecond_adapter,
    upfirst_adapter,
    upsecond_adapter,
    downfirst_adapter,
    downsecond_adapter,
):
    batches, seq_count, local_len, features = block_input.shape
    row_count = seq_count * local_len
    adapters = (
        infirst_adapter,
        insecond_adapter,
        outfirst_adapter,
        outsecond_adapter,
        gatefirst_adapter,
        gatesecond_adapter,
        upfirst_adapter,
        upsecond_adapter,
        downfirst_adapter,
        downsecond_adapter,
    )
    slot_count = infirst_adapter.shape[1]
    kernel = conv_weight.astype(jnp.float32)
    gain_first = first_gain.astype(jnp.float32)
    gain_second = second_gain.astype(jnp.float32)
    owners = lax.broadcasted_iota(jnp.int32, (1, 1, slot_count), 2) // R
    totals = [jnp.zeros(member.shape, jnp.float32) for member in adapters]
    outputs = []
    input_grads = []
    weight_in, weight_out, weight_gate_up, weight_down = gather_all(
        lax.axis_size("fsdp"), in_weight, out_weight, gate_weight, up_weight, down_weight
    )
    weight_gate, weight_up = weight_gate_up[0], weight_gate_up[1]
    for batch_index in range(batches):
        inputs = block_input[batch_index].reshape(row_count, features).astype(jnp.float32)
        matches = owners == adapter_ids[batch_index][:, None, None]
        select = (
            jnp.broadcast_to(matches, (seq_count, local_len, slot_count))
            .reshape(row_count, slot_count)
            .astype(jnp.bfloat16)
        )
        inverse_first, unit_first = rms_parts(inputs)
        normed = (unit_first * gain_first).astype(jnp.bfloat16)
        mixed_in, low_in = adapted(normed, weight_in, adapters[0], adapters[1], select)
        first_part = mixed_in[:, :features]
        middle_part = mixed_in[:, features : 2 * features]
        last_part = mixed_in[:, 2 * features :]
        gated_values = (first_part * last_part).reshape(seq_count, local_len, features)
        rim_rows = from_behind(gated_values[:, local_len - 2 :, :], "seq", 1)
        extended = jnp.concatenate([rim_rows, gated_values], axis=1)
        conv_out = (
            kernel[0] * extended[:, :local_len]
            + kernel[1] * extended[:, 1 : local_len + 1]
            + kernel[2] * extended[:, 2:]
        ).reshape(row_count, features)
        mixer_out = (middle_part * conv_out).astype(jnp.bfloat16)
        branch, low_out = adapted(mixer_out, weight_out, adapters[2], adapters[3], select)
        after_mixer = inputs + branch
        inverse_second, unit_second = rms_parts(after_mixer)
        second = (unit_second * gain_second).astype(jnp.bfloat16)
        gate_value, low_gate = adapted(second, weight_gate, adapters[4], adapters[5], select)
        up_value, low_up = adapted(second, weight_up, adapters[6], adapters[7], select)
        sigmoid_gate = jax.nn.sigmoid(gate_value)
        activated = gate_value * sigmoid_gate
        hidden = (activated * up_value).astype(jnp.bfloat16)
        down_value, low_down = adapted(hidden, weight_down, adapters[8], adapters[9], select)
        outputs.append(
            (after_mixer + down_value).astype(jnp.bfloat16).reshape(seq_count, local_len, features)
        )
        cotangent = output_grad[batch_index].reshape(row_count, features)
        grad_hidden, grad_first, grad_second = adapted_back(
            cotangent, hidden, low_down, weight_down, adapters[8], adapters[9], select
        )
        totals[8] = totals[8] + grad_first
        totals[9] = totals[9] + grad_second
        grad_gate = (
            grad_hidden * up_value * sigmoid_gate * (1.0 + gate_value * (1.0 - sigmoid_gate))
        ).astype(jnp.bfloat16)
        grad_upper = (grad_hidden * activated).astype(jnp.bfloat16)
        back_gate, grad_first, grad_second = adapted_back(
            grad_gate, second, low_gate, weight_gate, adapters[4], adapters[5], select
        )
        totals[4] = totals[4] + grad_first
        totals[5] = totals[5] + grad_second
        back_upper, grad_first, grad_second = adapted_back(
            grad_upper, second, low_up, weight_up, adapters[6], adapters[7], select
        )
        totals[6] = totals[6] + grad_first
        totals[7] = totals[7] + grad_second
        grad_after = cotangent.astype(jnp.float32) + rms_back(
            back_gate + back_upper, gain_second, inverse_second, unit_second
        )
        grad_mixer, grad_first, grad_second = adapted_back(
            grad_after.astype(jnp.bfloat16),
            mixer_out,
            low_out,
            weight_out,
            adapters[2],
            adapters[3],
            select,
        )
        totals[2] = totals[2] + grad_first
        totals[3] = totals[3] + grad_second
        grad_conv = (grad_mixer * middle_part).reshape(seq_count, local_len, features)
        rim_back = from_behind(grad_conv[:, :2, :], "seq", -1)
        beyond = jnp.concatenate([grad_conv, rim_back], axis=1)
        grad_gated = (
            kernel[2] * beyond[:, :local_len]
            + kernel[1] * beyond[:, 1 : local_len + 1]
            + kernel[0] * beyond[:, 2:]
        ).reshape(row_count, features)
        grad_mixed = jnp.concatenate(
            [grad_gated * last_part, grad_mixer * conv_out, grad_gated * first_part], axis=1
        ).astype(jnp.bfloat16)
        grad_normed, grad_first, grad_second = adapted_back(
            grad_mixed, normed, low_in, weight_in, adapters[0], adapters[1], select
        )
        totals[0] = totals[0] + grad_first
        totals[1] = totals[1] + grad_second
        grad_input = grad_after + rms_back(grad_normed, gain_first, inverse_first, unit_first)
        input_grads.append(grad_input.astype(jnp.bfloat16).reshape(seq_count, local_len, features))
    summed = lax.psum(
        tuple(t.astype(BF16) for t in (
            totals[0],
            totals[1],
            totals[2],
            totals[3],
            totals[4],
            totals[5],
            totals[6],
            totals[7],
            totals[8],
            totals[9],
        )),
        ("fsdp", "seq"),
    )
    return (
        jnp.stack(outputs),
        jnp.stack(input_grads),
        summed[0].astype(F32),
        summed[1].astype(F32),
        summed[2].astype(F32),
        summed[3].astype(F32),
        summed[4].astype(F32),
        summed[5].astype(F32),
        summed[6].astype(F32),
        summed[7].astype(F32),
        summed[8].astype(F32),
        summed[9].astype(F32),
    )


def solution(mesh):
    return jax.shard_map(
        per_device,
        mesh=mesh,
        in_specs=(
            P(None, "fsdp", "seq", None),
            P(None, "fsdp", "seq", None),
            P(None, "fsdp"),
            P("fsdp", None),
            P("fsdp", None),
            P("fsdp", None),
            P("fsdp", None),
            P("fsdp", None),
            P(),
            P(),
            P(),
            P(),
            P(),
            P(),
            P(),
            P(),
            P(),
            P(),
            P(),
            P(),
            P(),
        ),
        out_specs=(
            P(None, "fsdp", "seq", None),
            P(None, "fsdp", "seq", None),
            P(),
            P(),
            P(),
            P(),
            P(),
            P(),
            P(),
            P(),
            P(),
            P(),
        ),
        check_vma=False,
    )
```

```python
import functools

import jax
import jax.numpy as jnp
from jax import lax
from jax.experimental import pallas as pl
from jax.experimental.pallas import tpu as pltpu
from jax.sharding import PartitionSpec as P

R = 16
LANES = 128
EPSILON = 1e-05
ADAPTER_SCALE = 0.5
MESH = pl.DeviceIdType.MESH
BF16 = jnp.bfloat16
F32 = jnp.float32
VMEM_LIMIT = 62 * 1024 * 1024
FF_CHUNK = 768
ROW_BLOCK = 256


def from_behind(block, axis, distance):
    devices = range(lax.axis_size(axis))
    route = [(i - distance, i) for i in devices if i - distance in devices]
    return lax.ppermute(block, axis, route)


def dot_nn(left, right):
    return jnp.dot(left, right, preferred_element_type=F32)


def dot_nt(left, right):
    return lax.dot_general(left, right, (((1,), (1,)), ((), ())), preferred_element_type=F32)


def dot_tn(left, right):
    return lax.dot_general(left, right, (((0,), (0,)), ((), ())), preferred_element_type=F32)


def when(condition, action):
    if isinstance(condition, bool):
        if condition:
            action()
    else:
        pl.when(condition)(action)


class Ring:
    def __init__(self, fsdp_size):
        self.count = fsdp_size // 2
        self.me = lax.axis_index("fsdp")
        self.core = lax.rem(self.me, 2)
        chip = self.me // 2
        self.grid = fsdp_size == 16
        if self.grid:
            z, y = chip // 2, lax.rem(chip, 2)
            self.place = y * z + (1 - y) * (7 - z)
        else:
            self.place = chip
        x = lax.axis_index("seq")
        self.x = x
        self.role = lax.rem(x, 2)
        self.to_next = {"fsdp": self.device(lax.rem(self.place + 1, self.count))}
        self.to_prev = {"fsdp": self.device(lax.rem(self.place + self.count - 1, self.count))}
        self.to_core = {"fsdp": self.me + 1 - 2 * self.core}
        self.to_seq = {"seq": x + 1 - 2 * self.role}

    def device(self, place):
        if self.grid:
            y = 1 - place // 4
            z = y * place + (1 - y) * (7 - place)
            return (z * 2 + y) * 2 + self.core
        return place * 2 + self.core

    def at_step(self, direction, step):
        if direction == 0:
            return self.device(lax.rem(self.place + self.count - step, self.count))
        return self.device(lax.rem(self.place + step, self.count))

    def greet(self):
        barrier = pltpu.get_barrier_semaphore()
        for device in (self.to_next, self.to_prev, self.to_core, self.to_seq):
            pl.semaphore_signal(barrier, inc=1, device_id=device, device_id_type=MESH)
        pl.semaphore_wait(barrier, 4)


class Unit:
    def __init__(self, ring, number, spot, sems):
        self.ring, self.number, self.spot = ring, number, spot
        self.send, self.ring_sem, self.seq_sem, self.core_sem = sems
        half = ring.count // 2
        self.reaches = ((half, ring.count - 1 - half), (ring.count - 1 - half, half))
        self.steps = half
        self.others = ring.count - 1

    def copy(self, spot, slot, sem, device):
        return pltpu.make_async_remote_copy(
            src_ref=spot,
            dst_ref=spot,
            send_sem=self.send.at[self.number, slot],
            recv_sem=sem,
            device_id=device,
            device_id_type=MESH,
        )

    def arrived(self, spot, sem):
        self.copy(spot, 0, sem, self.ring.to_next).wait_recv()

    def own(self):
        ring, n = self.ring, self.number
        for slot, third in ((0, ring.role), (1, 2)):
            spot = self.spot(third, ring.me)
            self.copy(spot, 2 * slot, self.ring_sem.at[n, slot, 0], ring.to_next).start()
            self.copy(spot, 2 * slot + 1, self.ring_sem.at[n, slot, self.others - 1], ring.to_prev).start()
        for k, third in enumerate((ring.role, 1 - ring.role, 2)):
            self.copy(self.spot(third, ring.me), 4 + k, self.core_sem.at[n, third, 0], ring.to_core).start()

    def relay(self, step):
        ring, n, others = self.ring, self.number, self.others
        for slot, third in ((0, ring.role), (1, 2)):
            for direction in (0, 1):
                reach = self.reaches[slot][direction]
                lane = step - 1 if direction == 0 else others - step
                spot = self.spot(third, ring.at_step(direction, step))

                def forward(slot=slot, direction=direction, lane=lane, spot=spot):
                    onward = self.ring_sem.at[n, slot, lane + 1 - 2 * direction]
                    target = (ring.to_next, ring.to_prev)[direction]
                    self.copy(spot, 7 + slot * others + lane, onward, target).start()

                def take(slot=slot, third=third, reach=reach, lane=lane, spot=spot, forward=forward):
                    self.arrived(spot, self.ring_sem.at[n, slot, lane])
                    when(step < reach, forward)
                    if slot == 0:
                        self.copy(spot, 7 + 2 * others + lane, self.seq_sem.at[n, lane], ring.to_seq).start()
                    core = self.core_sem.at[n, third, 1 + lane]
                    self.copy(spot, 7 + (3 + slot) * others + lane, core, ring.to_core).start()

                when(step <= reach, take)

    def relay_seq(self, step):
        ring, n, others = self.ring, self.number, self.others
        third = 1 - ring.role
        for direction in (0, 1):
            reach = self.reaches[0][direction]
            lane = step - 1 if direction == 0 else others - step
            spot = self.spot(third, ring.at_step(direction, step))

            def take(lane=lane, spot=spot):
                self.arrived(spot, self.seq_sem.at[n, lane])
                core = self.core_sem.at[n, third, 1 + lane]
                self.copy(spot, 7 + 5 * others + lane, core, ring.to_core).start()

            when(step <= reach, take)

    def collect(self):
        for third in range(3):
            for lane in range(self.others + 1):
                self.arrived(self.spot(third, self.ring.me), self.core_sem.at[self.number, third, lane])

    def drain(self):
        ring, others = self.ring, self.others

        def done(third, slot):
            self.copy(self.spot(third, ring.me), slot, self.seq_sem.at[self.number, 0], ring.to_next).wait_send()

        for slot, third in ((0, 0), (1, 2)):
            done(third, 2 * slot)
            done(third, 2 * slot + 1)
            for direction in (0, 1):
                reach = self.reaches[slot][direction]
                for step in range(1, reach + 1):
                    lane = step - 1 if direction == 0 else others - step
                    if step < reach:
                        done(third, 7 + slot * others + lane)
                    done(third, 7 + (3 + slot) * others + lane)
        for lane in range(others):
            done(0, 7 + 2 * others + lane)
            done(0, 7 + 5 * others + lane)
        for k, third in enumerate((0, 0, 2)):
            done(third, 4 + k)


def unit_sems(units, count):
    return [
        pltpu.SemaphoreType.DMA((units, 7 + 6 * (count - 1))),
        pltpu.SemaphoreType.DMA((units, 2, count - 1)),
        pltpu.SemaphoreType.DMA((units, count - 1)),
        pltpu.SemaphoreType.DMA((units, 3, count)),
    ]


def in_order(units, lag=2):
    entries = []
    for k, unit in enumerate(units):
        entries.append((k, 0, unit.own))
        for step in range(1, unit.steps + 1):
            entries.append((k + step, 1, functools.partial(unit.relay, step)))
            entries.append((k + step + lag, 2, functools.partial(unit.relay_seq, step)))
    for entry in sorted(entries, key=lambda entry: entry[:2]):
        entry[2]()


def move_in(moves, sems):
    inward = [pltpu.make_async_copy(a, b, sems.at[0, k]) for k, (a, b, _) in enumerate(moves)]
    outward = [pltpu.make_async_copy(b, c, sems.at[1, k]) for k, (_, b, c) in enumerate(moves)]
    for copy in inward:
        copy.start()
    for first, second in zip(inward, outward):
        first.wait()
        second.start()
    return outward


def row_spot(landing, rows, third, owner, columns=None):
    return landing.at[pl.ds(owner * rows + third * (rows // 3), rows // 3), :]


def column_spot(landing, rows, width, last, third, owner):
    size = last if isinstance(third, int) and third == 2 else width
    start = third * width if isinstance(third, int) else pl.multiple_of(third * width, LANES)
    return landing.at[pl.ds(owner * rows, rows), pl.ds(start, size)]


def chunk_spot(landing, rows, size, chunk, third, owner):
    start = pl.multiple_of((chunk * 3 + third) * size, LANES)
    return landing.at[:, pl.ds(owner * rows, rows), pl.ds(start, size)]


def mixer_gather_kernel(fsdp_size, in_own, out_own, in_all, out_all, s0, s1, s2, s3, local_sem, held_in, held_out):
    ring = Ring(fsdp_size)
    rows = in_own.shape[0]
    mine = pl.ds(ring.me * rows, rows)
    moved = move_in([(in_own, held_in, in_all.at[mine, :]), (out_own, held_out, out_all.at[mine, :])], local_sem)
    ring.greet()
    for copy in moved:
        copy.wait()
    part = in_all.shape[1] // 3
    out_x = 3 * out_all.shape[1] // 8
    sems = (s0, s1, s2, s3)
    units = [
        Unit(ring, 0, functools.partial(column_spot, in_all, rows, part, part), sems),
        Unit(ring, 1, functools.partial(column_spot, out_all, rows, out_x, out_all.shape[1] - 2 * out_x), sems),
    ]
    in_order(units)
    for unit in units:
        unit.collect()
    for unit in units:
        unit.drain()


ANYWHERE = pl.BlockSpec(memory_space=pl.ANY)
IN_VMEM = pl.BlockSpec(memory_space=pltpu.VMEM)


def gather_mixer(fsdp_size, in_weight, out_weight):
    rows = fsdp_size * in_weight.shape[0]
    own = (in_weight, out_weight)
    return pl.pallas_call(
        functools.partial(mixer_gather_kernel, fsdp_size),
        out_shape=tuple(jax.ShapeDtypeStruct((rows, member.shape[1]), BF16) for member in own),
        in_specs=[ANYWHERE] * 2,
        out_specs=(ANYWHERE,) * 2,
        scratch_shapes=unit_sems(2, fsdp_size // 2)
        + [pltpu.SemaphoreType.DMA((2, 2))]
        + [pltpu.VMEM(member.shape, BF16) for member in own],
        compiler_params=pltpu.CompilerParams(collective_id=0, has_side_effects=True),
    )(*own)


def slot_mask(rows, slots, per_sequence, base=0):
    row = lax.broadcasted_iota(jnp.int32, (rows, slots), 0)
    column = lax.broadcasted_iota(jnp.int32, (rows, slots), 1)
    return (row // per_sequence == column // R).astype(F32)


def feed_forward_kernel(fsdp_size, per_sequence, *refs):
    (
        second, cotangent, after, pick, pick_t,
        gate_first, gate_second, up_first, up_second, down_first, down_second,
        gate_own, up_own, down_own,
    ) = refs[:14]
    block_out, grad_second, grads, gu_all, down_all = refs[14:19]
    sems, local_sem, load_sem = refs[19:23], refs[23], refs[24]
    (
        held_gate, held_up, held_down, total, grad_hidden, gate_w, up_w, down_w, hidden_s, gate_s, up_s,
        first_gu, first_down, second_gu, second_down, low_gu, grad_low_down, low_down, grad_low_gu,
    ) = refs[25:]
    ring = Ring(fsdp_size)
    rows, down_rows = gate_own.shape[0], down_own.shape[0]
    tokens, features = second.shape
    hidden_size = gate_own.shape[1]
    chunks = hidden_size // FF_CHUNK
    slots = pick.shape[1]
    blocks = tokens // ROW_BLOCK
    mine = pl.ds(ring.me * rows, rows)
    moved = move_in(
        [
            (down_own, held_down, down_all.at[pl.ds(ring.me * down_rows, down_rows), :]),
            (gate_own, held_gate, gu_all.at[0, mine, :]),
            (up_own, held_up, gu_all.at[1, mine, :]),
        ],
        local_sem,
    )
    started = pltpu.make_async_copy(after, total, load_sem.at[2, 0])
    started.start()
    ring.greet()
    for copy in moved:
        copy.wait()
    down_unit = Unit(ring, 0, functools.partial(row_spot, down_all, down_rows), sems)

    def chunk_unit(k):
        return Unit(ring, 1 + k, functools.partial(chunk_spot, gu_all, rows, FF_CHUNK // 3, k), sems)

    steps = down_unit.steps
    down_unit.own()
    chunk_unit(0).own()

    for k, (first, second_map) in enumerate(((gate_first, gate_second), (up_first, up_second))):
        first_gu[k] = dot_nn(first[...], pick[...]).astype(BF16)
        for j in range(chunks):
            part = dot_nn(pick_t[...], second_map[:, j * FF_CHUNK : (j + 1) * FF_CHUNK])
            second_gu[k, j] = part.astype(BF16)
    second_down[...] = dot_nn(pick_t[...], down_second[...]).astype(BF16)
    for j in range(chunks):
        first_down[j] = dot_nn(down_first[j * FF_CHUNK : (j + 1) * FF_CHUNK, :], pick[...]).astype(BF16)
    mask = slot_mask(tokens, slots, per_sequence)
    for k in range(2):
        low = (dot_nn(second[...], first_gu[k]) * mask).astype(BF16)
        low_gu[k] = low * ADAPTER_SCALE
    grad_low_down[...] = (ADAPTER_SCALE * dot_nt(cotangent[...], second_down[...]) * mask).astype(BF16)
    grad_second[...] = jnp.zeros_like(grad_second)
    low_down[...] = jnp.zeros_like(low_down)
    grad_low_gu[...] = jnp.zeros_like(grad_low_gu)

    for step in range(1, steps + 1):
        down_unit.relay(step)
    for step in range(1, steps + 1):
        down_unit.relay_seq(step)
    down_unit.collect()

    def down_load(j, s):
        place = pl.ds(pl.multiple_of(j * FF_CHUNK, FF_CHUNK), FF_CHUNK)
        return pltpu.make_async_copy(down_all.at[place, :], down_w.at[s], load_sem.at[s, 0])

    def gu_loads(j, s):
        place = pl.ds(pl.multiple_of(j * FF_CHUNK, FF_CHUNK), FF_CHUNK)
        return (
            pltpu.make_async_copy(gu_all.at[0, :, place], gate_w.at[s], load_sem.at[s, 1]),
            pltpu.make_async_copy(gu_all.at[1, :, place], up_w.at[s], load_sem.at[s, 2]),
        )

    per_tick = -(-steps // blocks)

    def ticks(unit_action, r):
        for k in range(per_tick):
            step = r * per_tick + k + 1
            when(step <= steps, functools.partial(unit_action, step))

    down_load(0, 0).start()

    @pl.loop(0, chunks)
    def _(j):
        s = lax.rem(j, 2)

        @pl.when(j + 1 < chunks)
        def _():
            down_load(j + 1, 1 - s).start()

        down_load(j, s).wait()

        @pl.loop(0, blocks)
        def _(r):
            at = pl.ds(pl.multiple_of(r * ROW_BLOCK, ROW_BLOCK), ROW_BLOCK)

            @pl.when(j == 0)
            def _():
                ticks(chunk_unit(0).relay, r)

            @pl.when((j == 1) & (r == 0))
            def _():
                chunk_unit(1).own()

            @pl.when(j == 2)
            def _():
                ticks(chunk_unit(0).relay_seq, r)

            @pl.when(j == 3)
            def _():
                ticks(chunk_unit(1).relay, r)

            @pl.when((j == 4) & (r == 0))
            def _():
                chunk_unit(2).own()

            grad_hidden[j, at, :] = dot_nt(cotangent[at, :], down_w[s]) + dot_nt(
                grad_low_down[at, :], first_down[j]
            )

    started.wait()
    chunk_unit(0).collect()
    for copy in gu_loads(0, 0):
        copy.start()
    down_load(0, 0).start()

    @pl.loop(0, chunks)
    def _(j):
        s = lax.rem(j, 2)
        for copy in (down_load(j, s),) + gu_loads(j, s):
            copy.wait()

        @pl.loop(0, blocks)
        def _(r):
            at = pl.ds(pl.multiple_of(r * ROW_BLOCK, ROW_BLOCK), ROW_BLOCK)

            @pl.when((r == 0) & (j + 3 < chunks))
            def _():
                chunk_unit(j + 3).own()

            @pl.when(j + 2 < chunks)
            def _():
                ticks(chunk_unit(j + 2).relay, r)

            @pl.when(j + 1 < chunks)
            def _():
                spread = -(-steps // max(blocks - 1, 1))
                for k in range(spread):
                    step = r * spread + k + 1
                    when(step <= steps, functools.partial(chunk_unit(j + 1).relay_seq, step))

                @pl.when(r == blocks - 1)
                def _():
                    chunk_unit(j + 1).collect()
                    for copy in (down_load(j + 1, 1 - s),) + gu_loads(j + 1, 1 - s):
                        copy.start()

            rows_in = second[at, :]
            gate = dot_nn(rows_in, gate_w[s]) + dot_nn(low_gu[0, at, :], second_gu[0, j])
            up = dot_nn(rows_in, up_w[s]) + dot_nn(low_gu[1, at, :], second_gu[1, j])
            back = grad_hidden[j, at, :]
            sigmoid = 1.0 / (1.0 + jnp.exp(-gate))
            active = gate * sigmoid
            hidden = (active * up).astype(BF16)
            grad_gate = (back * up * sigmoid * (1.0 + gate * (1.0 - sigmoid))).astype(BF16)
            grad_up = (back * active).astype(BF16)
            hidden_s[at, :] = hidden
            gate_s[at, :] = grad_gate
            up_s[at, :] = grad_up
            total[at, :] += dot_nn(hidden, down_w[s])
            grad_second[at, :] += dot_nt(grad_gate, gate_w[s]) + dot_nt(grad_up, up_w[s])
            low_down[at, :] += dot_nn(hidden, first_down[j])
            grad_low_gu[0, at, :] += dot_nt(grad_gate, second_gu[0, j])
            grad_low_gu[1, at, :] += dot_nt(grad_up, second_gu[1, j])

        base = j * FF_CHUNK
        for offset, left, right in (
            (2 * features, grad_low_down[...], hidden_s),
            (2 * features + hidden_size, low_gu[0], gate_s),
            (2 * features + 2 * hidden_size, low_gu[1], up_s),
        ):
            columns = pl.ds(pl.multiple_of(offset + base, LANES), FF_CHUNK)
            grads[:, columns] = dot_tn(left, right[...]).astype(BF16)

    half_low_down = (ADAPTER_SCALE * low_down[...] * mask).astype(BF16)
    block_out[...] = (total[...] + dot_nn(half_low_down, second_down[...])).astype(BF16)
    base = 2 * features + 3 * hidden_size
    grads[:, base : base + features] = dot_tn(half_low_down, cotangent[...]).astype(BF16)
    for k in range(2):
        back_low = (ADAPTER_SCALE * grad_low_gu[k] * mask).astype(BF16)
        grads[:, k * features : (k + 1) * features] = dot_tn(back_low, second[...]).astype(BF16)
        grad_second[...] += dot_nt(back_low, first_gu[k])

    down_unit.drain()

    @pl.loop(0, chunks)
    def _(k):
        chunk_unit(k).drain()


def feed_forward(fsdp_size, per_sequence, second, cotangent, after, pick, pick_t, adapters, own):
    tokens, features = second.shape
    hidden_size = own[0].shape[1]
    slots = pick.shape[1]
    chunks = hidden_size // FF_CHUNK
    grads_width = 3 * features + 3 * hidden_size
    return pl.pallas_call(
        functools.partial(feed_forward_kernel, fsdp_size, per_sequence),
        out_shape=(
            jax.ShapeDtypeStruct((tokens, features), BF16),
            jax.ShapeDtypeStruct((tokens, features), F32),
            jax.ShapeDtypeStruct((slots, grads_width), BF16),
            jax.ShapeDtypeStruct((2, features, hidden_size), BF16),
            jax.ShapeDtypeStruct((hidden_size, features), BF16),
        ),
        in_specs=[IN_VMEM, IN_VMEM, ANYWHERE] + [IN_VMEM] * 8 + [ANYWHERE] * 3,
        out_specs=(IN_VMEM, IN_VMEM, IN_VMEM, ANYWHERE, ANYWHERE),
        scratch_shapes=unit_sems(1 + chunks, fsdp_size // 2)
        + [pltpu.SemaphoreType.DMA((2, 3)), pltpu.SemaphoreType.DMA((3, 3))]
        + [pltpu.VMEM(member.shape, BF16) for member in own]
        + [
            pltpu.VMEM((tokens, features), F32),
            pltpu.VMEM((chunks, tokens, FF_CHUNK), F32),
            pltpu.VMEM((2, features, FF_CHUNK), BF16),
            pltpu.VMEM((2, features, FF_CHUNK), BF16),
            pltpu.VMEM((2, FF_CHUNK, features), BF16),
            pltpu.VMEM((tokens, FF_CHUNK), BF16),
            pltpu.VMEM((tokens, FF_CHUNK), BF16),
            pltpu.VMEM((tokens, FF_CHUNK), BF16),
            pltpu.VMEM((2, features, slots), BF16),
            pltpu.VMEM((chunks, FF_CHUNK, slots), BF16),
            pltpu.VMEM((2, chunks, slots, FF_CHUNK), BF16),
            pltpu.VMEM((slots, features), BF16),
            pltpu.VMEM((2, tokens, slots), BF16),
            pltpu.VMEM((tokens, slots), BF16),
            pltpu.VMEM((tokens, slots), F32),
            pltpu.VMEM((2, tokens, slots), F32),
        ],
        compiler_params=pltpu.CompilerParams(
            collective_id=1, has_side_effects=True, vmem_limit_bytes=VMEM_LIMIT
        ),
    )(second, cotangent, after, pick, pick_t, *adapters, *own)


def sum_kernel(sizes, first_tiles, packed, landing, s0, s1, s2, s3, send_sem, recv_sem, seq_sem, local_sem, got, result):
    fsdp_size, seq_size = sizes
    devices = fsdp_size * seq_size
    ring = Ring(fsdp_size)
    me = ring.me * seq_size + ring.x
    tiles = landing.shape[2]
    width = tiles * LANES
    barrier = pltpu.get_barrier_semaphore()

    def target(k):
        d = lax.rem(me + k, devices)
        return d, {"fsdp": d // seq_size, "seq": lax.rem(d, seq_size)}

    @pl.loop(1, devices)
    def _(k):
        pl.semaphore_signal(barrier, inc=1, device_id=target(k)[1], device_id_type=MESH)

    own = pltpu.make_async_copy(packed.at[me], got.at[me], local_sem.at[0])
    own.start()
    pl.semaphore_wait(barrier, devices - 1)

    def piece(k):
        d, device = target(k)
        return pltpu.make_async_remote_copy(
            src_ref=packed.at[d],
            dst_ref=got.at[me],
            send_sem=send_sem.at[k],
            recv_sem=recv_sem.at[k],
            device_id=device,
            device_id_type=MESH,
        )

    @pl.loop(1, devices)
    def _(k):
        piece(k).start()

    own.wait()

    @pl.loop(1, devices)
    def _(k):
        piece(k).wait_recv()

    everything = got[...].reshape(devices * got.shape[1], width + LANES)
    summed = dot_tn(everything[:, width:], everything[:, :width])
    for t in range(tiles):
        tile = summed[:, t * LANES : (t + 1) * LANES]
        result[t] = jnp.where(me * tiles + t < first_tiles, tile.T, tile).astype(BF16)
    place = landing.at[ring.me, ring.x]
    store = pltpu.make_async_copy(result, place, local_sem.at[1])
    store.start()
    store.wait()

    def across(k):
        x = lax.rem(ring.x + k, seq_size)
        return pltpu.make_async_remote_copy(
            src_ref=place,
            dst_ref=place,
            send_sem=seq_sem.at[0, k],
            recv_sem=seq_sem.at[1, k],
            device_id={"seq": x},
            device_id_type=MESH,
        )

    for k in range(1, seq_size):
        across(k).start()
    for k in range(1, seq_size):
        across(k).wait_recv()

    def spot(third, owner):
        size = 32 if isinstance(third, int) and third == 2 else 48
        return landing.at[owner, :, :, pl.ds(third * 48, size), :]

    unit = Unit(ring, 0, spot, (s0, s1, s2, s3))
    in_order([unit])
    unit.collect()
    unit.drain()
    for k in range(1, seq_size):
        across(k).wait_send()

    @pl.loop(1, devices)
    def _(k):
        piece(k).wait_send()


def sum_gradients(sizes, first_tiles, packed):
    devices, slots, width = packed.shape
    tiles = width // LANES - 1
    fsdp_size, seq_size = sizes
    return pl.pallas_call(
        functools.partial(sum_kernel, sizes, first_tiles),
        out_shape=jax.ShapeDtypeStruct((fsdp_size, seq_size, tiles, LANES, LANES), BF16),
        in_specs=[ANYWHERE],
        out_specs=ANYWHERE,
        scratch_shapes=unit_sems(1, fsdp_size // 2)
        + [
            pltpu.SemaphoreType.DMA((devices,)),
            pltpu.SemaphoreType.DMA((devices,)),
            pltpu.SemaphoreType.DMA((2, seq_size)),
            pltpu.SemaphoreType.DMA((2,)),
            pltpu.VMEM(packed.shape, BF16),
            pltpu.VMEM((tiles, LANES, LANES), BF16),
        ],
        compiler_params=pltpu.CompilerParams(
            collective_id=2, has_side_effects=True, vmem_limit_bytes=VMEM_LIMIT
        ),
    )(packed)


def rms_parts(values):
    inverse = lax.rsqrt(jnp.mean(values * values, axis=-1, keepdims=True) + EPSILON)
    return (inverse, values * inverse)


def rms_back(grad_normed, gain_vector, inverse, unit_rows):
    scaled = grad_normed * gain_vector
    return inverse * (scaled - unit_rows * jnp.mean(scaled * unit_rows, axis=-1, keepdims=True))


def per_device(
    block_input,
    output_grad,
    adapter_ids,
    in_weight,
    out_weight,
    gate_weight,
    up_weight,
    down_weight,
    conv_weight,
    first_gain,
    second_gain,
    infirst_adapter,
    insecond_adapter,
    outfirst_adapter,
    outsecond_adapter,
    gatefirst_adapter,
    gatesecond_adapter,
    upfirst_adapter,
    upsecond_adapter,
    downfirst_adapter,
    downsecond_adapter,
):
    batches, seq_count, local_len, features = block_input.shape
    sequences = batches * seq_count
    tokens = sequences * local_len
    fsdp_size, seq_size = lax.axis_size("fsdp"), lax.axis_size("seq")
    slots = sequences * R
    hidden_size = gate_weight.shape[1]
    kernel = conv_weight.astype(F32)
    gain_first = first_gain.astype(F32)
    gain_second = second_gain.astype(F32)
    wanted = jnp.repeat(adapter_ids.reshape(sequences) * R, R) + jnp.tile(jnp.arange(R), sequences)
    pick = (lax.broadcasted_iota(jnp.int32, (LANES, slots), 0) == wanted[None, :]).astype(BF16)
    pick_t = (lax.broadcasted_iota(jnp.int32, (slots, LANES), 1) == wanted[:, None]).astype(BF16)
    mask = slot_mask(tokens, slots, local_len)
    in_first, out_first = (dot_nn(m, pick).astype(BF16) for m in (infirst_adapter, outfirst_adapter))
    in_second, out_second = (dot_nn(pick_t, m).astype(BF16) for m in (insecond_adapter, outsecond_adapter))

    weight_in, weight_out = gather_mixer(fsdp_size, in_weight, out_weight)
    inputs = block_input.reshape(tokens, features).astype(F32)
    cotangent = output_grad.reshape(tokens, features)
    inverse_first, unit_first = rms_parts(inputs)
    normed = (unit_first * gain_first).astype(BF16)
    low_in = (dot_nn(normed, in_first) * mask * ADAPTER_SCALE).astype(BF16)
    mixed_in = dot_nn(normed, weight_in) + dot_nn(low_in, in_second)
    first_part = mixed_in[:, :features]
    middle_part = mixed_in[:, features : 2 * features]
    last_part = mixed_in[:, 2 * features :]
    gated_values = (first_part * last_part).reshape(sequences, local_len, features)
    rim_rows = from_behind(gated_values[:, local_len - 2 :, :], "seq", 1)
    extended = jnp.concatenate([rim_rows, gated_values], axis=1)
    conv_out = (
        kernel[0] * extended[:, :local_len]
        + kernel[1] * extended[:, 1 : local_len + 1]
        + kernel[2] * extended[:, 2:]
    ).reshape(tokens, features)
    mixer_out = (middle_part * conv_out).astype(BF16)
    low_out = (dot_nn(mixer_out, out_first) * mask * ADAPTER_SCALE).astype(BF16)
    after_mixer = inputs + (dot_nn(mixer_out, weight_out) + dot_nn(low_out, out_second))
    inverse_second, unit_second = rms_parts(after_mixer)
    second = (unit_second * gain_second).astype(BF16)

    block_output, grad_second, grads_late, _, _ = feed_forward(
        fsdp_size,
        local_len,
        second,
        cotangent,
        after_mixer,
        pick,
        pick_t,
        (
            gatefirst_adapter,
            gatesecond_adapter,
            upfirst_adapter,
            upsecond_adapter,
            downfirst_adapter,
            downsecond_adapter,
        ),
        (gate_weight, up_weight, down_weight),
    )

    grad_after = cotangent.astype(F32) + rms_back(grad_second, gain_second, inverse_second, unit_second)
    grad_branch = grad_after.astype(BF16)
    grad_outsecond = dot_tn(low_out, grad_branch)
    grad_low_out = (ADAPTER_SCALE * dot_nt(grad_branch, out_second) * mask).astype(BF16)
    grad_outfirst = dot_tn(grad_low_out, mixer_out)
    grad_mixer = dot_nt(grad_branch, weight_out) + dot_nt(grad_low_out, out_first)
    grad_conv = (grad_mixer * middle_part).reshape(sequences, local_len, features)
    rim_back = from_behind(grad_conv[:, :2, :], "seq", -1)
    beyond = jnp.concatenate([grad_conv, rim_back], axis=1)
    grad_gated = (
        kernel[2] * beyond[:, :local_len]
        + kernel[1] * beyond[:, 1 : local_len + 1]
        + kernel[0] * beyond[:, 2:]
    ).reshape(tokens, features)
    grad_mixed = jnp.concatenate(
        [grad_gated * last_part, grad_mixer * conv_out, grad_gated * first_part], axis=1
    ).astype(BF16)
    grad_insecond = dot_tn(low_in, grad_mixed)
    grad_low_in = (ADAPTER_SCALE * dot_nt(grad_mixed, in_second) * mask).astype(BF16)
    grad_infirst = dot_tn(grad_low_in, normed)

    grads = [
        grad_infirst.astype(BF16),
        grad_outfirst.astype(BF16),
        grads_late[:, : 2 * features + hidden_size],
        grad_insecond.astype(BF16),
        grad_outsecond.astype(BF16),
        grads_late[:, 2 * features + hidden_size :],
    ]
    total_width = sum(member.shape[1] for member in grads)
    devices = fsdp_size * seq_size
    tiles = -(-total_width // (LANES * devices))
    grads.append(jnp.zeros((slots, tiles * LANES * devices - total_width), BF16))
    packed = jnp.concatenate(grads, axis=1).reshape(slots, devices, tiles * LANES).transpose(1, 0, 2)
    packed = jnp.concatenate([packed, jnp.broadcast_to(pick_t, (devices, slots, LANES))], axis=2)
    first_tiles = (4 * features + hidden_size) // LANES
    summed = sum_gradients((fsdp_size, seq_size), first_tiles, packed).reshape(devices * tiles, LANES, LANES)

    grad_normed = dot_nt(grad_mixed, weight_in) + dot_nt(grad_low_in, in_first)
    grad_input = grad_after + rms_back(grad_normed, gain_first, inverse_first, unit_first)

    ones = summed[:first_tiles].reshape(first_tiles * LANES, LANES).astype(F32)
    twos = summed[first_tiles:].transpose(1, 0, 2).reshape(LANES, -1).astype(F32)
    at = [0, features, 2 * features, 3 * features, 4 * features, 4 * features + hidden_size]
    firsts = [ones[at[k] : at[k + 1]] for k in range(5)]
    at = [0]
    for width in (3 * features, features, hidden_size, hidden_size, features):
        at.append(at[-1] + width)
    seconds = [twos[:, at[k] : at[k + 1]] for k in range(5)]
    shape = block_input.shape
    return (
        block_output.reshape(shape),
        grad_input.astype(BF16).reshape(shape),
        firsts[0],
        seconds[0],
        firsts[1],
        seconds[1],
        firsts[2],
        seconds[2],
        firsts[3],
        seconds[3],
        firsts[4],
        seconds[4],
    )


def solution(mesh):
    return jax.shard_map(
        per_device,
        mesh=mesh,
        in_specs=(
            P(None, "fsdp", "seq", None),
            P(None, "fsdp", "seq", None),
            P(None, "fsdp"),
            P("fsdp", None),
            P("fsdp", None),
            P("fsdp", None),
            P("fsdp", None),
            P("fsdp", None),
            P(),
            P(),
            P(),
            P(),
            P(),
            P(),
            P(),
            P(),
            P(),
            P(),
            P(),
            P(),
            P(),
        ),
        out_specs=(
            P(None, "fsdp", "seq", None),
            P(None, "fsdp", "seq", None),
            P(),
            P(),
            P(),
            P(),
            P(),
            P(),
            P(),
            P(),
            P(),
            P(),
        ),
        check_vma=False,
    )
```

```python
import functools

import jax
import jax.numpy as jnp
from jax import lax
from jax.experimental import pallas as pl
from jax.experimental.pallas import tpu as pltpu
from jax.sharding import PartitionSpec as P

R = 16
LANES = 128
EPSILON = 1e-05
ADAPTER_SCALE = 0.5
MESH = pl.DeviceIdType.MESH
BF16 = jnp.bfloat16
F32 = jnp.float32
VMEM_LIMIT = 62 * 1024 * 1024
FF_CHUNK = 768
ROW_BLOCK = 256


def from_behind(block, axis, distance):
    devices = range(lax.axis_size(axis))
    route = [(i - distance, i) for i in devices if i - distance in devices]
    return lax.ppermute(block, axis, route)


def dot_nn(left, right):
    return jnp.dot(left, right, preferred_element_type=F32)


def dot_nt(left, right):
    return lax.dot_general(left, right, (((1,), (1,)), ((), ())), preferred_element_type=F32)


def dot_tn(left, right):
    return lax.dot_general(left, right, (((0,), (0,)), ((), ())), preferred_element_type=F32)


def when(condition, action):
    if isinstance(condition, bool):
        if condition:
            action()
    else:
        pl.when(condition)(action)


class Ring:
    def __init__(self, fsdp_size):
        self.count = fsdp_size // 2
        self.me = lax.axis_index("fsdp")
        self.core = lax.rem(self.me, 2)
        chip = self.me // 2
        self.grid = fsdp_size == 16
        if self.grid:
            z, y = chip // 2, lax.rem(chip, 2)
            self.place = y * z + (1 - y) * (7 - z)
        else:
            self.place = chip
        x = lax.axis_index("seq")
        self.x = x
        self.role = lax.rem(x, 2)
        self.to_next = {"fsdp": self.device(lax.rem(self.place + 1, self.count))}
        self.to_prev = {"fsdp": self.device(lax.rem(self.place + self.count - 1, self.count))}
        self.to_core = {"fsdp": self.me + 1 - 2 * self.core}
        self.to_seq = {"seq": x + 1 - 2 * self.role}

    def device(self, place):
        if self.grid:
            y = 1 - place // 4
            z = y * place + (1 - y) * (7 - place)
            return (z * 2 + y) * 2 + self.core
        return place * 2 + self.core

    def at_step(self, direction, step):
        if direction == 0:
            return self.device(lax.rem(self.place + self.count - step, self.count))
        return self.device(lax.rem(self.place + step, self.count))

    def greet(self):
        barrier = pltpu.get_barrier_semaphore()
        for device in (self.to_next, self.to_prev, self.to_core, self.to_seq):
            pl.semaphore_signal(barrier, inc=1, device_id=device, device_id_type=MESH)
        pl.semaphore_wait(barrier, 4)


class Unit:
    def __init__(self, ring, number, spot, sems):
        self.ring, self.number, self.spot = ring, number, spot
        self.send, self.ring_sem, self.seq_sem, self.core_sem = sems
        half = ring.count // 2
        self.reaches = ((half, ring.count - 1 - half), (ring.count - 1 - half, half))
        self.steps = half
        self.others = ring.count - 1

    def copy(self, spot, slot, sem, device):
        return pltpu.make_async_remote_copy(
            src_ref=spot,
            dst_ref=spot,
            send_sem=self.send.at[self.number, slot],
            recv_sem=sem,
            device_id=device,
            device_id_type=MESH,
        )

    def arrived(self, spot, sem):
        self.copy(spot, 0, sem, self.ring.to_next).wait_recv()

    def own(self):
        ring, n = self.ring, self.number
        for slot, third in ((0, ring.role), (1, 2)):
            spot = self.spot(third, ring.me)
            self.copy(spot, 2 * slot, self.ring_sem.at[n, slot, 0], ring.to_next).start()
            self.copy(spot, 2 * slot + 1, self.ring_sem.at[n, slot, self.others - 1], ring.to_prev).start()
        for k, third in enumerate((ring.role, 1 - ring.role, 2)):
            self.copy(self.spot(third, ring.me), 4 + k, self.core_sem.at[n, third, 0], ring.to_core).start()

    def relay(self, step):
        ring, n, others = self.ring, self.number, self.others
        for slot, third in ((0, ring.role), (1, 2)):
            for direction in (0, 1):
                reach = self.reaches[slot][direction]
                lane = step - 1 if direction == 0 else others - step
                spot = self.spot(third, ring.at_step(direction, step))

                def forward(slot=slot, direction=direction, lane=lane, spot=spot):
                    onward = self.ring_sem.at[n, slot, lane + 1 - 2 * direction]
                    target = (ring.to_next, ring.to_prev)[direction]
                    self.copy(spot, 7 + slot * others + lane, onward, target).start()

                def take(slot=slot, third=third, reach=reach, lane=lane, spot=spot, forward=forward):
                    self.arrived(spot, self.ring_sem.at[n, slot, lane])
                    when(step < reach, forward)
                    if slot == 0:
                        self.copy(spot, 7 + 2 * others + lane, self.seq_sem.at[n, lane], ring.to_seq).start()
                    core = self.core_sem.at[n, third, 1 + lane]
                    self.copy(spot, 7 + (3 + slot) * others + lane, core, ring.to_core).start()

                when(step <= reach, take)

    def relay_seq(self, step):
        ring, n, others = self.ring, self.number, self.others
        third = 1 - ring.role
        for direction in (0, 1):
            reach = self.reaches[0][direction]
            lane = step - 1 if direction == 0 else others - step
            spot = self.spot(third, ring.at_step(direction, step))

            def take(lane=lane, spot=spot):
                self.arrived(spot, self.seq_sem.at[n, lane])
                core = self.core_sem.at[n, third, 1 + lane]
                self.copy(spot, 7 + 5 * others + lane, core, ring.to_core).start()

            when(step <= reach, take)

    def collect(self):
        for third in range(3):
            for lane in range(self.others + 1):
                self.arrived(self.spot(third, self.ring.me), self.core_sem.at[self.number, third, lane])

    def drain(self):
        ring, others = self.ring, self.others

        def done(third, slot):
            self.copy(self.spot(third, ring.me), slot, self.seq_sem.at[self.number, 0], ring.to_next).wait_send()

        for slot, third in ((0, 0), (1, 2)):
            done(third, 2 * slot)
            done(third, 2 * slot + 1)
            for direction in (0, 1):
                reach = self.reaches[slot][direction]
                for step in range(1, reach + 1):
                    lane = step - 1 if direction == 0 else others - step
                    if step < reach:
                        done(third, 7 + slot * others + lane)
                    done(third, 7 + (3 + slot) * others + lane)
        for lane in range(others):
            done(0, 7 + 2 * others + lane)
            done(0, 7 + 5 * others + lane)
        for k, third in enumerate((0, 0, 2)):
            done(third, 4 + k)


def unit_sems(units, count):
    return [
        pltpu.SemaphoreType.DMA((units, 7 + 6 * (count - 1))),
        pltpu.SemaphoreType.DMA((units, 2, count - 1)),
        pltpu.SemaphoreType.DMA((units, count - 1)),
        pltpu.SemaphoreType.DMA((units, 3, count)),
    ]


def in_order(units, lag=2):
    entries = []
    for k, unit in enumerate(units):
        entries.append((k, 0, unit.own))
        for step in range(1, unit.steps + 1):
            entries.append((k + step, 1, functools.partial(unit.relay, step)))
            entries.append((k + step + lag, 2, functools.partial(unit.relay_seq, step)))
    for entry in sorted(entries, key=lambda entry: entry[:2]):
        entry[2]()


def move_in(moves, sems):
    inward = [pltpu.make_async_copy(a, b, sems.at[0, k]) for k, (a, b, _) in enumerate(moves)]
    outward = [pltpu.make_async_copy(b, c, sems.at[1, k]) for k, (_, b, c) in enumerate(moves)]
    for copy in inward:
        copy.start()
    for first, second in zip(inward, outward):
        first.wait()
        second.start()
    return outward


def row_spot(landing, rows, third, owner, columns=None):
    return landing.at[pl.ds(owner * rows + third * (rows // 3), rows // 3), :]


def column_spot(landing, rows, width, last, third, owner):
    size = last if isinstance(third, int) and third == 2 else width
    start = third * width if isinstance(third, int) else pl.multiple_of(third * width, LANES)
    return landing.at[pl.ds(owner * rows, rows), pl.ds(start, size)]


def chunk_spot(landing, rows, size, chunk, third, owner):
    start = pl.multiple_of((chunk * 3 + third) * size, LANES)
    return landing.at[:, pl.ds(owner * rows, rows), pl.ds(start, size)]


def mixer_gather_kernel(fsdp_size, in_own, out_own, in_all, out_all, s0, s1, s2, s3, local_sem, held_in, held_out):
    ring = Ring(fsdp_size)
    rows = in_own.shape[0]
    mine = pl.ds(ring.me * rows, rows)
    moved = move_in([(in_own, held_in, in_all.at[mine, :]), (out_own, held_out, out_all.at[mine, :])], local_sem)
    ring.greet()
    for copy in moved:
        copy.wait()
    part = in_all.shape[1] // 3
    out_x = 3 * out_all.shape[1] // 8
    sems = (s0, s1, s2, s3)
    units = [
        Unit(ring, 0, functools.partial(column_spot, in_all, rows, part, part), sems),
        Unit(ring, 1, functools.partial(column_spot, out_all, rows, out_x, out_all.shape[1] - 2 * out_x), sems),
    ]
    in_order(units)
    for unit in units:
        unit.collect()
    for unit in units:
        unit.drain()


ANYWHERE = pl.BlockSpec(memory_space=pl.ANY)
IN_VMEM = pl.BlockSpec(memory_space=pltpu.VMEM)


def gather_mixer(fsdp_size, in_weight, out_weight):
    rows = fsdp_size * in_weight.shape[0]
    own = (in_weight, out_weight)
    return pl.pallas_call(
        functools.partial(mixer_gather_kernel, fsdp_size),
        out_shape=tuple(jax.ShapeDtypeStruct((rows, member.shape[1]), BF16) for member in own),
        in_specs=[ANYWHERE] * 2,
        out_specs=(ANYWHERE,) * 2,
        scratch_shapes=unit_sems(2, fsdp_size // 2)
        + [pltpu.SemaphoreType.DMA((2, 2))]
        + [pltpu.VMEM(member.shape, BF16) for member in own],
        compiler_params=pltpu.CompilerParams(collective_id=0, has_side_effects=True),
    )(*own)


def slot_mask(rows, slots, per_sequence, base=0):
    row = lax.broadcasted_iota(jnp.int32, (rows, slots), 0)
    column = lax.broadcasted_iota(jnp.int32, (rows, slots), 1)
    return (row // per_sequence == column // R).astype(F32)


def feed_forward_kernel(fsdp_size, per_sequence, *refs):
    (
        second, cotangent, after, pick, pick_t,
        gate_first, gate_second, up_first, up_second, down_first, down_second,
        gate_own, up_own, down_own,
    ) = refs[:14]
    block_out, grad_second, grads, gu_all, down_all = refs[14:19]
    sems, local_sem, load_sem = refs[19:23], refs[23], refs[24]
    (
        held_gate, held_up, held_down, total, grad_hidden, gate_w, up_w, down_w, hidden_s, gate_s, up_s,
        first_gu, first_down, second_gu, second_down, low_gu, grad_low_down, low_down, grad_low_gu,
    ) = refs[25:]
    ring = Ring(fsdp_size)
    rows, down_rows = gate_own.shape[0], down_own.shape[0]
    tokens, features = second.shape
    hidden_size = gate_own.shape[1]
    chunks = hidden_size // FF_CHUNK
    slots = pick.shape[1]
    blocks = tokens // ROW_BLOCK
    mine = pl.ds(ring.me * rows, rows)
    moved = move_in(
        [
            (down_own, held_down, down_all.at[pl.ds(ring.me * down_rows, down_rows), :]),
            (gate_own, held_gate, gu_all.at[0, mine, :]),
            (up_own, held_up, gu_all.at[1, mine, :]),
        ],
        local_sem,
    )
    started = pltpu.make_async_copy(after, total, load_sem.at[2, 0])
    started.start()
    ring.greet()
    for copy in moved:
        copy.wait()
    down_unit = Unit(ring, 0, functools.partial(row_spot, down_all, down_rows), sems)

    def chunk_unit(k):
        return Unit(ring, 1 + k, functools.partial(chunk_spot, gu_all, rows, FF_CHUNK // 3, k), sems)

    steps = down_unit.steps
    down_unit.own()
    chunk_unit(0).own()

    for k, (first, second_map) in enumerate(((gate_first, gate_second), (up_first, up_second))):
        first_gu[k] = dot_nn(first[...], pick[...]).astype(BF16)
        for j in range(chunks):
            part = dot_nn(pick_t[...], second_map[:, j * FF_CHUNK : (j + 1) * FF_CHUNK])
            second_gu[k, j] = part.astype(BF16)
    second_down[...] = dot_nn(pick_t[...], down_second[...]).astype(BF16)
    for j in range(chunks):
        first_down[j] = dot_nn(down_first[j * FF_CHUNK : (j + 1) * FF_CHUNK, :], pick[...]).astype(BF16)
    mask = slot_mask(tokens, slots, per_sequence)
    for k in range(2):
        low = (dot_nn(second[...], first_gu[k]) * mask).astype(BF16)
        low_gu[k] = low * ADAPTER_SCALE
    grad_low_down[...] = (ADAPTER_SCALE * dot_nt(cotangent[...], second_down[...]) * mask).astype(BF16)
    grad_second[...] = jnp.zeros_like(grad_second)
    low_down[...] = jnp.zeros_like(low_down)
    grad_low_gu[...] = jnp.zeros_like(grad_low_gu)

    for step in range(1, steps + 1):
        down_unit.relay(step)
    for step in range(1, steps + 1):
        down_unit.relay_seq(step)
    down_unit.collect()

    def down_load(j, s):
        place = pl.ds(pl.multiple_of(j * FF_CHUNK, FF_CHUNK), FF_CHUNK)
        return pltpu.make_async_copy(down_all.at[place, :], down_w.at[s], load_sem.at[s, 0])

    def gu_loads(j, s):
        place = pl.ds(pl.multiple_of(j * FF_CHUNK, FF_CHUNK), FF_CHUNK)
        return (
            pltpu.make_async_copy(gu_all.at[0, :, place], gate_w.at[s], load_sem.at[s, 1]),
            pltpu.make_async_copy(gu_all.at[1, :, place], up_w.at[s], load_sem.at[s, 2]),
        )

    per_tick = -(-steps // blocks)

    def ticks(unit_action, r):
        for k in range(per_tick):
            step = r * per_tick + k + 1
            when(step <= steps, functools.partial(unit_action, step))

    down_load(0, 0).start()

    @pl.loop(0, chunks)
    def _(j):
        s = lax.rem(j, 2)

        @pl.when(j + 1 < chunks)
        def _():
            down_load(j + 1, 1 - s).start()

        down_load(j, s).wait()

        @pl.loop(0, blocks)
        def _(r):
            at = pl.ds(pl.multiple_of(r * ROW_BLOCK, ROW_BLOCK), ROW_BLOCK)

            @pl.when(j == 0)
            def _():
                ticks(chunk_unit(0).relay, r)

            @pl.when((j == 1) & (r == 0))
            def _():
                chunk_unit(1).own()

            @pl.when(j == 2)
            def _():
                ticks(chunk_unit(0).relay_seq, r)

            @pl.when(j == 3)
            def _():
                ticks(chunk_unit(1).relay, r)

            @pl.when((j == 4) & (r == 0))
            def _():
                chunk_unit(2).own()

            grad_hidden[j, at, :] = dot_nt(cotangent[at, :], down_w[s]) + dot_nt(
                grad_low_down[at, :], first_down[j]
            )

    started.wait()
    chunk_unit(0).collect()
    for copy in gu_loads(0, 0):
        copy.start()
    down_load(0, 0).start()

    @pl.loop(0, chunks)
    def _(j):
        s = lax.rem(j, 2)
        for copy in (down_load(j, s),) + gu_loads(j, s):
            copy.wait()

        @pl.loop(0, blocks)
        def _(r):
            at = pl.ds(pl.multiple_of(r * ROW_BLOCK, ROW_BLOCK), ROW_BLOCK)

            @pl.when((r == 0) & (j + 3 < chunks))
            def _():
                chunk_unit(j + 3).own()

            @pl.when(j + 2 < chunks)
            def _():
                ticks(chunk_unit(j + 2).relay, r)

            @pl.when(j + 1 < chunks)
            def _():
                spread = -(-steps // max(blocks - 1, 1))
                for k in range(spread):
                    step = r * spread + k + 1
                    when(step <= steps, functools.partial(chunk_unit(j + 1).relay_seq, step))

                @pl.when(r == blocks - 1)
                def _():
                    chunk_unit(j + 1).collect()
                    for copy in (down_load(j + 1, 1 - s),) + gu_loads(j + 1, 1 - s):
                        copy.start()

            rows_in = second[at, :]
            gate = dot_nn(rows_in, gate_w[s]) + dot_nn(low_gu[0, at, :], second_gu[0, j])
            up = dot_nn(rows_in, up_w[s]) + dot_nn(low_gu[1, at, :], second_gu[1, j])
            back = grad_hidden[j, at, :]
            sigmoid = 1.0 / (1.0 + jnp.exp(-gate))
            active = gate * sigmoid
            hidden = (active * up).astype(BF16)
            grad_gate = (back * up * sigmoid * (1.0 + gate * (1.0 - sigmoid))).astype(BF16)
            grad_up = (back * active).astype(BF16)
            hidden_s[at, :] = hidden
            gate_s[at, :] = grad_gate
            up_s[at, :] = grad_up
            total[at, :] += dot_nn(hidden, down_w[s])
            grad_second[at, :] += dot_nt(grad_gate, gate_w[s]) + dot_nt(grad_up, up_w[s])
            low_down[at, :] += dot_nn(hidden, first_down[j])
            grad_low_gu[0, at, :] += dot_nt(grad_gate, second_gu[0, j])
            grad_low_gu[1, at, :] += dot_nt(grad_up, second_gu[1, j])

        base = j * FF_CHUNK
        for offset, left, right in (
            (0, grad_low_down[...], hidden_s),
            (hidden_size, low_gu[0], gate_s),
            (2 * hidden_size, low_gu[1], up_s),
        ):
            columns = pl.ds(pl.multiple_of(offset + base, LANES), FF_CHUNK)
            grads[:, columns] = dot_tn(left, right[...]).astype(BF16)

    half_low_down = (ADAPTER_SCALE * low_down[...] * mask).astype(BF16)
    block_out[...] = (total[...] + dot_nn(half_low_down, second_down[...])).astype(BF16)
    base = 3 * hidden_size
    grads[:, base + 2 * features : base + 3 * features] = dot_tn(half_low_down, cotangent[...]).astype(BF16)
    for k in range(2):
        back_low = (ADAPTER_SCALE * grad_low_gu[k] * mask).astype(BF16)
        columns = slice(base + k * features, base + (k + 1) * features)
        grads[:, columns] = dot_tn(back_low, second[...]).astype(BF16)
        grad_second[...] += dot_nt(back_low, first_gu[k])

    down_unit.drain()

    @pl.loop(0, chunks)
    def _(k):
        chunk_unit(k).drain()


def feed_forward(fsdp_size, per_sequence, grads_width, second, cotangent, after, pick, pick_t, adapters, own):
    tokens, features = second.shape
    hidden_size = own[0].shape[1]
    slots = pick.shape[1]
    chunks = hidden_size // FF_CHUNK
    return pl.pallas_call(
        functools.partial(feed_forward_kernel, fsdp_size, per_sequence),
        out_shape=(
            jax.ShapeDtypeStruct((tokens, features), BF16),
            jax.ShapeDtypeStruct((tokens, features), F32),
            jax.ShapeDtypeStruct((slots, grads_width), BF16),
            jax.ShapeDtypeStruct((2, features, hidden_size), BF16),
            jax.ShapeDtypeStruct((hidden_size, features), BF16),
        ),
        in_specs=[IN_VMEM, IN_VMEM, ANYWHERE] + [IN_VMEM] * 8 + [ANYWHERE] * 3,
        out_specs=(IN_VMEM, IN_VMEM, IN_VMEM, ANYWHERE, ANYWHERE),
        scratch_shapes=unit_sems(1 + chunks, fsdp_size // 2)
        + [pltpu.SemaphoreType.DMA((2, 3)), pltpu.SemaphoreType.DMA((3, 3))]
        + [pltpu.VMEM(member.shape, BF16) for member in own]
        + [
            pltpu.VMEM((tokens, features), F32),
            pltpu.VMEM((chunks, tokens, FF_CHUNK), F32),
            pltpu.VMEM((2, features, FF_CHUNK), BF16),
            pltpu.VMEM((2, features, FF_CHUNK), BF16),
            pltpu.VMEM((2, FF_CHUNK, features), BF16),
            pltpu.VMEM((tokens, FF_CHUNK), BF16),
            pltpu.VMEM((tokens, FF_CHUNK), BF16),
            pltpu.VMEM((tokens, FF_CHUNK), BF16),
            pltpu.VMEM((2, features, slots), BF16),
            pltpu.VMEM((chunks, FF_CHUNK, slots), BF16),
            pltpu.VMEM((2, chunks, slots, FF_CHUNK), BF16),
            pltpu.VMEM((slots, features), BF16),
            pltpu.VMEM((2, tokens, slots), BF16),
            pltpu.VMEM((tokens, slots), BF16),
            pltpu.VMEM((tokens, slots), F32),
            pltpu.VMEM((2, tokens, slots), F32),
        ],
        compiler_params=pltpu.CompilerParams(
            collective_id=1, has_side_effects=True, vmem_limit_bytes=VMEM_LIMIT
        ),
    )(second, cotangent, after, pick, pick_t, *adapters, *own)


class Shares:
    def __init__(self, devices, features, hidden_size):
        self.early_all = (3 * hidden_size + 3 * features) // LANES
        self.early = max(1, self.early_all // devices)
        self.early_used = min(self.early_all, self.early * devices)
        self.rest = self.early_all - self.early_used
        self.late_used = self.rest + 6 * features // LANES
        self.late = -(-self.late_used // devices)
        self.wide, self.narrow = hidden_size // LANES, features // LANES
        self.early_width = max(self.early_all, self.early * devices) * LANES
        self.late_width = self.late * devices * LANES

    def early_is_first(self, t):
        lowest = 3 * self.wide
        return (t < self.wide) | ((t >= lowest) & (t < lowest + 2 * self.narrow))

    def late_is_first(self, t):
        return (t >= self.rest) & (t < self.rest + 2 * self.narrow)


class Sum:
    def __init__(self, ring, seq_size, number, source, landing, tiles, is_first, refs, unit_sems_refs):
        self.ring, self.seq_size, self.source, self.landing = ring, seq_size, source, landing
        self.tiles, self.is_first = tiles, is_first
        self.send_sem, self.recv_sem, self.seq_sem, self.local_sem, self.got, self.result = refs
        self.devices = self.got.shape[0]
        self.me = ring.me * seq_size + ring.x
        self.place = landing.at[ring.me, ring.x]
        self.unit = Unit(ring, number, self.spot, unit_sems_refs)

    def spot(self, third, owner):
        size = 32 if isinstance(third, int) and third == 2 else 48
        return self.landing.at[owner, :, :, pl.ds(third * 48, size), :]

    def columns(self, d):
        width = self.tiles * LANES
        return self.source.at[:, pl.ds(pl.multiple_of(d * width, LANES), width)]

    def target(self, k):
        d = lax.rem(self.me + k, self.devices)
        return d, {"fsdp": d // self.seq_size, "seq": lax.rem(d, self.seq_size)}

    def piece(self, k):
        d, device = self.target(k)
        return pltpu.make_async_remote_copy(
            src_ref=self.columns(d),
            dst_ref=self.got.at[self.me],
            send_sem=self.send_sem.at[k],
            recv_sem=self.recv_sem.at[k],
            device_id=device,
            device_id_type=MESH,
        )

    def own(self):
        return pltpu.make_async_copy(self.columns(self.me), self.got.at[self.me], self.local_sem.at[0])

    def start(self):
        self.own().start()

        @pl.loop(1, self.devices)
        def _(k):
            self.piece(k).start()

    def add(self, chosen):
        self.own().wait()

        @pl.loop(1, self.devices)
        def _(k):
            self.piece(k).wait_recv()

        everything = self.got[...].reshape(self.devices * self.got.shape[1], self.tiles * LANES)
        summed = dot_tn(chosen, everything)
        for t in range(self.tiles):
            tile = summed[:, t * LANES : (t + 1) * LANES]
            self.result[t] = jnp.where(self.is_first(self.me * self.tiles + t), tile.T, tile).astype(BF16)
        store = pltpu.make_async_copy(self.result, self.place, self.local_sem.at[1])
        store.start()
        store.wait()
        for k in range(1, self.seq_size):
            self.across(k).start()

    def across(self, k):
        return pltpu.make_async_remote_copy(
            src_ref=self.place,
            dst_ref=self.place,
            send_sem=self.seq_sem.at[0, k],
            recv_sem=self.seq_sem.at[1, k],
            device_id={"seq": lax.rem(self.ring.x + k, self.seq_size)},
            device_id_type=MESH,
        )

    def crossed(self):
        for k in range(1, self.seq_size):
            self.across(k).wait_recv()

    def drain(self):
        self.unit.drain()
        for k in range(1, self.seq_size):
            self.across(k).wait_send()

        @pl.loop(1, self.devices)
        def _(k):
            self.piece(k).wait_send()


def mixer_back_kernel(sizes, per_sequence, shares, *refs):
    (
        grad_second, after, cotangent, block_in, mixed, conv, mixer_out, normed, low_in, low_out,
        in_first, in_second, out_first, out_second, pick_t, taps, gain_first, gain_second, weight_in, weight_out,
        grads_early,
    ) = refs[:21]
    grad_input, landing_early, landing_late = refs[21:24]
    units_refs = refs[24:28]
    early_refs, late_refs = refs[28:34], refs[34:40]
    pick_send, pick_recv, rim_sem, load_sem = refs[40:44]
    (
        picks, rim_out, rim_in, grad_after, after_s, mixed_s, conv_s, in_w, out_w, branch,
        grad_mixer, grad_mixed, low_out_back, low_in_back, late,
    ) = refs[44:]
    fsdp_size, seq_size = sizes
    devices = fsdp_size * seq_size
    ring = Ring(fsdp_size)
    tokens, features = after_s.shape
    slots = low_in.shape[1]
    sequences = tokens // per_sequence
    block = min(ROW_BLOCK, per_sequence)
    early = Sum(
        ring, seq_size, 0, grads_early, landing_early, shares.early, shares.early_is_first, early_refs, units_refs
    )
    later = Sum(ring, seq_size, 1, late, landing_late, shares.late, shares.late_is_first, late_refs, units_refs)
    loads = [
        pltpu.make_async_copy(a, b, load_sem.at[k])
        for k, (a, b) in enumerate(
            (
                (after, after_s),
                (grad_second, grad_after),
                (weight_out, out_w),
                (mixed, mixed_s),
                (conv, conv_s),
                (weight_in, in_w),
                (
                    grads_early.at[:, pl.ds(shares.early_used * LANES, max(shares.rest, 1) * LANES)],
                    late.at[:, pl.ds(0, max(shares.rest, 1) * LANES)],
                ),
            )
        )
    ]
    for copy in loads[:6]:
        copy.start()

    barrier = pltpu.get_barrier_semaphore()

    @pl.loop(1, devices)
    def _(k):
        pl.semaphore_signal(barrier, inc=1, device_id=early.target(k)[1], device_id_type=MESH)

    late[:, shares.late_used * LANES :] = jnp.zeros((slots, shares.late_width - shares.late_used * LANES), BF16)
    if shares.rest:
        loads[6].start()
    pl.semaphore_wait(barrier, devices - 1)

    def pick_piece(k):
        return pltpu.make_async_remote_copy(
            src_ref=pick_t,
            dst_ref=picks.at[early.me],
            send_sem=pick_send.at[k],
            recv_sem=pick_recv.at[k],
            device_id=early.target(k)[1],
            device_id_type=MESH,
        )

    picks[early.me] = pick_t[...]

    @pl.loop(1, devices)
    def _(k):
        pick_piece(k).start()

    early.start()
    for copy in loads[:3]:
        copy.wait()
    mask = slot_mask(block, slots, per_sequence)

    def rows_of(r):
        return pl.ds(pl.multiple_of(r * block, block), block)

    def masked(r, values):
        row = r * block + lax.broadcasted_iota(jnp.int32, (block, slots), 0)
        column = lax.broadcasted_iota(jnp.int32, (block, slots), 1)
        return jnp.where(row // per_sequence == column // R, ADAPTER_SCALE * values, 0.0).astype(BF16)

    @pl.loop(0, tokens // block)
    def _(r):
        at = rows_of(r)
        rows = after_s[at, :]
        inverse = lax.rsqrt(jnp.mean(rows * rows, axis=-1, keepdims=True) + EPSILON)
        unit_rows = rows * inverse
        scaled = grad_after[at, :] * gain_second[...]
        gradient = cotangent[at, :].astype(F32) + inverse * (
            scaled - unit_rows * jnp.mean(scaled * unit_rows, axis=-1, keepdims=True)
        )
        grad_after[at, :] = gradient
        rounded = gradient.astype(BF16)
        branch[at, :] = rounded
        back_low = masked(r, dot_nt(rounded, out_second[...]))
        low_out_back[at, :] = back_low
        grad_mixer[at, :] = dot_nt(rounded, out_w[...]) + dot_nt(back_low, out_first[...])

    for copy in loads[3:5]:
        copy.wait()
    middle = slice(features, 2 * features)
    for k in range(sequences):
        at = slice(k * per_sequence, k * per_sequence + 8)
        rim_out[k] = grad_mixer[at, :] * mixed_s[at, middle]
    rim = pltpu.make_async_remote_copy(
        src_ref=rim_out,
        dst_ref=rim_in,
        send_sem=rim_sem.at[0],
        recv_sem=rim_sem.at[1],
        device_id={"seq": lax.rem(ring.x + seq_size - 1, seq_size)},
        device_id_type=MESH,
    )
    rim.start()
    base = shares.rest * LANES
    late[:, base + features : base + 2 * features] = dot_tn(low_out_back[...], mixer_out[...]).astype(BF16)
    base += 2 * features
    late[:, base + 3 * features : base + 4 * features] = dot_tn(low_out[...], branch[...]).astype(BF16)
    rim.wait_recv()
    inner = (ring.x < seq_size - 1).astype(F32)

    @pl.loop(0, tokens // block)
    def _(r):
        at = rows_of(r)
        back = grad_mixer[at, :]
        through = back * mixed_s[at, middle]
        after_at = pl.ds(pl.multiple_of(jnp.minimum((r + 1) * block, tokens - 8), 8), 8)
        beyond = grad_mixer[after_at, :] * mixed_s[after_at, middle]
        last = lax.rem((r + 1) * block, per_sequence) == 0
        beyond = jnp.where(last, rim_in[(r * block) // per_sequence] * inner, beyond)
        extended = jnp.concatenate([through, beyond], axis=0)
        gated = (
            taps[2:3, :] * through + taps[1:2, :] * extended[1 : block + 1] + taps[0:1, :] * extended[2 : block + 2]
        )
        grad_mixed[at, :features] = (gated * mixed_s[at, 2 * features :]).astype(BF16)
        grad_mixed[at, middle] = (back * conv_s[at, :]).astype(BF16)
        grad_mixed[at, 2 * features :] = (gated * mixed_s[at, :features]).astype(BF16)
        low_in_back[at, :] = masked(r, dot_nt(grad_mixed[at, :], in_second[...]))

    late[:, base : base + 3 * features] = dot_tn(low_in[...], grad_mixed[...]).astype(BF16)
    base -= 2 * features
    late[:, base : base + features] = dot_tn(low_in_back[...], normed[...]).astype(BF16)
    if shares.rest:
        loads[6].wait()
    later.start()
    loads[5].wait()

    @pl.loop(1, devices)
    def _(k):
        pick_piece(k).wait_recv()

    def finish(r):
        at = rows_of(r)
        rows = block_in[at, :].astype(F32)
        inverse = lax.rsqrt(jnp.mean(rows * rows, axis=-1, keepdims=True) + EPSILON)
        unit_rows = rows * inverse
        gradient = dot_nt(grad_mixed[at, :], in_w[...]) + dot_nt(low_in_back[at, :], in_first[...])
        scaled = gradient * gain_first[...]
        grad_input[at, :] = (
            grad_after[at, :]
            + inverse * (scaled - unit_rows * jnp.mean(scaled * unit_rows, axis=-1, keepdims=True))
        ).astype(BF16)

    chosen = picks[...].reshape(devices * slots, LANES)
    early.add(chosen)
    parts = tokens // block
    half = parts // 2

    @pl.loop(0, half)
    def _(r):
        finish(r)

    early.crossed()
    early.unit.own()
    later.add(chosen)

    @pl.loop(half, parts)
    def _(r):
        finish(r)

    steps = early.unit.steps
    early.unit.relay(1)
    later.crossed()
    later.unit.own()
    for step in range(2, steps + 3):
        if step <= steps:
            early.unit.relay(step)
        if step >= 3:
            early.unit.relay_seq(step - 2)
        if step <= steps + 1:
            later.unit.relay(step - 1)
    for step in range(1, steps + 1):
        later.unit.relay_seq(step)
    early.unit.collect()
    later.unit.collect()
    early.drain()
    later.drain()
    rim.wait_send()

    @pl.loop(1, devices)
    def _(k):
        pick_piece(k).wait_send()


def mixer_back(sizes, per_sequence, shares, operands):
    fsdp_size, seq_size = sizes
    devices = fsdp_size * seq_size
    tokens, features = operands[0].shape
    slots = operands[8].shape[1]
    sequences = tokens // per_sequence

    def sum_refs(tiles):
        return [
            pltpu.SemaphoreType.DMA((devices,)),
            pltpu.SemaphoreType.DMA((devices,)),
            pltpu.SemaphoreType.DMA((2, seq_size)),
            pltpu.SemaphoreType.DMA((2,)),
            pltpu.VMEM((devices, slots, tiles * LANES), BF16),
            pltpu.VMEM((tiles, LANES, LANES), BF16),
        ]

    in_specs = [IN_VMEM] * len(operands)
    for k in (0, 1, 4, 5, 18, 19, 20):
        in_specs[k] = ANYWHERE
    return pl.pallas_call(
        functools.partial(mixer_back_kernel, sizes, per_sequence, shares),
        out_shape=(
            jax.ShapeDtypeStruct((tokens, features), BF16),
            jax.ShapeDtypeStruct((fsdp_size, seq_size, shares.early, LANES, LANES), BF16),
            jax.ShapeDtypeStruct((fsdp_size, seq_size, shares.late, LANES, LANES), BF16),
        ),
        in_specs=in_specs,
        out_specs=(IN_VMEM, ANYWHERE, ANYWHERE),
        scratch_shapes=unit_sems(2, fsdp_size // 2)
        + sum_refs(shares.early)
        + sum_refs(shares.late)
        + [
            pltpu.SemaphoreType.DMA((devices,)),
            pltpu.SemaphoreType.DMA((devices,)),
            pltpu.SemaphoreType.DMA((2,)),
            pltpu.SemaphoreType.DMA((7,)),
            pltpu.VMEM((devices, slots, LANES), BF16),
            pltpu.VMEM((sequences, 8, features), F32),
            pltpu.VMEM((sequences, 8, features), F32),
            pltpu.VMEM((tokens, features), F32),
            pltpu.VMEM((tokens, features), F32),
            pltpu.VMEM((tokens, 3 * features), F32),
            pltpu.VMEM((tokens, features), F32),
            pltpu.VMEM((features, 3 * features), BF16),
            pltpu.VMEM((features, features), BF16),
            pltpu.VMEM((tokens, features), BF16),
            pltpu.VMEM((tokens, features), F32),
            pltpu.VMEM((tokens, 3 * features), BF16),
            pltpu.VMEM((tokens, slots), BF16),
            pltpu.VMEM((tokens, slots), BF16),
            pltpu.VMEM((slots, shares.late_width), BF16),
        ],
        compiler_params=pltpu.CompilerParams(
            collective_id=2, has_side_effects=True, vmem_limit_bytes=VMEM_LIMIT
        ),
    )(*operands)


def spread_kernel(layout, early, late, *outs):
    for out, pieces in zip(outs, layout):
        for is_late, start, count, first in pieces:
            source = late if is_late else early
            offset = pieces[0][2] if len(pieces) > 1 and (is_late, start) == pieces[1][:2] else 0

            @pl.loop(0, count)
            def _(k, source=source, start=start, offset=offset, out=out, first=first):
                at = pl.ds(pl.multiple_of((offset + k) * LANES, LANES), LANES)
                tile = source[start + k].astype(F32)
                if first:
                    out[at, :] = tile
                else:
                    out[:, at] = tile


def spread(shares, early, late):
    wide, narrow, rest = shares.wide, shares.narrow, shares.rest
    low = 3 * wide
    layout = (
        ((True, rest, narrow, True),),
        ((True, rest + 2 * narrow, 3 * narrow, False),),
        ((True, rest + narrow, narrow, True),),
        ((True, rest + 5 * narrow, narrow, False),),
        ((False, low, narrow, True),),
        ((False, wide, wide, False),),
        ((False, low + narrow, narrow, True),),
        ((False, 2 * wide, wide, False),),
        ((False, 0, wide, True),),
        ((False, low + 2 * narrow, narrow - rest, False), (True, 0, rest, False)),
    )
    shapes = []
    for pieces in layout:
        length = sum(piece[2] for piece in pieces) * LANES
        shapes.append(jax.ShapeDtypeStruct((length, LANES) if pieces[0][3] else (LANES, length), F32))
    return pl.pallas_call(
        functools.partial(spread_kernel, layout),
        out_shape=tuple(shapes),
        in_specs=[IN_VMEM] * 2,
        out_specs=(IN_VMEM,) * len(shapes),
        compiler_params=pltpu.CompilerParams(vmem_limit_bytes=VMEM_LIMIT),
    )(early.reshape(-1, LANES, LANES), late.reshape(-1, LANES, LANES))


def rms_parts(values):
    inverse = lax.rsqrt(jnp.mean(values * values, axis=-1, keepdims=True) + EPSILON)
    return (inverse, values * inverse)


def per_device(
    block_input,
    output_grad,
    adapter_ids,
    in_weight,
    out_weight,
    gate_weight,
    up_weight,
    down_weight,
    conv_weight,
    first_gain,
    second_gain,
    infirst_adapter,
    insecond_adapter,
    outfirst_adapter,
    outsecond_adapter,
    gatefirst_adapter,
    gatesecond_adapter,
    upfirst_adapter,
    upsecond_adapter,
    downfirst_adapter,
    downsecond_adapter,
):
    batches, seq_count, local_len, features = block_input.shape
    sequences = batches * seq_count
    tokens = sequences * local_len
    fsdp_size, seq_size = lax.axis_size("fsdp"), lax.axis_size("seq")
    slots = sequences * R
    hidden_size = gate_weight.shape[1]
    shares = Shares(fsdp_size * seq_size, features, hidden_size)
    kernel = conv_weight.astype(F32)
    gain_first = first_gain.astype(F32)
    gain_second = second_gain.astype(F32)
    wanted = jnp.repeat(adapter_ids.reshape(sequences) * R, R) + jnp.tile(jnp.arange(R), sequences)
    pick = (lax.broadcasted_iota(jnp.int32, (LANES, slots), 0) == wanted[None, :]).astype(BF16)
    pick_t = (lax.broadcasted_iota(jnp.int32, (slots, LANES), 1) == wanted[:, None]).astype(BF16)
    mask = slot_mask(tokens, slots, local_len)
    in_first, out_first = (dot_nn(m, pick).astype(BF16) for m in (infirst_adapter, outfirst_adapter))
    in_second, out_second = (dot_nn(pick_t, m).astype(BF16) for m in (insecond_adapter, outsecond_adapter))

    weight_in, weight_out = gather_mixer(fsdp_size, in_weight, out_weight)
    inputs = block_input.reshape(tokens, features).astype(F32)
    cotangent = output_grad.reshape(tokens, features)
    inverse_first, unit_first = rms_parts(inputs)
    normed = (unit_first * gain_first).astype(BF16)
    low_in = (dot_nn(normed, in_first) * mask * ADAPTER_SCALE).astype(BF16)
    mixed_in = dot_nn(normed, weight_in) + dot_nn(low_in, in_second)
    first_part = mixed_in[:, :features]
    middle_part = mixed_in[:, features : 2 * features]
    last_part = mixed_in[:, 2 * features :]
    gated_values = (first_part * last_part).reshape(sequences, local_len, features)
    rim_rows = from_behind(gated_values[:, local_len - 2 :, :], "seq", 1)
    extended = jnp.concatenate([rim_rows, gated_values], axis=1)
    conv_out = (
        kernel[0] * extended[:, :local_len]
        + kernel[1] * extended[:, 1 : local_len + 1]
        + kernel[2] * extended[:, 2:]
    ).reshape(tokens, features)
    mixer_out = (middle_part * conv_out).astype(BF16)
    low_out = (dot_nn(mixer_out, out_first) * mask * ADAPTER_SCALE).astype(BF16)
    after_mixer = inputs + (dot_nn(mixer_out, weight_out) + dot_nn(low_out, out_second))
    inverse_second, unit_second = rms_parts(after_mixer)
    second = (unit_second * gain_second).astype(BF16)

    block_output, grad_second, grads_late, _, _ = feed_forward(
        fsdp_size,
        local_len,
        shares.early_width,
        second,
        cotangent,
        after_mixer,
        pick,
        pick_t,
        (
            gatefirst_adapter,
            gatesecond_adapter,
            upfirst_adapter,
            upsecond_adapter,
            downfirst_adapter,
            downsecond_adapter,
        ),
        (gate_weight, up_weight, down_weight),
    )

    grad_input, early, late = mixer_back(
        (fsdp_size, seq_size),
        local_len,
        shares,
        (
            grad_second,
            after_mixer,
            cotangent,
            block_input.reshape(tokens, features),
            mixed_in,
            conv_out,
            mixer_out,
            normed,
            low_in,
            low_out,
            in_first,
            in_second,
            out_first,
            out_second,
            pick_t,
            kernel,
            gain_first[None, :],
            gain_second[None, :],
            weight_in,
            weight_out,
            grads_late,
        ),
    )
    shape = block_input.shape
    return (block_output.reshape(shape), grad_input.reshape(shape)) + tuple(spread(shares, early, late))


def solution(mesh):
    return jax.shard_map(
        per_device,
        mesh=mesh,
        in_specs=(
            P(None, "fsdp", "seq", None),
            P(None, "fsdp", "seq", None),
            P(None, "fsdp"),
            P("fsdp", None),
            P("fsdp", None),
            P("fsdp", None),
            P("fsdp", None),
            P("fsdp", None),
            P(),
            P(),
            P(),
            P(),
            P(),
            P(),
            P(),
            P(),
            P(),
            P(),
            P(),
            P(),
            P(),
        ),
        out_specs=(
            P(None, "fsdp", "seq", None),
            P(None, "fsdp", "seq", None),
            P(),
            P(),
            P(),
            P(),
            P(),
            P(),
            P(),
            P(),
            P(),
            P(),
        ),
        check_vma=False,
    )
```

```python
import functools

import jax
import jax.numpy as jnp
from jax import lax
from jax.experimental import pallas as pl
from jax.experimental.pallas import tpu as pltpu
from jax.sharding import PartitionSpec as P

R = 16
LANES = 128
EPSILON = 1e-05
ADAPTER_SCALE = 0.5
MESH = pl.DeviceIdType.MESH
BF16 = jnp.bfloat16
F32 = jnp.float32
VMEM_LIMIT = 62 * 1024 * 1024
FF_CHUNK = 512
ROW_BLOCK = 256
WIDE_BLOCK = 512
VMEM_LIMIT_FRONT = 63 * 1024 * 1024


def dot_nn(left, right):
    return jnp.dot(left, right, preferred_element_type=F32)


def dot_nt(left, right):
    return lax.dot_general(left, right, (((1,), (1,)), ((), ())), preferred_element_type=F32)


def dot_tn(left, right):
    return lax.dot_general(left, right, (((0,), (0,)), ((), ())), preferred_element_type=F32)


def when(condition, action):
    if isinstance(condition, bool):
        if condition:
            action()
    else:
        pl.when(condition)(action)


class Ring:
    def __init__(self, fsdp_size):
        self.count = fsdp_size // 2
        self.me = lax.axis_index("fsdp")
        self.core = lax.rem(self.me, 2)
        chip = self.me // 2
        self.grid = fsdp_size == 16
        if self.grid:
            z, y = chip // 2, lax.rem(chip, 2)
            self.place = y * z + (1 - y) * (7 - z)
        else:
            self.place = chip
        x = lax.axis_index("seq")
        self.x = x
        self.role = lax.rem(x, 2)
        self.to_next = {"fsdp": self.device(lax.rem(self.place + 1, self.count))}
        self.to_prev = {"fsdp": self.device(lax.rem(self.place + self.count - 1, self.count))}
        self.to_core = {"fsdp": self.me + 1 - 2 * self.core}
        self.to_seq = {"seq": x + 1 - 2 * self.role}

    def device(self, place):
        if self.grid:
            y = 1 - place // 4
            z = y * place + (1 - y) * (7 - place)
            return (z * 2 + y) * 2 + self.core
        return place * 2 + self.core

    def at_step(self, direction, step):
        if direction == 0:
            return self.device(lax.rem(self.place + self.count - step, self.count))
        return self.device(lax.rem(self.place + step, self.count))

    def greet(self, seq_size):
        barrier = pltpu.get_barrier_semaphore()
        devices = [self.to_next, self.to_prev, self.to_core, self.to_seq]
        if seq_size > 2:
            devices.append({"seq": lax.rem(self.x + seq_size - 1, seq_size)})
        for device in devices:
            pl.semaphore_signal(barrier, inc=1, device_id=device, device_id_type=MESH)
        pl.semaphore_wait(barrier, len(devices))


class Unit:
    def __init__(self, ring, number, spot, sems):
        self.ring, self.number, self.spot = ring, number, spot
        self.send, self.ring_sem, self.seq_sem, self.core_sem = sems
        half = ring.count // 2
        self.reaches = ((half, ring.count - 1 - half), (ring.count - 1 - half, half))
        self.steps = half
        self.others = ring.count - 1

    def copy(self, spot, slot, sem, device):
        return pltpu.make_async_remote_copy(
            src_ref=spot,
            dst_ref=spot,
            send_sem=self.send.at[self.number, slot],
            recv_sem=sem,
            device_id=device,
            device_id_type=MESH,
        )

    def arrived(self, spot, sem):
        self.copy(spot, 0, sem, self.ring.to_next).wait_recv()

    def own(self):
        ring, n = self.ring, self.number
        for slot, third in ((0, ring.role), (1, 2)):
            spot = self.spot(third, ring.me)
            self.copy(spot, 2 * slot, self.ring_sem.at[n, slot, 0], ring.to_next).start()
            self.copy(spot, 2 * slot + 1, self.ring_sem.at[n, slot, self.others - 1], ring.to_prev).start()
        for k, third in enumerate((ring.role, 1 - ring.role, 2)):
            self.copy(self.spot(third, ring.me), 4 + k, self.core_sem.at[n, third, 0], ring.to_core).start()

    def relay(self, step):
        ring, n, others = self.ring, self.number, self.others
        for slot, third in ((0, ring.role), (1, 2)):
            for direction in (0, 1):
                reach = self.reaches[slot][direction]
                lane = step - 1 if direction == 0 else others - step
                spot = self.spot(third, ring.at_step(direction, step))

                def forward(slot=slot, direction=direction, lane=lane, spot=spot):
                    onward = self.ring_sem.at[n, slot, lane + 1 - 2 * direction]
                    target = (ring.to_next, ring.to_prev)[direction]
                    self.copy(spot, 7 + slot * others + lane, onward, target).start()

                def take(slot=slot, third=third, reach=reach, lane=lane, spot=spot, forward=forward):
                    self.arrived(spot, self.ring_sem.at[n, slot, lane])
                    when(step < reach, forward)
                    if slot == 0:
                        self.copy(spot, 7 + 2 * others + lane, self.seq_sem.at[n, lane], ring.to_seq).start()
                    core = self.core_sem.at[n, third, 1 + lane]
                    self.copy(spot, 7 + (3 + slot) * others + lane, core, ring.to_core).start()

                when(step <= reach, take)

    def relay_seq(self, step):
        ring, n, others = self.ring, self.number, self.others
        third = 1 - ring.role
        for direction in (0, 1):
            reach = self.reaches[0][direction]
            lane = step - 1 if direction == 0 else others - step
            spot = self.spot(third, ring.at_step(direction, step))

            def take(lane=lane, spot=spot):
                self.arrived(spot, self.seq_sem.at[n, lane])
                core = self.core_sem.at[n, third, 1 + lane]
                self.copy(spot, 7 + 5 * others + lane, core, ring.to_core).start()

            when(step <= reach, take)

    def collect(self):
        for third in range(3):
            for lane in range(self.others + 1):
                self.arrived(self.spot(third, self.ring.me), self.core_sem.at[self.number, third, lane])

    def drain(self):
        ring, others = self.ring, self.others

        def done(third, slot):
            self.copy(self.spot(third, ring.me), slot, self.seq_sem.at[self.number, 0], ring.to_next).wait_send()

        for slot, third in ((0, 0), (1, 2)):
            done(third, 2 * slot)
            done(third, 2 * slot + 1)
            for direction in (0, 1):
                reach = self.reaches[slot][direction]
                for step in range(1, reach + 1):
                    lane = step - 1 if direction == 0 else others - step
                    if step < reach:
                        done(third, 7 + slot * others + lane)
                    done(third, 7 + (3 + slot) * others + lane)
        for lane in range(others):
            done(0, 7 + 2 * others + lane)
            done(0, 7 + 5 * others + lane)
        for k, third in enumerate((0, 0, 2)):
            done(third, 4 + k)


def unit_sems(units, count):
    return [
        pltpu.SemaphoreType.DMA((units, 7 + 6 * (count - 1))),
        pltpu.SemaphoreType.DMA((units, 2, count - 1)),
        pltpu.SemaphoreType.DMA((units, count - 1)),
        pltpu.SemaphoreType.DMA((units, 3, count)),
    ]


def move_in(moves, sems):
    inward = [pltpu.make_async_copy(a, b, sems.at[0, k]) for k, (a, b, _) in enumerate(moves)]
    outward = [pltpu.make_async_copy(b, c, sems.at[1, k]) for k, (_, b, c) in enumerate(moves)]
    for copy in inward:
        copy.start()
    for first, second in zip(inward, outward):
        first.wait()
        second.start()
    return outward


def row_spot(landing, rows, start, size, third, owner):
    return landing.at[pl.ds(owner * rows + start + third * size, size), :]


def column_spot(landing, rows, width, last, third, owner):
    size = last if isinstance(third, int) and third == 2 else width
    start = third * width if isinstance(third, int) else pl.multiple_of(third * width, LANES)
    return landing.at[pl.ds(owner * rows, rows), pl.ds(start, size)]


def chunk_spot(landing, rows, size, chunk, third, owner):
    start = pl.multiple_of((chunk * 3 + third) * size, LANES)
    return landing.at[:, pl.ds(owner * rows, rows), pl.ds(start, size)]


def share_out(actions, ticks):
    cuts = [len(actions) * k // ticks for k in range(ticks + 1)]
    return [actions[cuts[k] : cuts[k + 1]] for k in range(ticks)]


def run_tick(lists, tick):
    for k, actions in enumerate(lists):

        @pl.when(tick == k)
        def _(actions=actions):
            for action in actions:
                action()


def rms_unit(rows):
    inverse = lax.rsqrt(jnp.mean(rows * rows, axis=-1, keepdims=True) + EPSILON)
    return inverse, rows * inverse


def rms_back(scaled, inverse, unit_rows):
    return inverse * (scaled - unit_rows * jnp.mean(scaled * unit_rows, axis=-1, keepdims=True))


ANYWHERE = pl.BlockSpec(memory_space=pl.ANY)
IN_VMEM = pl.BlockSpec(memory_space=pltpu.VMEM)


def front_kernel(sizes, per_sequence, *refs):
    (
        block_in, cotangent, pick, pick_t, taps, gain_first, gain_second,
        in_first, in_second, out_first, out_second, gate_first, up_first, down_second,
        gate_second, up_second, down_first, in_own, out_own, gate_own, up_own, down_own,
    ) = refs[:22]
    (
        grad_second, grads, low_in, low_out, in_first_s, in_second_s, out_first_s, out_second_s,
        block_out, after_out, mixed_out, conv_out, mixer_out, normed_out, in_all, out_all, gu_all, down_all,
    ) = refs[22:40]
    sems, local_sem, load_sem, stage_sem, rim_sem, out_sem = refs[40:44], refs[44], refs[45], refs[46], refs[47], refs[48]
    held = refs[49:54]
    (
        total, wide, gate_w, up_w, down_w, normed, mixer, second, gate_up_first, first_down, second_gu, second_down,
        low_gu, grad_low_down, low_down, grad_low_gu, partial, rim_out, rim_in,
    ) = refs[54:]
    fsdp_size, seq_size = sizes
    ring = Ring(fsdp_size)
    rows, down_rows = gate_own.shape[0], down_own.shape[0]
    tokens, features = cotangent.shape
    hidden_size = gate_own.shape[1]
    chunks = hidden_size // FF_CHUNK
    sequences = tokens // per_sequence
    block = min(ROW_BLOCK, per_sequence)
    wide_block = min(WIDE_BLOCK, tokens)
    blocks, wide_blocks = tokens // block, tokens // wide_block
    slots = pick.shape[1]
    mine = pl.ds(ring.me * rows, rows)
    moved = move_in(
        [
            (in_own, held[0], in_all.at[mine, :]),
            (out_own, held[1], out_all.at[mine, :]),
            (down_own, held[4], down_all.at[pl.ds(ring.me * down_rows, down_rows), :]),
            (gate_own, held[2], gu_all.at[0, mine, :]),
            (up_own, held[3], gu_all.at[1, mine, :]),
        ],
        local_sem,
    )
    stages = []
    for k in range(-(-hidden_size // features)):
        width = min(features, hidden_size - k * features)
        part, lanes = pl.ds(k * features, width), pl.ds(k * LANES, LANES)
        stages += [
            (gate_second.at[:, part], second.at[lanes, pl.ds(0, width)]),
            (up_second.at[:, part], normed.at[lanes, pl.ds(0, width)]),
            (down_first.at[part, :], mixer.at[pl.ds(0, width), lanes]),
        ]
    stages = [pltpu.make_async_copy(a, b, stage_sem.at[k]) for k, (a, b) in enumerate(stages)]
    for copy in stages:
        copy.start()
    ring.greet(seq_size)

    part = in_all.shape[1] // 3
    out_x = 3 * features // 8
    unit_list = [
        Unit(ring, 0, functools.partial(column_spot, in_all, rows, part, part), sems),
        Unit(ring, 1, functools.partial(column_spot, out_all, rows, out_x, features - 2 * out_x), sems),
    ]
    pieces = 2 if down_rows % 96 == 0 else 1
    for k in range(pieces):
        size = down_rows // pieces // 3
        unit_list.append(Unit(ring, 2 + k, functools.partial(row_spot, down_all, down_rows, 3 * size * k, size), sems))
    fixed = len(unit_list)
    comm_chunks = 2 * chunks // 3
    comm_size = hidden_size // comm_chunks // 3

    def chunk_unit(k):
        return Unit(ring, fixed + k, functools.partial(chunk_spot, gu_all, rows, comm_size, k), sems)

    steps = unit_list[0].steps
    stepped = steps == 4 and wide_blocks == 2
    starts = {0: 0, 1: 1, 2: 2, 3: 4}
    entries = []

    def enter(start, unit, last=10**6):
        plan = [(start, 0, unit.own)]
        for step in range(1, steps + 1):
            plan.append((start + step, 1, functools.partial(unit.relay, step)))
            plan.append((start + step + 1, 2, functools.partial(unit.relay_seq, step)))
        entries.extend((slot, kind, unit.number, action) for slot, kind, action in plan if slot <= last)

    for k, unit in enumerate(unit_list):
        enter(starts[k], unit)
    chunk_start = 2 * fixed - 2
    if stepped:
        for k in range(comm_chunks):
            if 2 * k <= 6:
                enter(chunk_start + 2 * k, chunk_unit(k), chunk_start + 6)
    else:
        enter(chunk_start, chunk_unit(0))
    entries.sort(key=lambda entry: entry[:3])

    def until(numbers):
        last = max(k for k, entry in enumerate(entries) if entry[2] in numbers)
        taken = [entry[3] for entry in entries[: last + 1]]
        del entries[: last + 1]
        return taken

    for copy in moved:
        copy.wait()
    early = until((0,))
    early[0]()
    early[1]()

    def rows_of(r, size=block):
        return pl.ds(pl.multiple_of(r * size, size), size)

    def masked(r, values, size=block):
        row = r * size + lax.broadcasted_iota(jnp.int32, (size, slots), 0)
        column = lax.broadcasted_iota(jnp.int32, (size, slots), 1)
        return jnp.where(row // per_sequence == column // R, ADAPTER_SCALE * values, 0.0).astype(BF16)

    for copy in stages:
        copy.wait()
    for k in range(-(-hidden_size // features)):
        width = min(features, hidden_size - k * features)
        at, lanes = slice(k * features, k * features + width), slice(k * LANES, (k + 1) * LANES)
        second_gu[0, :, at] = dot_nn(pick_t[...], second[lanes, :width]).astype(BF16)
        second_gu[1, :, at] = dot_nn(pick_t[...], normed[lanes, :width]).astype(BF16)
        first_down[at, :] = dot_nn(mixer[:width, lanes], pick[...]).astype(BF16)
    second_down[...] = dot_nn(pick_t[...], down_second[...]).astype(BF16)
    in_second_s[...] = dot_nn(pick_t[...], in_second[...]).astype(BF16)
    out_second_s[...] = dot_nn(pick_t[...], out_second[...]).astype(BF16)
    in_first_s[...] = dot_nn(in_first[...], pick[...]).astype(BF16)
    out_first_s[...] = dot_nn(out_first[...], pick[...]).astype(BF16)
    gate_up_first[0] = dot_nn(gate_first[...], pick[...]).astype(BF16)
    gate_up_first[1] = dot_nn(up_first[...], pick[...]).astype(BF16)

    @pl.loop(0, blocks)
    def _(r):
        at = rows_of(r)
        normed_rows = (rms_unit(block_in[at, :].astype(F32))[1] * gain_first[...]).astype(BF16)
        normed[at, :] = normed_rows
        low_in[at, :] = masked(r, dot_nn(normed_rows, in_first_s[...]))
        grad_low_down[at, :] = masked(r, dot_nt(cotangent[at, :], second_down[...]))
        grad_second[at, :] = jnp.zeros((block, features), F32)

    low_down[...] = jnp.zeros_like(low_down)
    grad_low_gu[...] = jnp.zeros_like(grad_low_gu)
    for action in early[2:]:
        action()
    unit_list[0].collect()

    half = FF_CHUNK
    middle, last_part, conv_part = (slice(k * features, (k + 1) * features) for k in (1, 2, 3))
    in_loads = []
    for k in range(2):
        for part_number, buffer in ((0, gate_w), (1, up_w)):
            columns = pl.ds(part_number * features + k * half, half)
            in_loads.append(pltpu.make_async_copy(in_all.at[:, columns], buffer.at[k], load_sem.at[k, part_number]))
        place = in_all.at[pl.ds(k * half, half), pl.ds(2 * features, features)]
        in_loads.append(pltpu.make_async_copy(place, down_w.at[k], load_sem.at[k, 2]))
    for copy in in_loads:
        copy.start()
    for copy in in_loads:
        copy.wait()
    lists = share_out(until((1,)), blocks)

    @pl.loop(0, blocks)
    def _(r):
        run_tick(lists, r)
        at = rows_of(r)
        values, low = normed[at, :], low_in[at, :]
        for part_number, buffer in ((0, gate_w), (1, up_w)):
            for k in range(2):
                start = part_number * features + k * half
                columns = slice(start, start + half)
                wide[at, columns] = dot_nn(values, buffer[k]) + dot_nn(low, in_second_s[:, columns])
        wide[at, last_part] = (
            dot_nn(values[:, :half], down_w[0])
            + dot_nn(values[:, half:], down_w[1])
            + dot_nn(low, in_second_s[:, last_part])
        )

    unit_list[1].collect()
    out_loads = [
        pltpu.make_async_copy(out_all.at[:, pl.ds(k * half, half)], gate_w.at[k], load_sem.at[k, 0]) for k in range(2)
    ]
    for copy in out_loads:
        copy.start()
    for k in range(sequences):
        at = slice((k + 1) * per_sequence - 8, (k + 1) * per_sequence)
        rim_out[k] = wide[at, :features] * wide[at, last_part]
    rim = pltpu.make_async_remote_copy(
        src_ref=rim_out,
        dst_ref=rim_in,
        send_sem=rim_sem.at[0],
        recv_sem=rim_sem.at[1],
        device_id={"seq": lax.rem(ring.x + 1, seq_size)},
        device_id_type=MESH,
    )
    rim.start()
    mixed_store = pltpu.make_async_copy(wide.at[:, pl.ds(0, 3 * features)], mixed_out, out_sem.at[0])
    mixed_store.start()
    normed_store = pltpu.make_async_copy(normed.at[pl.ds(0, tokens), :], normed_out, out_sem.at[1])
    normed_store.start()
    for copy in out_loads:
        copy.wait()
    rim.wait_recv()
    inner = (ring.x > 0).astype(F32)
    lists = share_out(until(range(2, fixed)), blocks)

    @pl.loop(0, blocks)
    def _(r):
        run_tick(lists, r)
        at = rows_of(r)
        gated = wide[at, :features] * wide[at, last_part]
        before_at = pl.ds(pl.multiple_of(jnp.maximum(r * block - 8, 0), 8), 8)
        before = wide[before_at, :features] * wide[before_at, last_part]
        first = lax.rem(r * block, per_sequence) == 0
        before = jnp.where(first, rim_in[(r * block) // per_sequence] * inner, before)
        extended = jnp.concatenate([before, gated], axis=0)
        convolved = (
            taps[0:1, :] * extended[6 : block + 6] + taps[1:2, :] * extended[7 : block + 7] + taps[2:3, :] * gated
        )
        wide[at, conv_part] = convolved
        mixed = (wide[at, middle] * convolved).astype(BF16)
        mixer[at, :] = mixed
        low = masked(r, dot_nn(mixed, out_first_s[...]))
        low_out[at, :] = low
        branch = jnp.concatenate([dot_nn(mixed, gate_w[0]), dot_nn(mixed, gate_w[1])], axis=1)
        after = block_in[at, :].astype(F32) + (branch + dot_nn(low, out_second_s[...]))
        total[at, :] = after
        second_rows = (rms_unit(after)[1] * gain_second[...]).astype(BF16)
        second[at, :] = second_rows
        for k in range(2):
            low_gu[k, at, :] = masked(r, dot_nn(second_rows, gate_up_first[k]))

    stores = [
        pltpu.make_async_copy(wide.at[:, pl.ds(3 * features, features)], conv_out, out_sem.at[2]),
        pltpu.make_async_copy(mixer.at[pl.ds(0, tokens), :], mixer_out, out_sem.at[3]),
        pltpu.make_async_copy(total, after_out, out_sem.at[4]),
    ]
    for copy in stores:
        copy.start()
    for unit in unit_list[2:]:
        unit.collect()

    def down_load(j, s):
        return pltpu.make_async_copy(down_all.at[rows_of(j, FF_CHUNK), :], down_w.at[s], load_sem.at[s, 2])

    def gu_loads(j, s):
        place = rows_of(j, FF_CHUNK)
        return (
            pltpu.make_async_copy(gu_all.at[0, :, place], gate_w.at[s], load_sem.at[s, 0]),
            pltpu.make_async_copy(gu_all.at[1, :, place], up_w.at[s], load_sem.at[s, 1]),
        )

    down_load(0, 0).start()
    mixed_store.wait()
    for copy in stores:
        copy.wait()
    lists = share_out([entry[3] for entry in entries], chunks)

    @pl.loop(0, chunks)
    def _(j):
        s = lax.rem(j, 2)

        @pl.when(j + 1 < chunks)
        def _():
            down_load(j + 1, 1 - s).start()

        down_load(j, s).wait()
        run_tick(lists, j)
        columns = rows_of(j, FF_CHUNK)

        @pl.loop(0, wide_blocks)
        def _(r):
            at = rows_of(r, wide_block)
            wide[at, columns] = dot_nt(cotangent[at, :], down_w[s]) + dot_nt(
                grad_low_down[at, :], first_down[columns, :]
            )

    chunk_unit(0).collect()

    def begin(j, s):
        for copy in (down_load(j, s),) + gu_loads(j, s):
            copy.start()

    begin(0, 0)

    def guarded(k, action):
        when(k < comm_chunks, lambda: action(chunk_unit(k)))

    def whole_unit(k, with_own):
        unit = chunk_unit(k)
        if with_own:
            unit.own()
        for step in range(1, steps + 1):
            unit.relay(step)
        for step in range(1, steps + 1):
            unit.relay_seq(step)
        unit.collect()

    def group_ticks(i, s):
        n = 2 * i

        def go(k, name, *step):
            return lambda: guarded(n + k, lambda unit: getattr(unit, name)(*step))

        def take(k, chunk):
            def action():
                chunk_unit(n + k).collect()
                begin(3 * i + chunk, lax.rem(s + chunk, 2))

            return action

        def only(chunk):
            return lambda: begin(3 * i + chunk, lax.rem(s + chunk, 2))

        more = i + 1 < chunks // 3
        if not stepped:
            return {
                (0, 0): [lambda: whole_unit(n + 1, True), only(1)],
                (1, 0): [only(2)],
                (2, 0): [lambda: when(more, lambda: (whole_unit(n + 2, True), only(3)())[0])],
            }
        return {
            (0, 0): [go(2, "relay", 3), go(3, "relay", 1), go(1, "relay_seq", 4), go(2, "relay_seq", 2)],
            (0, 1): [take(1, 1), go(4, "own"), go(2, "relay", 4), go(3, "relay", 2), go(2, "relay_seq", 3), go(3, "relay_seq", 1)],
            (1, 0): [go(3, "relay", 3), go(4, "relay", 1), go(2, "relay_seq", 4), go(3, "relay_seq", 2)],
            (1, 1): [only(2), go(5, "own"), go(3, "relay", 4), go(4, "relay", 2)],
            (2, 0): [go(3, "relay_seq", 3), go(4, "relay_seq", 1)],
            (2, 1): [lambda: when(more, take(2, 3))],
        }

    @pl.loop(0, chunks // 3)
    def _(i):
        for c in range(3):
            j = 3 * i + c
            s = lax.rem(j, 2)
            columns = rows_of(j, FF_CHUNK)
            for copy in (down_load(j, s),) + gu_loads(j, s):
                copy.wait()
            ticks = group_ticks(i, lax.rem(3 * i, 2))
            partial[...] = jnp.zeros_like(partial)

            @pl.loop(0, wide_blocks)
            def _(r, c=c, j=j, s=s, columns=columns, ticks=ticks):
                for (wanted, tick), actions in ticks.items():
                    if wanted == c:

                        @pl.when(r == tick)
                        def _(actions=actions):
                            for action in actions:
                                action()

                at = rows_of(r, wide_block)
                values = second[at, :]
                lows = (grad_low_down[at, :], low_gu[0, at, :], low_gu[1, at, :])
                gate = dot_nn(values, gate_w[s]) + dot_nn(lows[1], second_gu[0, :, columns])
                up = dot_nn(values, up_w[s]) + dot_nn(lows[2], second_gu[1, :, columns])
                back = wide[at, columns]
                sigmoid = 1.0 / (1.0 + jnp.exp(-gate))
                active = gate * sigmoid
                hidden = (active * up).astype(BF16)
                grad_gate = (back * up * (sigmoid + active * (1.0 - sigmoid))).astype(BF16)
                grad_up = (back * active).astype(BF16)
                total[at, :] += dot_nn(hidden, down_w[s])
                grad_second[at, :] += dot_nt(grad_gate, gate_w[s]) + dot_nt(grad_up, up_w[s])
                low_down[at, :] += dot_nn(hidden, first_down[columns, :])
                grad_low_gu[0, at, :] += dot_nt(grad_gate, second_gu[0, :, columns])
                grad_low_gu[1, at, :] += dot_nt(grad_up, second_gu[1, :, columns])
                for k, right in enumerate((hidden, grad_gate, grad_up)):
                    partial[k] += dot_tn(lows[k], right)

            for k in range(3):
                place = pl.ds(pl.multiple_of(k * hidden_size + j * FF_CHUNK, FF_CHUNK), FF_CHUNK)
                grads[:, place] = partial[k].astype(BF16)

    normed_store.wait()
    base = 3 * hidden_size

    @pl.loop(0, blocks)
    def _(r):
        at = rows_of(r)
        low = masked(r, low_down[at, :])
        grad_low_down[at, :] = low
        normed[at, :] = (total[at, :] + dot_nn(low, second_down[...])).astype(BF16)
        for k in range(2):
            back_low = masked(r, grad_low_gu[k, at, :])
            low_gu[k, at, :] = back_low
            grad_second[at, :] += dot_nt(back_low, gate_up_first[k])

    block_store = pltpu.make_async_copy(normed.at[pl.ds(0, tokens), :], block_out, out_sem.at[1])
    block_store.start()
    grads[:, base + 2 * features : base + 3 * features] = dot_tn(grad_low_down[...], cotangent[...]).astype(BF16)
    for k in range(2):
        columns = slice(base + k * features, base + (k + 1) * features)
        grads[:, columns] = dot_tn(low_gu[k], second[:tokens, :]).astype(BF16)

    for unit in unit_list:
        unit.drain()

    @pl.loop(0, comm_chunks)
    def _(k):
        chunk_unit(k).drain()

    rim.wait_send()
    block_store.wait()


def front(sizes, per_sequence, grads_width, operands):
    fsdp_size, seq_size = sizes
    block_in, cotangent, pick = operands[:3]
    own = operands[-5:]
    tokens, features = cotangent.shape
    hidden_size = own[2].shape[1]
    slots = pick.shape[1]
    sequences = tokens // per_sequence
    units = 4 + 2 * (hidden_size // FF_CHUNK) // 3
    tall = max(tokens, features)
    stages = 3 * -(-hidden_size // features)

    def shape(*dims, kind=BF16):
        return jax.ShapeDtypeStruct(dims, kind)

    return pl.pallas_call(
        functools.partial(front_kernel, sizes, per_sequence),
        out_shape=(
            shape(tokens, features, kind=F32),
            shape(slots, grads_width),
            shape(tokens, slots),
            shape(tokens, slots),
            shape(features, slots),
            shape(slots, 3 * features),
            shape(features, slots),
            shape(slots, features),
            shape(tokens, features),
            shape(tokens, features, kind=F32),
            shape(tokens, 3 * features, kind=F32),
            shape(tokens, features, kind=F32),
            shape(tokens, features),
            shape(tokens, features),
            shape(features, 3 * features),
            shape(features, features),
            shape(2, features, hidden_size),
            shape(hidden_size, features),
        ),
        in_specs=[IN_VMEM] * 14 + [ANYWHERE] * 8,
        out_specs=(IN_VMEM,) * 8 + (ANYWHERE,) * 10,
        scratch_shapes=unit_sems(units, fsdp_size // 2)
        + [
            pltpu.SemaphoreType.DMA((2, 5)),
            pltpu.SemaphoreType.DMA((2, 3)),
            pltpu.SemaphoreType.DMA((stages,)),
            pltpu.SemaphoreType.DMA((2,)),
            pltpu.SemaphoreType.DMA((5,)),
        ]
        + [pltpu.VMEM(member.shape, BF16) for member in own]
        + [
            pltpu.VMEM((tokens, features), F32),
            pltpu.VMEM((tokens, hidden_size), F32),
            pltpu.VMEM((2, features, FF_CHUNK), BF16),
            pltpu.VMEM((2, features, FF_CHUNK), BF16),
            pltpu.VMEM((2, FF_CHUNK, features), BF16),
            pltpu.VMEM((tall, features), BF16),
            pltpu.VMEM((tall, features), BF16),
            pltpu.VMEM((tall, features), BF16),
            pltpu.VMEM((2, features, slots), BF16),
            pltpu.VMEM((hidden_size, slots), BF16),
            pltpu.VMEM((2, slots, hidden_size), BF16),
            pltpu.VMEM((slots, features), BF16),
            pltpu.VMEM((2, tokens, slots), BF16),
            pltpu.VMEM((tokens, slots), BF16),
            pltpu.VMEM((tokens, slots), F32),
            pltpu.VMEM((2, tokens, slots), F32),
            pltpu.VMEM((3, slots, FF_CHUNK), F32),
            pltpu.VMEM((sequences, 8, features), F32),
            pltpu.VMEM((sequences, 8, features), F32),
        ],
        compiler_params=pltpu.CompilerParams(
            collective_id=0, has_side_effects=True, vmem_limit_bytes=VMEM_LIMIT_FRONT
        ),
    )(*operands)


class Shares:
    def __init__(self, devices, features, hidden_size):
        self.early_all = (3 * hidden_size + 3 * features) // LANES
        self.early = max(1, self.early_all // devices)
        self.early_used = min(self.early_all, self.early * devices)
        self.rest = self.early_all - self.early_used
        self.late_used = self.rest + 6 * features // LANES
        self.late = -(-self.late_used // devices)
        self.wide, self.narrow = hidden_size // LANES, features // LANES
        self.early_width = max(self.early_all, self.early * devices) * LANES
        self.late_width = self.late * devices * LANES

    def early_is_first(self, t):
        lowest = 3 * self.wide
        return (t < self.wide) | ((t >= lowest) & (t < lowest + 2 * self.narrow))

    def late_is_first(self, t):
        return (t >= self.rest) & (t < self.rest + 2 * self.narrow)


class Sum:
    def __init__(self, ring, seq_size, number, source, landing, tiles, is_first, refs, unit_sems_refs):
        self.ring, self.seq_size, self.source, self.landing = ring, seq_size, source, landing
        self.tiles, self.is_first = tiles, is_first
        self.send_sem, self.recv_sem, self.seq_sem, self.local_sem, self.got, self.result = refs
        self.devices = self.got.shape[0]
        self.me = ring.me * seq_size + ring.x
        self.place = landing.at[ring.me, ring.x]
        self.unit = Unit(ring, number, self.spot, unit_sems_refs)

    def spot(self, third, owner):
        size = 32 if isinstance(third, int) and third == 2 else 48
        return self.landing.at[owner, :, :, pl.ds(third * 48, size), :]

    def columns(self, d):
        width = self.tiles * LANES
        return self.source.at[:, pl.ds(pl.multiple_of(d * width, LANES), width)]

    def target(self, k):
        d = lax.rem(self.me + k, self.devices)
        return d, {"fsdp": d // self.seq_size, "seq": lax.rem(d, self.seq_size)}

    def piece(self, k):
        d, device = self.target(k)
        return pltpu.make_async_remote_copy(
            src_ref=self.columns(d),
            dst_ref=self.got.at[self.me],
            send_sem=self.send_sem.at[k],
            recv_sem=self.recv_sem.at[k],
            device_id=device,
            device_id_type=MESH,
        )

    def own(self):
        return pltpu.make_async_copy(self.columns(self.me), self.got.at[self.me], self.local_sem.at[0])

    def start(self):
        self.own().start()

        @pl.loop(1, self.devices)
        def _(k):
            self.piece(k).start()

    def add(self, chosen):
        self.own().wait()

        @pl.loop(1, self.devices)
        def _(k):
            self.piece(k).wait_recv()

        everything = self.got[...].reshape(self.devices * self.got.shape[1], self.tiles * LANES)
        summed = dot_tn(chosen, everything)
        for t in range(self.tiles):
            tile = summed[:, t * LANES : (t + 1) * LANES]
            self.result[t] = jnp.where(self.is_first(self.me * self.tiles + t), tile.T, tile).astype(BF16)
        store = pltpu.make_async_copy(self.result, self.place, self.local_sem.at[1])
        store.start()
        store.wait()
        for k in range(1, self.seq_size):
            self.across(k).start()

    def across(self, k):
        return pltpu.make_async_remote_copy(
            src_ref=self.place,
            dst_ref=self.place,
            send_sem=self.seq_sem.at[0, k],
            recv_sem=self.seq_sem.at[1, k],
            device_id={"seq": lax.rem(self.ring.x + k, self.seq_size)},
            device_id_type=MESH,
        )

    def crossed(self):
        for k in range(1, self.seq_size):
            self.across(k).wait_recv()

    def drain(self):
        self.unit.drain()
        for k in range(1, self.seq_size):
            self.across(k).wait_send()

        @pl.loop(1, self.devices)
        def _(k):
            self.piece(k).wait_send()


def mixer_back_kernel(sizes, per_sequence, shares, *refs):
    (
        grad_second, after, cotangent, block_in, mixed, conv, mixer_out, normed, low_in, low_out,
        in_first, in_second, out_first, out_second, pick_t, taps, gain_first, gain_second, weight_in, weight_out,
        grads_early,
    ) = refs[:21]
    grad_input, landing_early, landing_late = refs[21:24]
    units_refs = refs[24:28]
    early_refs, late_refs = refs[28:34], refs[34:40]
    pick_send, pick_recv, rim_sem, load_sem = refs[40:44]
    (
        picks, rim_out, rim_in, grad_after, after_s, mixed_s, conv_s, in_w, out_w, branch,
        grad_mixer, grad_mixed, low_out_back, low_in_back, late,
    ) = refs[44:]
    fsdp_size, seq_size = sizes
    devices = fsdp_size * seq_size
    ring = Ring(fsdp_size)
    tokens, features = after_s.shape
    slots = low_in.shape[1]
    sequences = tokens // per_sequence
    block = min(ROW_BLOCK, per_sequence)
    early = Sum(
        ring, seq_size, 0, grads_early, landing_early, shares.early, shares.early_is_first, early_refs, units_refs
    )
    later = Sum(ring, seq_size, 1, late, landing_late, shares.late, shares.late_is_first, late_refs, units_refs)
    loads = [
        pltpu.make_async_copy(a, b, load_sem.at[k])
        for k, (a, b) in enumerate(
            (
                (after, after_s),
                (grad_second, grad_after),
                (weight_out, out_w),
                (mixed, mixed_s),
                (conv, conv_s),
                (weight_in, in_w),
                (
                    grads_early.at[:, pl.ds(shares.early_used * LANES, max(shares.rest, 1) * LANES)],
                    late.at[:, pl.ds(0, max(shares.rest, 1) * LANES)],
                ),
            )
        )
    ]
    for copy in loads[:6]:
        copy.start()

    barrier = pltpu.get_barrier_semaphore()

    @pl.loop(1, devices)
    def _(k):
        pl.semaphore_signal(barrier, inc=1, device_id=early.target(k)[1], device_id_type=MESH)

    late[:, shares.late_used * LANES :] = jnp.zeros((slots, shares.late_width - shares.late_used * LANES), BF16)
    if shares.rest:
        loads[6].start()
    pl.semaphore_wait(barrier, devices - 1)

    def pick_piece(k):
        return pltpu.make_async_remote_copy(
            src_ref=pick_t,
            dst_ref=picks.at[early.me],
            send_sem=pick_send.at[k],
            recv_sem=pick_recv.at[k],
            device_id=early.target(k)[1],
            device_id_type=MESH,
        )

    picks[early.me] = pick_t[...]

    @pl.loop(1, devices)
    def _(k):
        pick_piece(k).start()

    early.start()
    for copy in loads[:3]:
        copy.wait()

    def rows_of(r):
        return pl.ds(pl.multiple_of(r * block, block), block)

    def masked(r, values):
        row = r * block + lax.broadcasted_iota(jnp.int32, (block, slots), 0)
        column = lax.broadcasted_iota(jnp.int32, (block, slots), 1)
        return jnp.where(row // per_sequence == column // R, ADAPTER_SCALE * values, 0.0).astype(BF16)

    @pl.loop(0, tokens // block)
    def _(r):
        at = rows_of(r)
        rows = after_s[at, :]
        inverse = lax.rsqrt(jnp.mean(rows * rows, axis=-1, keepdims=True) + EPSILON)
        unit_rows = rows * inverse
        scaled = grad_after[at, :] * gain_second[...]
        gradient = cotangent[at, :].astype(F32) + inverse * (
            scaled - unit_rows * jnp.mean(scaled * unit_rows, axis=-1, keepdims=True)
        )
        grad_after[at, :] = gradient
        rounded = gradient.astype(BF16)
        branch[at, :] = rounded
        back_low = masked(r, dot_nt(rounded, out_second[...]))
        low_out_back[at, :] = back_low
        grad_mixer[at, :] = dot_nt(rounded, out_w[...]) + dot_nt(back_low, out_first[...])

    for copy in loads[3:5]:
        copy.wait()
    middle = slice(features, 2 * features)
    for k in range(sequences):
        at = slice(k * per_sequence, k * per_sequence + 8)
        rim_out[k] = grad_mixer[at, :] * mixed_s[at, middle]
    rim = pltpu.make_async_remote_copy(
        src_ref=rim_out,
        dst_ref=rim_in,
        send_sem=rim_sem.at[0],
        recv_sem=rim_sem.at[1],
        device_id={"seq": lax.rem(ring.x + seq_size - 1, seq_size)},
        device_id_type=MESH,
    )
    rim.start()
    base = shares.rest * LANES
    late[:, base + features : base + 2 * features] = dot_tn(low_out_back[...], mixer_out[...]).astype(BF16)
    base += 2 * features
    late[:, base + 3 * features : base + 4 * features] = dot_tn(low_out[...], branch[...]).astype(BF16)
    rim.wait_recv()
    inner = (ring.x < seq_size - 1).astype(F32)

    @pl.loop(0, tokens // block)
    def _(r):
        at = rows_of(r)
        back = grad_mixer[at, :]
        through = back * mixed_s[at, middle]
        after_at = pl.ds(pl.multiple_of(jnp.minimum((r + 1) * block, tokens - 8), 8), 8)
        beyond = grad_mixer[after_at, :] * mixed_s[after_at, middle]
        last = lax.rem((r + 1) * block, per_sequence) == 0
        beyond = jnp.where(last, rim_in[(r * block) // per_sequence] * inner, beyond)
        extended = jnp.concatenate([through, beyond], axis=0)
        gated = (
            taps[2:3, :] * through + taps[1:2, :] * extended[1 : block + 1] + taps[0:1, :] * extended[2 : block + 2]
        )
        grad_mixed[at, :features] = (gated * mixed_s[at, 2 * features :]).astype(BF16)
        grad_mixed[at, middle] = (back * conv_s[at, :]).astype(BF16)
        grad_mixed[at, 2 * features :] = (gated * mixed_s[at, :features]).astype(BF16)
        low_in_back[at, :] = masked(r, dot_nt(grad_mixed[at, :], in_second[...]))

    late[:, base : base + 3 * features] = dot_tn(low_in[...], grad_mixed[...]).astype(BF16)
    base -= 2 * features
    late[:, base : base + features] = dot_tn(low_in_back[...], normed[...]).astype(BF16)
    if shares.rest:
        loads[6].wait()
    later.start()
    loads[5].wait()

    @pl.loop(1, devices)
    def _(k):
        pick_piece(k).wait_recv()

    def finish(r):
        at = rows_of(r)
        rows = block_in[at, :].astype(F32)
        inverse = lax.rsqrt(jnp.mean(rows * rows, axis=-1, keepdims=True) + EPSILON)
        unit_rows = rows * inverse
        gradient = dot_nt(grad_mixed[at, :], in_w[...]) + dot_nt(low_in_back[at, :], in_first[...])
        scaled = gradient * gain_first[...]
        grad_input[at, :] = (
            grad_after[at, :]
            + inverse * (scaled - unit_rows * jnp.mean(scaled * unit_rows, axis=-1, keepdims=True))
        ).astype(BF16)

    chosen = picks[...].reshape(devices * slots, LANES)
    early.add(chosen)
    parts = tokens // block
    half = parts // 2

    @pl.loop(0, half)
    def _(r):
        finish(r)

    early.crossed()
    early.unit.own()
    later.add(chosen)

    @pl.loop(half, parts)
    def _(r):
        finish(r)

    steps = early.unit.steps
    early.unit.relay(1)
    later.crossed()
    later.unit.own()
    for step in range(2, steps + 3):
        if step <= steps:
            early.unit.relay(step)
        if step >= 3:
            early.unit.relay_seq(step - 2)
        if step <= steps + 1:
            later.unit.relay(step - 1)
    for step in range(1, steps + 1):
        later.unit.relay_seq(step)
    early.unit.collect()
    later.unit.collect()
    early.drain()
    later.drain()
    rim.wait_send()

    @pl.loop(1, devices)
    def _(k):
        pick_piece(k).wait_send()


def mixer_back(sizes, per_sequence, shares, operands):
    fsdp_size, seq_size = sizes
    devices = fsdp_size * seq_size
    tokens, features = operands[0].shape
    slots = operands[8].shape[1]
    sequences = tokens // per_sequence

    def sum_refs(tiles):
        return [
            pltpu.SemaphoreType.DMA((devices,)),
            pltpu.SemaphoreType.DMA((devices,)),
            pltpu.SemaphoreType.DMA((2, seq_size)),
            pltpu.SemaphoreType.DMA((2,)),
            pltpu.VMEM((devices, slots, tiles * LANES), BF16),
            pltpu.VMEM((tiles, LANES, LANES), BF16),
        ]

    in_specs = [IN_VMEM] * len(operands)
    for k in (0, 1, 4, 5, 18, 19, 20):
        in_specs[k] = ANYWHERE
    return pl.pallas_call(
        functools.partial(mixer_back_kernel, sizes, per_sequence, shares),
        out_shape=(
            jax.ShapeDtypeStruct((tokens, features), BF16),
            jax.ShapeDtypeStruct((fsdp_size, seq_size, shares.early, LANES, LANES), BF16),
            jax.ShapeDtypeStruct((fsdp_size, seq_size, shares.late, LANES, LANES), BF16),
        ),
        in_specs=in_specs,
        out_specs=(IN_VMEM, ANYWHERE, ANYWHERE),
        scratch_shapes=unit_sems(2, fsdp_size // 2)
        + sum_refs(shares.early)
        + sum_refs(shares.late)
        + [
            pltpu.SemaphoreType.DMA((devices,)),
            pltpu.SemaphoreType.DMA((devices,)),
            pltpu.SemaphoreType.DMA((2,)),
            pltpu.SemaphoreType.DMA((7,)),
            pltpu.VMEM((devices, slots, LANES), BF16),
            pltpu.VMEM((sequences, 8, features), F32),
            pltpu.VMEM((sequences, 8, features), F32),
            pltpu.VMEM((tokens, features), F32),
            pltpu.VMEM((tokens, features), F32),
            pltpu.VMEM((tokens, 3 * features), F32),
            pltpu.VMEM((tokens, features), F32),
            pltpu.VMEM((features, 3 * features), BF16),
            pltpu.VMEM((features, features), BF16),
            pltpu.VMEM((tokens, features), BF16),
            pltpu.VMEM((tokens, features), F32),
            pltpu.VMEM((tokens, 3 * features), BF16),
            pltpu.VMEM((tokens, slots), BF16),
            pltpu.VMEM((tokens, slots), BF16),
            pltpu.VMEM((slots, shares.late_width), BF16),
        ],
        compiler_params=pltpu.CompilerParams(
            collective_id=2, has_side_effects=True, vmem_limit_bytes=VMEM_LIMIT
        ),
    )(*operands)


def spread_kernel(layout, early, late, *outs):
    for out, pieces in zip(outs, layout):
        for is_late, start, count, first in pieces:
            source = late if is_late else early
            offset = pieces[0][2] if len(pieces) > 1 and (is_late, start) == pieces[1][:2] else 0

            @pl.loop(0, count)
            def _(k, source=source, start=start, offset=offset, out=out, first=first):
                at = pl.ds(pl.multiple_of((offset + k) * LANES, LANES), LANES)
                tile = source[start + k].astype(F32)
                if first:
                    out[at, :] = tile
                else:
                    out[:, at] = tile


def spread(shares, early, late):
    wide, narrow, rest = shares.wide, shares.narrow, shares.rest
    low = 3 * wide
    layout = (
        ((True, rest, narrow, True),),
        ((True, rest + 2 * narrow, 3 * narrow, False),),
        ((True, rest + narrow, narrow, True),),
        ((True, rest + 5 * narrow, narrow, False),),
        ((False, low, narrow, True),),
        ((False, wide, wide, False),),
        ((False, low + narrow, narrow, True),),
        ((False, 2 * wide, wide, False),),
        ((False, 0, wide, True),),
        ((False, low + 2 * narrow, narrow - rest, False), (True, 0, rest, False)),
    )
    shapes = []
    for pieces in layout:
        length = sum(piece[2] for piece in pieces) * LANES
        shapes.append(jax.ShapeDtypeStruct((length, LANES) if pieces[0][3] else (LANES, length), F32))
    return pl.pallas_call(
        functools.partial(spread_kernel, layout),
        out_shape=tuple(shapes),
        in_specs=[IN_VMEM] * 2,
        out_specs=(IN_VMEM,) * len(shapes),
        compiler_params=pltpu.CompilerParams(vmem_limit_bytes=VMEM_LIMIT),
    )(early.reshape(-1, LANES, LANES), late.reshape(-1, LANES, LANES))


def per_device(
    block_input,
    output_grad,
    adapter_ids,
    in_weight,
    out_weight,
    gate_weight,
    up_weight,
    down_weight,
    conv_weight,
    first_gain,
    second_gain,
    infirst_adapter,
    insecond_adapter,
    outfirst_adapter,
    outsecond_adapter,
    gatefirst_adapter,
    gatesecond_adapter,
    upfirst_adapter,
    upsecond_adapter,
    downfirst_adapter,
    downsecond_adapter,
):
    batches, seq_count, local_len, features = block_input.shape
    sequences = batches * seq_count
    tokens = sequences * local_len
    fsdp_size, seq_size = lax.axis_size("fsdp"), lax.axis_size("seq")
    slots = sequences * R
    hidden_size = gate_weight.shape[1]
    shares = Shares(fsdp_size * seq_size, features, hidden_size)
    kernel = conv_weight.astype(F32)
    gain_first = first_gain.astype(F32)[None, :]
    gain_second = second_gain.astype(F32)[None, :]
    wanted = jnp.repeat(adapter_ids.reshape(sequences) * R, R) + jnp.tile(jnp.arange(R), sequences)
    pick = (lax.broadcasted_iota(jnp.int32, (LANES, slots), 0) == wanted[None, :]).astype(BF16)
    pick_t = (lax.broadcasted_iota(jnp.int32, (slots, LANES), 1) == wanted[:, None]).astype(BF16)
    cotangent = output_grad.reshape(tokens, features)
    block_in = block_input.reshape(tokens, features)
    (
        grad_second, grads_early, low_in, low_out, in_first, in_second, out_first, out_second,
        block_output, after_mixer, mixed_in, conv_out, mixer_out, normed, weight_in, weight_out, _, _,
    ) = front(
        (fsdp_size, seq_size),
        local_len,
        shares.early_width,
        (
            block_in,
            cotangent,
            pick,
            pick_t,
            kernel,
            gain_first,
            gain_second,
            infirst_adapter,
            insecond_adapter,
            outfirst_adapter,
            outsecond_adapter,
            gatefirst_adapter,
            upfirst_adapter,
            downsecond_adapter,
            gatesecond_adapter,
            upsecond_adapter,
            downfirst_adapter,
            in_weight,
            out_weight,
            gate_weight,
            up_weight,
            down_weight,
        ),
    )
    grad_input, early, late = mixer_back(
        (fsdp_size, seq_size),
        local_len,
        shares,
        (
            grad_second,
            after_mixer,
            cotangent,
            block_in,
            mixed_in,
            conv_out,
            mixer_out,
            normed,
            low_in,
            low_out,
            in_first,
            in_second,
            out_first,
            out_second,
            pick_t,
            kernel,
            gain_first,
            gain_second,
            weight_in,
            weight_out,
            grads_early,
        ),
    )
    shape = block_input.shape
    return (block_output.reshape(shape), grad_input.reshape(shape)) + tuple(spread(shares, early, late))


def solution(mesh):
    return jax.shard_map(
        per_device,
        mesh=mesh,
        in_specs=(
            P(None, "fsdp", "seq", None),
            P(None, "fsdp", "seq", None),
            P(None, "fsdp"),
            P("fsdp", None),
            P("fsdp", None),
            P("fsdp", None),
            P("fsdp", None),
            P("fsdp", None),
            P(),
            P(),
            P(),
            P(),
            P(),
            P(),
            P(),
            P(),
            P(),
            P(),
            P(),
            P(),
            P(),
        ),
        out_specs=(
            P(None, "fsdp", "seq", None),
            P(None, "fsdp", "seq", None),
            P(),
            P(),
            P(),
            P(),
            P(),
            P(),
            P(),
            P(),
            P(),
            P(),
        ),
        check_vma=False,
    )
```

```python
import functools

import jax
import jax.numpy as jnp
from jax import lax
from jax.experimental import pallas as pl
from jax.experimental.pallas import tpu as pltpu
from jax.sharding import PartitionSpec as P

R = 16
LANES = 128
EPSILON = 1e-05
ADAPTER_SCALE = 0.5
MESH = pl.DeviceIdType.MESH
BF16 = jnp.bfloat16
F32 = jnp.float32
VMEM_LIMIT = 62 * 1024 * 1024
FF_CHUNK = 512
ROW_BLOCK = 256
WIDE_BLOCK = 512
VMEM_LIMIT_FRONT = 63 * 1024 * 1024


def dot_nn(left, right):
    return jnp.dot(left, right, preferred_element_type=F32)


def dot_nt(left, right):
    return lax.dot_general(left, right, (((1,), (1,)), ((), ())), preferred_element_type=F32)


def dot_tn(left, right):
    return lax.dot_general(left, right, (((0,), (0,)), ((), ())), preferred_element_type=F32)


def when(condition, action):
    if isinstance(condition, bool):
        if condition:
            action()
    else:
        pl.when(condition)(action)


class Ring:
    def __init__(self, fsdp_size):
        self.count = fsdp_size // 2
        self.me = lax.axis_index("fsdp")
        self.core = lax.rem(self.me, 2)
        chip = self.me // 2
        self.grid = fsdp_size == 16
        if self.grid:
            z, y = chip // 2, lax.rem(chip, 2)
            self.place = y * z + (1 - y) * (7 - z)
        else:
            self.place = chip
        x = lax.axis_index("seq")
        self.x = x
        self.role = lax.rem(x, 2)
        self.to_next = {"fsdp": self.device(lax.rem(self.place + 1, self.count))}
        self.to_prev = {"fsdp": self.device(lax.rem(self.place + self.count - 1, self.count))}
        self.to_core = {"fsdp": self.me + 1 - 2 * self.core}
        self.to_seq = {"seq": x + 1 - 2 * self.role}

    def device(self, place):
        if self.grid:
            y = 1 - place // 4
            z = y * place + (1 - y) * (7 - place)
            return (z * 2 + y) * 2 + self.core
        return place * 2 + self.core

    def at_step(self, direction, step):
        if direction == 0:
            return self.device(lax.rem(self.place + self.count - step, self.count))
        return self.device(lax.rem(self.place + step, self.count))

    def target(self, k, seq_size, devices):
        d = lax.rem(self.me * seq_size + self.x + k, devices)
        return d, {"fsdp": d // seq_size, "seq": lax.rem(d, seq_size)}

    def greet(self, seq_size, devices):
        barrier = pltpu.get_barrier_semaphore()

        @pl.loop(1, devices)
        def _(k):
            device = self.target(k, seq_size, devices)[1]
            pl.semaphore_signal(barrier, inc=1, device_id=device, device_id_type=MESH)

        pl.semaphore_wait(barrier, devices - 1)


class Exchange:
    def __init__(self, ring, seq_size, devices, source, got, sems):
        self.ring, self.seq_size, self.devices = ring, seq_size, devices
        self.source, self.got, self.sems = source, got, sems
        self.me = ring.me * seq_size + ring.x

    def own(self):
        return pltpu.make_async_copy(self.source(self.me), self.got.at[self.me], self.sems.at[2])

    def start(self):
        self.own().start()

        @pl.loop(1, self.devices)
        def _(k):
            d, device = self.ring.target(k, self.seq_size, self.devices)
            pltpu.make_async_remote_copy(
                src_ref=self.source(d),
                dst_ref=self.got.at[self.me],
                send_sem=self.sems.at[0],
                recv_sem=self.sems.at[1],
                device_id=device,
                device_id_type=MESH,
            ).start()

    def all_pieces(self):
        others = self.got.at[pl.ds(0, self.devices - 1)]
        return pltpu.make_async_remote_copy(
            src_ref=others,
            dst_ref=others,
            send_sem=self.sems.at[0],
            recv_sem=self.sems.at[1],
            device_id=self.ring.to_next,
            device_id_type=MESH,
        )

    def arrived(self):
        self.own().wait()
        self.all_pieces().wait_recv()

    def drain(self):
        self.all_pieces().wait_send()


class Unit:
    def __init__(self, ring, number, spot, sems):
        self.ring, self.number, self.spot = ring, number, spot
        self.send, self.ring_sem, self.seq_sem, self.core_sem = sems
        half = ring.count // 2
        self.reaches = ((half, ring.count - 1 - half), (ring.count - 1 - half, half))
        self.steps = half
        self.others = ring.count - 1

    def copy(self, spot, slot, sem, device):
        return pltpu.make_async_remote_copy(
            src_ref=spot,
            dst_ref=spot,
            send_sem=self.send.at[self.number, slot],
            recv_sem=sem,
            device_id=device,
            device_id_type=MESH,
        )

    def arrived(self, spot, sem):
        self.copy(spot, 0, sem, self.ring.to_next).wait_recv()

    def own(self):
        ring, n = self.ring, self.number
        for slot, third in ((0, ring.role), (1, 2)):
            spot = self.spot(third, ring.me)
            self.copy(spot, 2 * slot, self.ring_sem.at[n, slot, 0], ring.to_next).start()
            self.copy(spot, 2 * slot + 1, self.ring_sem.at[n, slot, self.others - 1], ring.to_prev).start()
        for k, third in enumerate((ring.role, 1 - ring.role, 2)):
            self.copy(self.spot(third, ring.me), 4 + k, self.core_sem.at[n, third, 0], ring.to_core).start()

    def relay(self, step):
        ring, n, others = self.ring, self.number, self.others
        for slot, third in ((0, ring.role), (1, 2)):
            for direction in (0, 1):
                reach = self.reaches[slot][direction]
                lane = step - 1 if direction == 0 else others - step
                spot = self.spot(third, ring.at_step(direction, step))

                def forward(slot=slot, direction=direction, lane=lane, spot=spot):
                    onward = self.ring_sem.at[n, slot, lane + 1 - 2 * direction]
                    target = (ring.to_next, ring.to_prev)[direction]
                    self.copy(spot, 7 + slot * others + lane, onward, target).start()

                def take(slot=slot, third=third, reach=reach, lane=lane, spot=spot, forward=forward):
                    self.arrived(spot, self.ring_sem.at[n, slot, lane])
                    when(step < reach, forward)
                    if slot == 0:
                        self.copy(spot, 7 + 2 * others + lane, self.seq_sem.at[n, lane], ring.to_seq).start()
                    core = self.core_sem.at[n, third, 1 + lane]
                    self.copy(spot, 7 + (3 + slot) * others + lane, core, ring.to_core).start()

                when(step <= reach, take)

    def relay_seq(self, step):
        ring, n, others = self.ring, self.number, self.others
        third = 1 - ring.role
        for direction in (0, 1):
            reach = self.reaches[0][direction]
            lane = step - 1 if direction == 0 else others - step
            spot = self.spot(third, ring.at_step(direction, step))

            def take(lane=lane, spot=spot):
                self.arrived(spot, self.seq_sem.at[n, lane])
                core = self.core_sem.at[n, third, 1 + lane]
                self.copy(spot, 7 + 5 * others + lane, core, ring.to_core).start()

            when(step <= reach, take)

    def collect(self):
        for third in range(3):
            for lane in range(self.others + 1):
                self.arrived(self.spot(third, self.ring.me), self.core_sem.at[self.number, third, lane])

    def drain(self):
        ring, others = self.ring, self.others

        def done(third, slot):
            self.copy(self.spot(third, ring.me), slot, self.seq_sem.at[self.number, 0], ring.to_next).wait_send()

        for slot, third in ((0, 0), (1, 2)):
            done(third, 2 * slot)
            done(third, 2 * slot + 1)
            for direction in (0, 1):
                reach = self.reaches[slot][direction]
                for step in range(1, reach + 1):
                    lane = step - 1 if direction == 0 else others - step
                    if step < reach:
                        done(third, 7 + slot * others + lane)
                    done(third, 7 + (3 + slot) * others + lane)
        for lane in range(others):
            done(0, 7 + 2 * others + lane)
            done(0, 7 + 5 * others + lane)
        for k, third in enumerate((0, 0, 2)):
            done(third, 4 + k)


def unit_sems(units, count):
    return [
        pltpu.SemaphoreType.DMA((units, 7 + 6 * (count - 1))),
        pltpu.SemaphoreType.DMA((units, 2, count - 1)),
        pltpu.SemaphoreType.DMA((units, count - 1)),
        pltpu.SemaphoreType.DMA((units, 3, count)),
    ]


def move_in(moves, sems):
    inward = [pltpu.make_async_copy(a, b, sems.at[0, k]) for k, (a, b, _) in enumerate(moves)]
    outward = [pltpu.make_async_copy(b, c, sems.at[1, k]) for k, (_, b, c) in enumerate(moves)]
    for copy in inward:
        copy.start()
    for first, second in zip(inward, outward):
        first.wait()
        second.start()
    return outward


def row_spot(landing, rows, start, size, third, owner):
    return landing.at[pl.ds(owner * rows + start + third * size, size), :]


def column_spot(landing, rows, width, last, third, owner):
    size = last if isinstance(third, int) and third == 2 else width
    start = third * width if isinstance(third, int) else pl.multiple_of(third * width, LANES)
    return landing.at[pl.ds(owner * rows, rows), pl.ds(start, size)]


def down_pieces(down_rows):
    return 3 if down_rows % 288 == 0 else 1


def in_spot(landing, rows, part, half, third, owner):
    start = pl.multiple_of(third * part + half * (part // 2), LANES)
    return landing.at[pl.ds(owner * rows, rows), pl.ds(start, part // 2)]


def chunk_spot(landing, rows, size, chunk, third, owner):
    start = pl.multiple_of((chunk * 3 + third) * size, LANES)
    return landing.at[:, pl.ds(owner * rows, rows), pl.ds(start, size)]


class Plan:
    LINK, CORE, DELAY, COST = 37e3, 200e3, 1.7, 0.25
    WINDOWS = (4, 8, 1.5, 6, 1.5, 4, 1, 8, 1, 3, 2, 2)

    def __init__(self, units, sizes):
        self.units, self.sizes = units, sizes
        self.now = 0.0
        self.free = {"next": 0.0, "prev": 0.0, "seq": 0.0, "core": 0.0}
        self.steps = units[0].steps
        self.owned = 0
        self.arrival, self.core, self.left, self.collected = {}, {}, {}, set()
        self.list = []

    def send(self, link, size):
        if size:
            rate = self.CORE if link == "core" else self.LINK
            self.free[link] = max(self.free[link], self.now) + size / rate
        return self.free[link] + self.DELAY

    def run_own(self):
        u = self.owned
        self.owned += 1
        shared, common = self.sizes[u]
        self.list.append(self.units[u].own)
        self.now += self.COST
        size = shared + common
        self.arrival[(u, "ring", 1)] = max(self.send("next", size), self.send("prev", size))
        self.core[u] = self.send("core", 2 * shared + common)
        self.left[u] = 2 * self.steps

    def run(self, key):
        u, kind, step = key
        del self.arrival[key]
        shared, common = self.sizes[u]
        unit = self.units[u]
        self.left[u] -= 1
        self.now += self.COST
        if kind == "seq":
            self.list.append(functools.partial(unit.relay_seq, step))
            lanes = sum(step <= reach for reach in unit.reaches[0])
            self.core[u] = max(self.core[u], self.send("core", lanes * shared))
            return
        self.list.append(functools.partial(unit.relay, step))
        across = inward = 0
        onward = []
        for size, reaches, is_shared in ((shared, unit.reaches[0], True), (common, unit.reaches[1], False)):
            for link, reach in zip(("next", "prev"), reaches):
                if step <= reach:
                    inward += size
                    across += size if is_shared else 0
                if step < reach:
                    onward.append(self.send(link, size))
        if onward:
            self.arrival[(u, "ring", step + 1)] = max(onward)
        self.arrival[(u, "seq", step)] = self.send("seq", across)
        self.core[u] = max(self.core[u], self.send("core", inward))

    def ready(self):
        return [key for key, at in sorted(self.arrival.items()) if at <= self.now]

    def pump(self):
        while True:
            keys = self.ready()
            if keys:
                self.run(keys[0])
            elif (
                self.owned < len(self.units)
                and max(self.free["next"], self.free["prev"]) - self.now < self.WINDOWS[self.owned % 12]
            ):
                self.run_own()
            else:
                return

    def can_collect(self, u):
        return u < self.owned and self.left[u] == 0 and self.core[u] <= self.now

    def collect(self, u):
        if u not in self.collected:
            self.collected.add(u)
            self.list.append(self.units[u].collect)
            self.now += self.COST

    def need(self, numbers):
        for u in numbers:
            if u in self.collected:
                continue
            while not self.can_collect(u):
                self.pump()
                if self.can_collect(u):
                    break
                if u < self.owned and self.left[u] == 0:
                    self.now = max(self.now, self.core[u])
                elif self.arrival:
                    self.now = max(self.now, min(self.arrival.values()))
                else:
                    self.run_own()
            self.collect(u)

    def take(self):
        taken, self.list = self.list, []
        return taken

    def tick(self, duration):
        self.pump()
        taken = self.take()
        self.now += duration
        return taken


def run_tick(lists, tick):
    for k, actions in enumerate(lists):
        if not actions:
            continue

        @pl.when(tick == k)
        def _(actions=actions):
            for action in actions:
                action()


def rms_unit(rows):
    inverse = lax.rsqrt(jnp.mean(rows * rows, axis=-1, keepdims=True) + EPSILON)
    return inverse, rows * inverse


def rms_back(scaled, inverse, unit_rows):
    return inverse * (scaled - unit_rows * jnp.mean(scaled * unit_rows, axis=-1, keepdims=True))


ANYWHERE = pl.BlockSpec(memory_space=pl.ANY)
IN_VMEM = pl.BlockSpec(memory_space=pltpu.VMEM)


class Shares:
    def __init__(self, devices, features, hidden_size):
        self.devices = devices
        self.wide, self.narrow = hidden_size // LANES, features // LANES
        self.chunk = FF_CHUNK // LANES
        self.per_chunk = 3 * self.chunk
        third = 3 * self.per_chunk
        names = ("down_first", "gate_second", "up_second")

        def of_third(k):
            return [
                (name, (3 * k + c) * self.chunk + i) for c in range(3) for name in names for i in range(self.chunk)
            ]

        def all_of(name, count):
            return [(name, i) for i in range(count)]

        self.used = min(third, devices)
        self.pitch = third
        sets = [of_third(0), of_third(1)]
        self.spare = [tiles[self.used :] for tiles in sets]
        sets = [tiles[: self.used] for tiles in sets]
        narrow = self.narrow
        rest = of_third(2) + all_of("gate_first", narrow) + all_of("up_first", narrow)
        rest += all_of("down_second", narrow) + self.spare[0] + self.spare[1]
        self.rest_all = len(rest)
        self.per = max(1, len(rest) // devices)
        self.rest_used = min(len(rest), self.per * devices)
        self.left = len(rest) - self.rest_used
        sets.append(rest[: self.rest_used])
        sets.append(rest[self.rest_used :] + all_of("out_first", narrow) + all_of("out_second", narrow))
        sets.append(all_of("in_first", narrow) + all_of("in_second", 3 * narrow))
        self.sets = sets
        self.rest_start = 2 * self.pitch
        self.grads_width = (self.rest_start + self.rest_all) * LANES

    def is_first(self, number, tile):
        flags = [name.endswith("first") for name, _ in self.sets[number]]
        found, start = tile < 0, 0
        for k in range(1, len(flags) + 1):
            if k == len(flags) or flags[k] != flags[start]:
                if flags[start]:
                    found = found | ((tile >= start) & (tile < k))
                start = k
        return found

    def places(self):
        found = {}
        for number, tiles in enumerate(self.sets):
            for k, tile in enumerate(tiles):
                if number == 2:
                    found[tile] = (0, (2 + self.per) * (k // self.per) + 2 + k % self.per)
                else:
                    found[tile] = (0, (2 + self.per) * k + number) if number < 2 else (1, 2 * k + number - 3)
        return found


def column_tiles(source, start, count, used, d, devices):
    if used // count < devices:
        d = lax.rem(d, used // count)
    return source.at[:, pl.ds(pl.multiple_of((start + d * count) * LANES, LANES), count * LANES)]


class Sum:
    def __init__(self, ring, seq_size, number, landing, is_first, got, result, sems, unit_sems_refs):
        self.ring, self.seq_size, self.landing = ring, seq_size, landing
        self.is_first, self.got, self.result = is_first, got, result
        self.seq_sem, self.local_sem = sems
        self.place = landing.at[ring.me, ring.x]
        self.unit = Unit(ring, number, self.spot, unit_sems_refs)

    def spot(self, third, owner):
        size = 32 if isinstance(third, int) and third == 2 else 48
        return self.landing.at[owner, :, :, pl.ds(third * 48, size), :]

    def add(self, chosen):
        tiles = self.result.shape[0]
        for t in range(tiles):
            tile = dot_tn(chosen, self.got(t))
            self.result[t] = jnp.where(self.is_first(t), tile.T, tile).astype(BF16)
        store = pltpu.make_async_copy(self.result, self.place, self.local_sem.at[0])
        store.start()
        store.wait()
        for k in range(1, self.seq_size):
            self.across(k).start()

    def across(self, k):
        return pltpu.make_async_remote_copy(
            src_ref=self.place,
            dst_ref=self.place,
            send_sem=self.seq_sem.at[0, k],
            recv_sem=self.seq_sem.at[1, k],
            device_id={"seq": lax.rem(self.ring.x + k, self.seq_size)},
            device_id_type=MESH,
        )

    def crossed(self):
        for k in range(1, self.seq_size):
            self.across(k).wait_recv()

    def groups(self):
        unit = self.unit
        found = [[self.crossed, unit.own], [functools.partial(unit.relay, 1)]]
        for step in range(2, unit.steps + 1):
            found.append([functools.partial(unit.relay, step), functools.partial(unit.relay_seq, step - 1)])
        return found + [[functools.partial(unit.relay_seq, unit.steps)]]

    def drain(self):
        self.unit.drain()
        for k in range(1, self.seq_size):
            self.across(k).wait_send()


def share_out(groups, ticks):
    cuts = [len(groups) * k // ticks for k in range(ticks + 1)]
    return [sum(groups[cuts[k] : cuts[k + 1]], []) for k in range(ticks)]


def front_kernel(sizes, per_sequence, shares, *refs):
    (
        block_in, cotangent, ids, taps_in, gain_first_in, gain_second_in,
        in_first, in_second, out_first, out_second, gate_first, up_first, down_second,
        gate_second, up_second, down_first, in_own, out_own, gate_own, up_own, down_own,
    ) = refs[:21]
    (
        grad_second, grads, low_in, low_out, in_first_s, in_second_s, out_first_s, out_second_s, pick_t,
        block_out, after_out, mixed_out, conv_out, mixer_out, normed_out, in_all, out_all, gu_all, down_all,
        grad_mixer_out, got_front, got_rest, got_out, picks,
    ) = refs[21:45]
    sems, local_sem, load_sem, stage_sem, rim_sem, out_sem = refs[45:49], refs[49], refs[50], refs[51], refs[52], refs[53]
    exchange_sems = refs[54:59]
    held = refs[59:64]
    pick, taps, gain_first, gain_second, out_grads, out_tiles = refs[-6:]
    (
        total, wide, gate_w, up_w, down_w, normed, mixer, second, gate_up_first, first_down, second_gu, second_down,
        low_gu, grad_low_down, low_down, grad_low_gu, partial, rim_out, rim_in,
    ) = refs[64:-6]
    fsdp_size, seq_size = sizes
    ring = Ring(fsdp_size)
    rows, down_rows = gate_own.shape[0], down_own.shape[0]
    tokens, features = cotangent.shape
    hidden_size = gate_own.shape[1]
    chunks = hidden_size // FF_CHUNK
    sequences = tokens // per_sequence
    block = min(ROW_BLOCK, per_sequence)
    wide_block = min(WIDE_BLOCK, tokens)
    blocks, wide_blocks = tokens // block, tokens // wide_block
    slots = low_in.shape[1]
    mine = pl.ds(ring.me * rows, rows)
    moved = move_in(
        [
            (in_own, held[0], in_all.at[mine, :]),
            (out_own, held[1], out_all.at[mine, :]),
            (down_own, held[4], down_all.at[pl.ds(ring.me * down_rows, down_rows), :]),
            (gate_own, held[2], gu_all.at[0, mine, :]),
            (up_own, held[3], gu_all.at[1, mine, :]),
        ],
        local_sem,
    )
    stages = []
    for k in range(-(-hidden_size // features)):
        width = min(features, hidden_size - k * features)
        part, lanes = pl.ds(k * features, width), pl.ds(k * LANES, LANES)
        stages += [
            (gate_second.at[:, part], second.at[lanes, pl.ds(0, width)]),
            (up_second.at[:, part], normed.at[lanes, pl.ds(0, width)]),
            (down_first.at[part, :], mixer.at[pl.ds(0, width), lanes]),
        ]
    stages = [pltpu.make_async_copy(a, b, stage_sem.at[k]) for k, (a, b) in enumerate(stages)]
    for copy in stages:
        copy.start()
    devices = fsdp_size * seq_size
    ring.greet(seq_size, devices)

    part = in_all.shape[1] // 3
    out_x = 3 * features // 8
    unit_list, sizes_of = [], []

    def add_unit(spot, shared, common):
        unit_list.append(Unit(ring, len(unit_list), spot, sems))
        sizes_of.append((2 * shared, 2 * common))

    for k in range(2):
        add_unit(functools.partial(in_spot, in_all, rows, part, k), rows * part // 2, rows * part // 2)
    last_out = features - 2 * out_x
    add_unit(functools.partial(column_spot, out_all, rows, out_x, last_out), rows * out_x, rows * last_out)
    pieces = down_pieces(down_rows)
    for k in range(pieces):
        size = down_rows // pieces // 3
        add_unit(functools.partial(row_spot, down_all, down_rows, 3 * size * k, size), size * features, size * features)
    fixed = len(unit_list)
    comm_chunks = 2 * chunks // 3
    comm_size = hidden_size // comm_chunks // 3
    for k in range(comm_chunks):
        add_unit(functools.partial(chunk_spot, gu_all, rows, comm_size, k), 2 * rows * comm_size, 2 * rows * comm_size)
    plan = Plan(unit_list, sizes_of)

    def run_all(actions):
        for action in actions:
            action()

    for copy in moved:
        copy.wait()
    run_all(plan.tick(5.0))
    sequence_row = lax.broadcasted_iota(jnp.int32, (slots, LANES), 0)
    sequence_column = lax.broadcasted_iota(jnp.int32, (LANES, slots), 1)
    wanted_row, wanted_column = lax.rem(sequence_row, R), lax.rem(sequence_column, R)
    for k in range(sequences):
        base = ids[k] * R
        wanted_row += jnp.where(sequence_row // R == k, base, 0)
        wanted_column += jnp.where(sequence_column // R == k, base, 0)
    pick_t[...] = (wanted_row == lax.broadcasted_iota(jnp.int32, (slots, LANES), 1)).astype(F32).astype(BF16)
    pick[...] = (wanted_column == lax.broadcasted_iota(jnp.int32, (LANES, slots), 0)).astype(F32).astype(BF16)
    taps[...] = taps_in[...].astype(F32)
    gain_first[...] = gain_first_in[...].astype(F32)
    gain_second[...] = gain_second_in[...].astype(F32)

    def rows_of(r, size=block):
        return pl.ds(pl.multiple_of(r * size, size), size)

    def masked(r, values, size=block):
        row = r * size + lax.broadcasted_iota(jnp.int32, (size, slots), 0)
        column = lax.broadcasted_iota(jnp.int32, (size, slots), 1)
        return jnp.where(row // per_sequence == column // R, ADAPTER_SCALE * values, 0.0).astype(BF16)

    for copy in stages:
        copy.wait()
    for k in range(-(-hidden_size // features)):
        width = min(features, hidden_size - k * features)
        at, lanes = slice(k * features, k * features + width), slice(k * LANES, (k + 1) * LANES)
        second_gu[0, :, at] = dot_nn(pick_t[...], second[lanes, :width]).astype(BF16)
        second_gu[1, :, at] = dot_nn(pick_t[...], normed[lanes, :width]).astype(BF16)
        first_down[at, :] = dot_nn(mixer[:width, lanes], pick[...]).astype(BF16)
    second_down[...] = dot_nn(pick_t[...], down_second[...]).astype(BF16)
    in_second_s[...] = dot_nn(pick_t[...], in_second[...]).astype(BF16)
    out_second_s[...] = dot_nn(pick_t[...], out_second[...]).astype(BF16)
    in_first_s[...] = dot_nn(in_first[...], pick[...]).astype(BF16)
    out_first_s[...] = dot_nn(out_first[...], pick[...]).astype(BF16)
    gate_up_first[0] = dot_nn(gate_first[...], pick[...]).astype(BF16)
    gate_up_first[1] = dot_nn(up_first[...], pick[...]).astype(BF16)
    lists = [plan.tick(0.9) for _ in range(blocks)]

    @pl.loop(0, blocks)
    def _(r):
        run_tick(lists, r)
        at = rows_of(r)
        normed_rows = (rms_unit(block_in[at, :].astype(F32))[1] * gain_first[...]).astype(BF16)
        normed[at, :] = normed_rows
        low_in[at, :] = masked(r, dot_nn(normed_rows, in_first_s[...]))
        grad_low_down[at, :] = masked(r, dot_nt(cotangent[at, :], second_down[...]))
        grad_second[at, :] = jnp.zeros((block, features), F32)

    low_down[...] = jnp.zeros_like(low_down)
    grad_low_gu[...] = jnp.zeros_like(grad_low_gu)
    plan.need((0, 1))
    run_all(plan.take())

    half = FF_CHUNK
    middle, last_part, conv_part = (slice(k * features, (k + 1) * features) for k in (1, 2, 3))
    in_loads = []
    for k in range(2):
        for part_number, buffer in ((0, gate_w), (1, up_w)):
            columns = pl.ds(part_number * features + k * half, half)
            in_loads.append(pltpu.make_async_copy(in_all.at[:, columns], buffer.at[k], load_sem.at[k, part_number]))
        place = in_all.at[pl.ds(k * half, half), pl.ds(2 * features, features)]
        in_loads.append(pltpu.make_async_copy(place, down_w.at[k], load_sem.at[k, 2]))
    for copy in in_loads:
        copy.start()
    run_all(plan.tick(2.0))
    for copy in in_loads:
        copy.wait()
    lists = [plan.tick(1.6) for _ in range(blocks)]

    @pl.loop(0, blocks)
    def _(r):
        run_tick(lists, r)
        at = rows_of(r)
        values, low = normed[at, :], low_in[at, :]
        for part_number, buffer in ((0, gate_w), (1, up_w)):
            for k in range(2):
                start = part_number * features + k * half
                columns = slice(start, start + half)
                wide[at, columns] = dot_nn(values, buffer[k]) + dot_nn(low, in_second_s[:, columns])
        wide[at, last_part] = (
            dot_nn(values[:, :half], down_w[0])
            + dot_nn(values[:, half:], down_w[1])
            + dot_nn(low, in_second_s[:, last_part])
        )

    plan.need((2,))
    run_all(plan.take())
    out_loads = [
        pltpu.make_async_copy(out_all.at[:, pl.ds(k * half, half)], gate_w.at[k], load_sem.at[k, 0]) for k in range(2)
    ]
    for copy in out_loads:
        copy.start()
    for k in range(sequences):
        at = slice((k + 1) * per_sequence - 8, (k + 1) * per_sequence)
        rim_out[k] = wide[at, :features] * wide[at, last_part]
    rim = pltpu.make_async_remote_copy(
        src_ref=rim_out,
        dst_ref=rim_in,
        send_sem=rim_sem.at[0],
        recv_sem=rim_sem.at[1],
        device_id={"seq": lax.rem(ring.x + 1, seq_size)},
        device_id_type=MESH,
    )
    rim.start()
    mixed_store = pltpu.make_async_copy(wide.at[:, pl.ds(0, 3 * features)], mixed_out, out_sem.at[0])
    mixed_store.start()
    normed_store = pltpu.make_async_copy(normed.at[pl.ds(0, tokens), :], normed_out, out_sem.at[1])
    normed_store.start()
    run_all(plan.tick(2.0))
    for copy in out_loads:
        copy.wait()
    rim.wait_recv()
    inner = (ring.x > 0).astype(F32)
    lists = [plan.tick(2.2) for _ in range(blocks)]

    @pl.loop(0, blocks)
    def _(r):
        run_tick(lists, r)
        at = rows_of(r)
        gated = wide[at, :features] * wide[at, last_part]
        before_at = pl.ds(pl.multiple_of(jnp.maximum(r * block - 8, 0), 8), 8)
        before = wide[before_at, :features] * wide[before_at, last_part]
        first = lax.rem(r * block, per_sequence) == 0
        before = jnp.where(first, rim_in[(r * block) // per_sequence] * inner, before)
        extended = jnp.concatenate([before, gated], axis=0)
        convolved = (
            taps[0:1, :] * extended[6 : block + 6] + taps[1:2, :] * extended[7 : block + 7] + taps[2:3, :] * gated
        )
        wide[at, conv_part] = convolved
        mixed = (wide[at, middle] * convolved).astype(BF16)
        mixer[at, :] = mixed
        low = masked(r, dot_nn(mixed, out_first_s[...]))
        low_out[at, :] = low
        branch = jnp.concatenate([dot_nn(mixed, gate_w[0]), dot_nn(mixed, gate_w[1])], axis=1)
        after = block_in[at, :].astype(F32) + (branch + dot_nn(low, out_second_s[...]))
        total[at, :] = after
        second_rows = (rms_unit(after)[1] * gain_second[...]).astype(BF16)
        second[at, :] = second_rows
        for k in range(2):
            low_gu[k, at, :] = masked(r, dot_nn(second_rows, gate_up_first[k]))

    stores = [
        pltpu.make_async_copy(wide.at[:, pl.ds(3 * features, features)], conv_out, out_sem.at[2]),
        pltpu.make_async_copy(mixer.at[pl.ds(0, tokens), :], mixer_out, out_sem.at[3]),
        pltpu.make_async_copy(total, after_out, out_sem.at[4]),
    ]
    for copy in stores:
        copy.start()
    plan.need(range(3, fixed))
    run_all(plan.take())

    def down_load(j, s):
        return pltpu.make_async_copy(down_all.at[rows_of(j, FF_CHUNK), :], down_w.at[s], load_sem.at[s, 2])

    def gu_loads(j, s):
        place = rows_of(j, FF_CHUNK)
        return (
            pltpu.make_async_copy(gu_all.at[0, :, place], gate_w.at[s], load_sem.at[s, 0]),
            pltpu.make_async_copy(gu_all.at[1, :, place], up_w.at[s], load_sem.at[s, 1]),
        )

    down_load(0, 0).start()
    mixed_store.wait()
    for copy in stores:
        copy.wait()
    lists = [plan.tick(1.7) for _ in range(chunks)]

    @pl.loop(0, chunks)
    def _(j):
        s = lax.rem(j, 2)

        @pl.when(j + 1 < chunks)
        def _():
            down_load(j + 1, 1 - s).start()

        down_load(j, s).wait()
        run_tick(lists, j)
        columns = rows_of(j, FF_CHUNK)

        @pl.loop(0, wide_blocks)
        def _(r):
            at = rows_of(r, wide_block)
            wide[at, columns] = dot_nt(cotangent[at, :], down_w[s]) + dot_nt(
                grad_low_down[at, :], first_down[columns, :]
            )

    def begin(j):
        for copy in (down_load(j, j % 2),) + gu_loads(j, j % 2):
            copy.start()

    def units_of(j):
        first, last = j * FF_CHUNK // (3 * comm_size), (j * FF_CHUNK + FF_CHUNK - 1) // (3 * comm_size)
        return range(fixed + first, fixed + last + 1)

    plan.need(units_of(0))
    plan.list.append(functools.partial(begin, 0))
    run_all(plan.tick(1.0))

    def tile_columns(start):
        return lambda d: column_tiles(grads, start, 1, shares.used, d, devices)

    sources = [tile_columns(k * shares.pitch) for k in range(2)]
    sources.append(
        lambda d: column_tiles(grads, shares.rest_start, shares.per, shares.rest_used, d, devices)
    )
    sources.append(lambda d: column_tiles(out_tiles, 0, 1, shares.left + 2 * shares.narrow, d, devices))
    sources.append(lambda d: pick_t)
    places = (got_front.at[0], got_front.at[1], got_rest, got_out, picks)
    exchanges = [
        Exchange(ring, seq_size, devices, source, place, exchange_sems[k])
        for k, (source, place) in enumerate(zip(sources, places))
    ]
    spare_slot = chunks % 2
    back_loads = [
        pltpu.make_async_copy(out_all.at[:, pl.ds(k * half, half)], buffer.at[spare_slot], load_sem.at[2, k])
        for k, buffer in enumerate((gate_w, up_w))
    ]
    back_loads.append(pltpu.make_async_copy(after_out, wide.at[:, pl.ds(0, features)], load_sem.at[2, 2]))

    def load_back():
        for copy in back_loads:
            copy.start()

    lists, begun = [], 0
    for tick in range(chunks * wide_blocks):
        j = tick // wide_blocks
        plan.pump()
        if begun == j and j + 1 < chunks:
            possible = all(u in plan.collected or plan.can_collect(u) for u in units_of(j + 1))
            if possible or (tick + 1) % wide_blocks == 0:
                plan.need(units_of(j + 1))
                plan.list.append(functools.partial(begin, j + 1))
                begun += 1
        if tick == (chunks - 2) * wide_blocks:
            plan.list += [exchanges[0].start, exchanges[4].start]
        if tick == (chunks - 1) * wide_blocks:
            plan.list += [load_back, exchanges[1].start]
        lists.append(plan.tick(3.9))

    @pl.loop(0, chunks * wide_blocks)
    def _(tick):
        j, r = tick // wide_blocks, lax.rem(tick, wide_blocks)
        s = lax.rem(j, 2)
        columns = rows_of(j, FF_CHUNK)

        @pl.when(r == 0)
        def _():
            for copy in (down_load(j, s),) + gu_loads(j, s):
                copy.wait()
            partial[...] = jnp.zeros_like(partial)

        run_tick(lists, tick)
        at = rows_of(r, wide_block)
        values = second[at, :]
        lows = (grad_low_down[at, :], low_gu[0, at, :], low_gu[1, at, :])
        gate = dot_nn(values, gate_w[s]) + dot_nn(lows[1], second_gu[0, :, columns])
        up = dot_nn(values, up_w[s]) + dot_nn(lows[2], second_gu[1, :, columns])
        back = wide[at, columns]
        sigmoid = 1.0 / (1.0 + jnp.exp(-gate))
        active = gate * sigmoid
        hidden = (active * up).astype(BF16)
        grad_gate = (back * up * (sigmoid + active * (1.0 - sigmoid))).astype(BF16)
        grad_up = (back * active).astype(BF16)
        total[at, :] += dot_nn(hidden, down_w[s])
        grad_second[at, :] += dot_nt(grad_gate, gate_w[s]) + dot_nt(grad_up, up_w[s])
        low_down[at, :] += dot_nn(hidden, first_down[columns, :])
        grad_low_gu[0, at, :] += dot_nt(grad_gate, second_gu[0, :, columns])
        grad_low_gu[1, at, :] += dot_nt(grad_up, second_gu[1, :, columns])
        for k, right in enumerate((hidden, grad_gate, grad_up)):
            partial[k] += dot_tn(lows[k], right)

        @pl.when(r == wide_blocks - 1)
        def _():
            for k in range(3):
                start = (j // 3) * shares.pitch + lax.rem(j, 3) * shares.per_chunk + k * shares.chunk
                place = pl.ds(pl.multiple_of(start * LANES, LANES), FF_CHUNK)
                grads[:, place] = partial[k].astype(BF16)

    normed_store.wait()
    rest_tiles = shares.rest_start + 3 * shares.per_chunk
    base = rest_tiles * LANES

    @pl.loop(0, blocks)
    def _(r):
        at = rows_of(r)
        low = masked(r, low_down[at, :])
        grad_low_down[at, :] = low
        normed[at, :] = (total[at, :] + dot_nn(low, second_down[...])).astype(BF16)
        for k in range(2):
            back_low = masked(r, grad_low_gu[k, at, :])
            low_gu[k, at, :] = back_low
            grad_second[at, :] += dot_nt(back_low, gate_up_first[k])

    block_store = pltpu.make_async_copy(normed.at[pl.ds(0, tokens), :], block_out, out_sem.at[1])
    block_store.start()
    grads[:, base + 2 * features : base + 3 * features] = dot_tn(grad_low_down[...], cotangent[...]).astype(BF16)
    for k in range(2):
        columns = slice(base + k * features, base + (k + 1) * features)
        grads[:, columns] = dot_tn(low_gu[k], second[:tokens, :]).astype(BF16)
    start = base + 3 * features
    for k in range(2):
        width = len(shares.spare[k]) * LANES
        if width:
            spare = (k * shares.pitch + shares.used) * LANES
            grads[:, start : start + width] = grads[:, spare : spare + width]
            start += width
    exchanges[2].start()

    for copy in back_loads:
        copy.wait()
    out_grads[...] = jnp.zeros_like(out_grads)

    @pl.loop(0, blocks)
    def _(r):
        at = rows_of(r)
        inverse, unit_rows = rms_unit(wide[at, :features])
        gradient = cotangent[at, :].astype(F32) + rms_back(
            grad_second[at, :] * gain_second[...], inverse, unit_rows
        )
        grad_second[at, :] = gradient
        rounded = gradient.astype(BF16)
        back_low = masked(r, dot_nt(rounded, out_second_s[...]))
        total[at, :] = (
            dot_nt(rounded[:, :half], gate_w[spare_slot])
            + dot_nt(rounded[:, half:], up_w[spare_slot])
            + dot_nt(back_low, out_first_s[...])
        )
        out_grads[0] += dot_tn(back_low, mixer[at, :])
        out_grads[1] += dot_tn(low_out[at, :], rounded)

    mixer_store = pltpu.make_async_copy(total, grad_mixer_out, out_sem.at[0])
    mixer_store.start()
    if shares.left:
        start = (shares.rest_start + shares.rest_used) * LANES
        out_tiles[:, : shares.left * LANES] = grads[:, start : start + shares.left * LANES]
    for k in range(2):
        start = shares.left * LANES + k * features
        out_tiles[:, start : start + features] = out_grads[k].astype(BF16)
    exchanges[3].start()
    for unit in unit_list[:fixed]:
        unit.drain()

    @pl.loop(0, comm_chunks)
    def _(k):
        Unit(ring, fixed + k, functools.partial(chunk_spot, gu_all, rows, comm_size, k), sems).drain()

    rim.wait_send()
    block_store.wait()
    mixer_store.wait()
    for member in exchanges:
        member.arrived()
    for member in exchanges:
        member.drain()


def front(sizes, per_sequence, shares, operands):
    fsdp_size, seq_size = sizes
    cotangent, ids = operands[1:3]
    own = operands[-5:]
    tokens, features = cotangent.shape
    hidden_size = own[2].shape[1]
    sequences = ids.shape[0]
    slots = sequences * R
    units = 3 + down_pieces(own[4].shape[0]) + 2 * (hidden_size // FF_CHUNK) // 3
    tall = max(tokens, features)
    stages = 3 * -(-hidden_size // features)

    def shape(*dims, kind=BF16):
        return jax.ShapeDtypeStruct(dims, kind)

    return pl.pallas_call(
        functools.partial(front_kernel, sizes, per_sequence, shares),
        out_shape=(
            shape(tokens, features, kind=F32),
            shape(slots, shares.grads_width),
            shape(tokens, slots),
            shape(tokens, slots),
            shape(features, slots),
            shape(slots, 3 * features),
            shape(features, slots),
            shape(slots, features),
            shape(slots, LANES),
            shape(tokens, features),
            shape(tokens, features, kind=F32),
            shape(tokens, 3 * features, kind=F32),
            shape(tokens, features, kind=F32),
            shape(tokens, features),
            shape(tokens, features),
            shape(features, 3 * features),
            shape(features, features),
            shape(2, features, hidden_size),
            shape(hidden_size, features),
            shape(tokens, features, kind=F32),
            shape(2, shares.devices, slots, LANES),
            shape(shares.devices, slots, shares.per * LANES),
            shape(shares.devices, slots, LANES),
            shape(shares.devices, slots, LANES),
        ),
        in_specs=[IN_VMEM] * 2 + [pl.BlockSpec(memory_space=pltpu.SMEM)] + [IN_VMEM] * 10 + [ANYWHERE] * 8,
        out_specs=(IN_VMEM,) * 9 + (ANYWHERE,) * 15,
        scratch_shapes=unit_sems(units, fsdp_size // 2)
        + [
            pltpu.SemaphoreType.DMA((2, 5)),
            pltpu.SemaphoreType.DMA((3, 3)),
            pltpu.SemaphoreType.DMA((stages,)),
            pltpu.SemaphoreType.DMA((2,)),
            pltpu.SemaphoreType.DMA((5,)),
        ]
        + [pltpu.SemaphoreType.DMA((3,))] * 5
        + [pltpu.VMEM(member.shape, BF16) for member in own]
        + [
            pltpu.VMEM((tokens, features), F32),
            pltpu.VMEM((tokens, hidden_size), F32),
            pltpu.VMEM((2, features, FF_CHUNK), BF16),
            pltpu.VMEM((2, features, FF_CHUNK), BF16),
            pltpu.VMEM((2, FF_CHUNK, features), BF16),
            pltpu.VMEM((tall, features), BF16),
            pltpu.VMEM((tall, features), BF16),
            pltpu.VMEM((tall, features), BF16),
            pltpu.VMEM((2, features, slots), BF16),
            pltpu.VMEM((hidden_size, slots), BF16),
            pltpu.VMEM((2, slots, hidden_size), BF16),
            pltpu.VMEM((slots, features), BF16),
            pltpu.VMEM((2, tokens, slots), BF16),
            pltpu.VMEM((tokens, slots), BF16),
            pltpu.VMEM((tokens, slots), F32),
            pltpu.VMEM((2, tokens, slots), F32),
            pltpu.VMEM((3, slots, FF_CHUNK), F32),
            pltpu.VMEM((sequences, 8, features), F32),
            pltpu.VMEM((sequences, 8, features), F32),
            pltpu.VMEM((LANES, slots), BF16),
            pltpu.VMEM((3, features), F32),
            pltpu.VMEM((1, features), F32),
            pltpu.VMEM((1, features), F32),
            pltpu.VMEM((2, slots, features), F32),
            pltpu.VMEM((slots, (shares.left + 2 * shares.narrow) * LANES), BF16),
        ],
        compiler_params=pltpu.CompilerParams(
            collective_id=0, has_side_effects=True, vmem_limit_bytes=VMEM_LIMIT_FRONT
        ),
    )(*operands)


def mixer_back_kernel(sizes, per_sequence, shares, *refs):
    (
        grad_after_in, grad_mixer_in, block_in_in, mixed, conv, normed_in, weight_in, low_in, in_first, in_second,
        taps_in, gain_first_in, got_front, got_rest, got_out, picks,
    ) = refs[:16]
    grad_input = refs[16]
    landings = refs[17:19]
    units_refs = refs[19:23]
    exchange_sem, seq_sems, local_sems = refs[23], refs[24:26], refs[26:28]
    rim_sem, load_sem = refs[28:30]
    got_in, results = refs[30], refs[31:33]
    (
        rim_out, rim_in, grad_after, mixed_s, conv_s, in_w, grad_mixer, grad_mixed,
        low_in_back, in_tiles, block_in, normed, taps, gain_first,
    ) = refs[33:]
    fsdp_size, seq_size = sizes
    devices = fsdp_size * seq_size
    ring = Ring(fsdp_size)
    me = ring.me * seq_size + ring.x
    tokens, features = grad_mixer.shape
    slots = low_in.shape[1]
    sequences = tokens // per_sequence
    block = min(ROW_BLOCK, per_sequence)
    loads = [
        pltpu.make_async_copy(a, b, load_sem.at[k])
        for k, (a, b) in enumerate(
            (
                (grad_mixer_in, grad_mixer),
                (mixed, mixed_s),
                (conv, conv_s),
                (normed_in, normed),
                (weight_in, in_w),
                (block_in_in, block_in),
                (grad_after_in, grad_after),
            )
        )
    ]
    for copy in loads[:3]:
        copy.start()
    ring.greet(seq_size, devices)
    in_exchange = Exchange(
        ring, seq_size, devices, lambda d: column_tiles(in_tiles, 0, 1, 4 * shares.narrow, d, devices), got_in,
        exchange_sem,
    )
    total_slots = devices * slots
    per = shares.per

    def front_got(t):
        if t < 2:
            return got_front[t].reshape(total_slots, LANES)
        return got_rest[:, :, (t - 2) * LANES : (t - 1) * LANES].reshape(total_slots, LANES)

    def front_first(t):
        return shares.is_first(t, me) if t < 2 else shares.is_first(2, me * per + t - 2)

    def back_got(t):
        return (got_out, got_in)[t][...].reshape(total_slots, LANES)

    sums = [
        Sum(ring, seq_size, k, landings[k], is_first, got, results[k], (seq_sems[k], local_sems[k]), units_refs)
        for k, (got, is_first) in enumerate(
            ((front_got, front_first), (back_got, lambda t: shares.is_first(3 + t, me)))
        )
    ]
    chosen = picks[...].reshape(total_slots, LANES)
    sums[0].add(chosen)
    taps[...] = taps_in[...].astype(F32)
    gain_first[...] = gain_first_in[...].astype(F32)
    parts = tokens // block
    groups = sums[0].groups()
    while len(groups) < 2 * parts - 1:
        groups.append([])

    def rows_of(r):
        return pl.ds(pl.multiple_of(r * block, block), block)

    def masked(r, values):
        row = r * block + lax.broadcasted_iota(jnp.int32, (block, slots), 0)
        column = lax.broadcasted_iota(jnp.int32, (block, slots), 1)
        return jnp.where(row // per_sequence == column // R, ADAPTER_SCALE * values, 0.0).astype(BF16)

    for copy in loads[:3]:
        copy.wait()
    for copy in loads[3:]:
        copy.start()
    middle = slice(features, 2 * features)
    for k in range(sequences):
        at = slice(k * per_sequence, k * per_sequence + 8)
        rim_out[k] = grad_mixer[at, :] * mixed_s[at, middle]
    rim = pltpu.make_async_remote_copy(
        src_ref=rim_out,
        dst_ref=rim_in,
        send_sem=rim_sem.at[0],
        recv_sem=rim_sem.at[1],
        device_id={"seq": lax.rem(ring.x + seq_size - 1, seq_size)},
        device_id_type=MESH,
    )
    rim.start()
    rim.wait_recv()
    inner = (ring.x < seq_size - 1).astype(F32)

    first_lists = share_out(groups[: parts - 1], parts - 1)

    @pl.loop(0, parts)
    def _(r):
        run_tick([[]] + first_lists, r)
        at = rows_of(r)
        back = grad_mixer[at, :]
        through = back * mixed_s[at, middle]
        after_at = pl.ds(pl.multiple_of(jnp.minimum((r + 1) * block, tokens - 8), 8), 8)
        beyond = grad_mixer[after_at, :] * mixed_s[after_at, middle]
        last = lax.rem((r + 1) * block, per_sequence) == 0
        beyond = jnp.where(last, rim_in[(r * block) // per_sequence] * inner, beyond)
        extended = jnp.concatenate([through, beyond], axis=0)
        gated = (
            taps[2:3, :] * through + taps[1:2, :] * extended[1 : block + 1] + taps[0:1, :] * extended[2 : block + 2]
        )
        grad_mixed[at, :features] = (gated * mixed_s[at, 2 * features :]).astype(BF16)
        grad_mixed[at, middle] = (back * conv_s[at, :]).astype(BF16)
        grad_mixed[at, 2 * features :] = (gated * mixed_s[at, :features]).astype(BF16)
        low_in_back[at, :] = masked(r, dot_nt(grad_mixed[at, :], in_second[...]))

    for copy in loads[3:]:
        copy.wait()
    in_tiles[:, features : 4 * features] = dot_tn(low_in[...], grad_mixed[...]).astype(BF16)
    in_tiles[:, :features] = dot_tn(low_in_back[...], normed[...]).astype(BF16)
    in_exchange.start()

    def finish(r):
        at = rows_of(r)
        rows = block_in[at, :].astype(F32)
        inverse = lax.rsqrt(jnp.mean(rows * rows, axis=-1, keepdims=True) + EPSILON)
        unit_rows = rows * inverse
        gradient = dot_nt(grad_mixed[at, :], in_w[...]) + dot_nt(low_in_back[at, :], in_first[...])
        scaled = gradient * gain_first[...]
        grad_input[at, :] = (
            grad_after[at, :]
            + inverse * (scaled - unit_rows * jnp.mean(scaled * unit_rows, axis=-1, keepdims=True))
        ).astype(BF16)

    def add_last():
        in_exchange.arrived()
        sums[1].add(chosen)

    rest = share_out(groups[parts - 1 :], parts)
    rest[-1] = rest[-1] + [add_last]

    @pl.loop(0, parts)
    def _(r):
        run_tick(rest, r)
        finish(r)

    for actions in sums[1].groups():
        for action in actions:
            action()
    for member in sums:
        member.unit.collect()
    for member in sums:
        member.drain()
    in_exchange.drain()
    rim.wait_send()


def mixer_back(sizes, per_sequence, shares, operands):
    fsdp_size, seq_size = sizes
    devices = fsdp_size * seq_size
    tokens, features = operands[0].shape
    slots = operands[7].shape[1]
    sequences = tokens // per_sequence
    tiles = (2 + shares.per, 2)
    return pl.pallas_call(
        functools.partial(mixer_back_kernel, sizes, per_sequence, shares),
        out_shape=(jax.ShapeDtypeStruct((tokens, features), BF16),)
        + tuple(jax.ShapeDtypeStruct((fsdp_size, seq_size, count, LANES, LANES), BF16) for count in tiles),
        in_specs=[ANYWHERE] * 7 + [IN_VMEM] * 9,
        out_specs=(IN_VMEM,) + (ANYWHERE,) * 2,
        scratch_shapes=unit_sems(2, fsdp_size // 2)
        + [pltpu.SemaphoreType.DMA((3,))]
        + [pltpu.SemaphoreType.DMA((2, seq_size))] * 2
        + [pltpu.SemaphoreType.DMA((1,))] * 2
        + [
            pltpu.SemaphoreType.DMA((2,)),
            pltpu.SemaphoreType.DMA((7,)),
            pltpu.VMEM((devices, slots, LANES), BF16),
        ]
        + [pltpu.VMEM((count, LANES, LANES), BF16) for count in tiles]
        + [
            pltpu.VMEM((sequences, 8, features), F32),
            pltpu.VMEM((sequences, 8, features), F32),
            pltpu.VMEM((tokens, features), F32),
            pltpu.VMEM((tokens, 3 * features), F32),
            pltpu.VMEM((tokens, features), F32),
            pltpu.VMEM((features, 3 * features), BF16),
            pltpu.VMEM((tokens, features), F32),
            pltpu.VMEM((tokens, 3 * features), BF16),
            pltpu.VMEM((tokens, slots), BF16),
            pltpu.VMEM((slots, 4 * shares.narrow * LANES), BF16),
            pltpu.VMEM((tokens, features), BF16),
            pltpu.VMEM((tokens, features), BF16),
            pltpu.VMEM((3, features), F32),
            pltpu.VMEM((1, features), F32),
        ],
        compiler_params=pltpu.CompilerParams(
            collective_id=2, has_side_effects=True, vmem_limit_bytes=VMEM_LIMIT_FRONT
        ),
    )(*operands)


def spread_kernel(layout, *refs):
    sources, outs = refs[:2], refs[2:]
    for out, (first, runs) in zip(outs, layout):
        for source, start, stride, offset, count in runs:

            @pl.loop(0, count)
            def _(k, source=sources[source], start=start, stride=stride, offset=offset, out=out, first=first):
                at = pl.ds(pl.multiple_of((offset + k) * LANES, LANES), LANES)
                tile = source[start + k * stride].astype(F32)
                if first:
                    out[at, :] = tile
                else:
                    out[:, at] = tile


def spread(shares, landings):
    wide, narrow = shares.wide, shares.narrow
    places = shares.places()
    layout, shapes = [], []
    for name, count in (
        ("in_first", narrow),
        ("in_second", 3 * narrow),
        ("out_first", narrow),
        ("out_second", narrow),
        ("gate_first", narrow),
        ("gate_second", wide),
        ("up_first", narrow),
        ("up_second", wide),
        ("down_first", wide),
        ("down_second", narrow),
    ):
        runs, k = [], 0
        while k < count:
            source, start = places[(name, k)]
            stride, length = 1, 1
            if k + 1 < count and places[(name, k + 1)][0] == source:
                stride = places[(name, k + 1)][1] - start
            while k + length < count and places[(name, k + length)] == (source, start + length * stride):
                length += 1
            runs.append((source, start, stride, k, length))
            k += length
        first = name.endswith("first")
        layout.append((first, tuple(runs)))
        shapes.append(jax.ShapeDtypeStruct((count * LANES, LANES) if first else (LANES, count * LANES), F32))
    return pl.pallas_call(
        functools.partial(spread_kernel, tuple(layout)),
        out_shape=tuple(shapes),
        in_specs=[IN_VMEM] * 2,
        out_specs=(IN_VMEM,) * len(shapes),
        compiler_params=pltpu.CompilerParams(vmem_limit_bytes=VMEM_LIMIT),
    )(*(landing.reshape(-1, LANES, LANES) for landing in landings))


def per_device(
    block_input,
    output_grad,
    adapter_ids,
    in_weight,
    out_weight,
    gate_weight,
    up_weight,
    down_weight,
    conv_weight,
    first_gain,
    second_gain,
    infirst_adapter,
    insecond_adapter,
    outfirst_adapter,
    outsecond_adapter,
    gatefirst_adapter,
    gatesecond_adapter,
    upfirst_adapter,
    upsecond_adapter,
    downfirst_adapter,
    downsecond_adapter,
):
    batches, seq_count, local_len, features = block_input.shape
    sequences = batches * seq_count
    tokens = sequences * local_len
    fsdp_size, seq_size = lax.axis_size("fsdp"), lax.axis_size("seq")
    hidden_size = gate_weight.shape[1]
    shares = Shares(fsdp_size * seq_size, features, hidden_size)
    gain_first, gain_second = first_gain[None, :], second_gain[None, :]
    cotangent = output_grad.reshape(tokens, features)
    block_in = block_input.reshape(tokens, features)
    (
        grad_after, _, low_in, _, in_first, in_second, _, _, _,
        block_output, _, mixed_in, conv_out, _, normed, weight_in, _, _, _,
        grad_mixer, got_front, got_rest, got_out, picks,
    ) = front(
        (fsdp_size, seq_size),
        local_len,
        shares,
        (
            block_in,
            cotangent,
            adapter_ids.reshape(sequences),
            conv_weight,
            gain_first,
            gain_second,
            infirst_adapter,
            insecond_adapter,
            outfirst_adapter,
            outsecond_adapter,
            gatefirst_adapter,
            upfirst_adapter,
            downsecond_adapter,
            gatesecond_adapter,
            upsecond_adapter,
            downfirst_adapter,
            in_weight,
            out_weight,
            gate_weight,
            up_weight,
            down_weight,
        ),
    )
    grad_input, *landings = mixer_back(
        (fsdp_size, seq_size),
        local_len,
        shares,
        (
            grad_after,
            grad_mixer,
            block_in,
            mixed_in,
            conv_out,
            normed,
            weight_in,
            low_in,
            in_first,
            in_second,
            conv_weight,
            gain_first,
            got_front,
            got_rest,
            got_out,
            picks,
        ),
    )
    shape = block_input.shape
    return (block_output.reshape(shape), grad_input.reshape(shape)) + tuple(spread(shares, landings))


def solution(mesh):
    return jax.shard_map(
        per_device,
        mesh=mesh,
        in_specs=(
            P(None, "fsdp", "seq", None),
            P(None, "fsdp", "seq", None),
            P(None, "fsdp"),
            P("fsdp", None),
            P("fsdp", None),
            P("fsdp", None),
            P("fsdp", None),
            P("fsdp", None),
            P(),
            P(),
            P(),
            P(),
            P(),
            P(),
            P(),
            P(),
            P(),
            P(),
            P(),
            P(),
            P(),
        ),
        out_specs=(
            P(None, "fsdp", "seq", None),
            P(None, "fsdp", "seq", None),
            P(),
            P(),
            P(),
            P(),
            P(),
            P(),
            P(),
            P(),
            P(),
            P(),
        ),
        check_vma=False,
    )
```

```python
import functools

import jax
import jax.numpy as jnp
from jax import lax
from jax.experimental import pallas as pl
from jax.experimental.pallas import tpu as pltpu
from jax.sharding import PartitionSpec as P

R = 16
LANES = 128
EPSILON = 1e-05
ADAPTER_SCALE = 0.5
MESH = pl.DeviceIdType.MESH
BF16 = jnp.bfloat16
F32 = jnp.float32
VMEM_LIMIT = 62 * 1024 * 1024
FF_CHUNK = 512
ROW_BLOCK = 256
WIDE_BLOCK = 512
VMEM_LIMIT_FRONT = 63 * 1024 * 1024


def dot_nn(left, right):
    return jnp.dot(left, right, preferred_element_type=F32)


def dot_nt(left, right):
    return lax.dot_general(left, right, (((1,), (1,)), ((), ())), preferred_element_type=F32)


def dot_tn(left, right):
    return lax.dot_general(left, right, (((0,), (0,)), ((), ())), preferred_element_type=F32)


def when(condition, action):
    if isinstance(condition, bool):
        if condition:
            action()
    else:
        pl.when(condition)(action)


class Ring:
    def __init__(self, fsdp_size):
        self.count = fsdp_size // 2
        self.me = lax.axis_index("fsdp")
        self.core = lax.rem(self.me, 2)
        chip = self.me // 2
        self.grid = fsdp_size == 16
        if self.grid:
            z, y = chip // 2, lax.rem(chip, 2)
            self.place = y * z + (1 - y) * (7 - z)
        else:
            self.place = chip
        x = lax.axis_index("seq")
        self.x = x
        self.role = lax.rem(x, 2)
        self.to_next = {"fsdp": self.device(lax.rem(self.place + 1, self.count))}
        self.to_prev = {"fsdp": self.device(lax.rem(self.place + self.count - 1, self.count))}
        self.to_core = {"fsdp": self.me + 1 - 2 * self.core}
        self.to_seq = {"seq": x + 1 - 2 * self.role}

    def device(self, place):
        if self.grid:
            y = 1 - place // 4
            z = y * place + (1 - y) * (7 - place)
            return (z * 2 + y) * 2 + self.core
        return place * 2 + self.core

    def at_step(self, direction, step):
        if direction == 0:
            return self.device(lax.rem(self.place + self.count - step, self.count))
        return self.device(lax.rem(self.place + step, self.count))

    def target(self, k, seq_size, devices):
        d = lax.rem(self.me * seq_size + self.x + k, devices)
        return d, {"fsdp": d // seq_size, "seq": lax.rem(d, seq_size)}

    def greet(self, seq_size, devices):
        barrier = pltpu.get_barrier_semaphore()

        @pl.loop(1, devices)
        def _(k):
            device = self.target(k, seq_size, devices)[1]
            pl.semaphore_signal(barrier, inc=1, device_id=device, device_id_type=MESH)

        pl.semaphore_wait(barrier, devices - 1)


class Exchange:
    def __init__(self, ring, seq_size, devices, source, got, sems):
        self.ring, self.seq_size, self.devices = ring, seq_size, devices
        self.source, self.got, self.sems = source, got, sems
        self.me = ring.me * seq_size + ring.x

    def own(self):
        return pltpu.make_async_copy(self.source(self.me), self.got.at[self.me], self.sems.at[2])

    def start(self):
        self.own().start()

        @pl.loop(1, self.devices)
        def _(k):
            d, device = self.ring.target(k, self.seq_size, self.devices)
            pltpu.make_async_remote_copy(
                src_ref=self.source(d),
                dst_ref=self.got.at[self.me],
                send_sem=self.sems.at[0],
                recv_sem=self.sems.at[1],
                device_id=device,
                device_id_type=MESH,
            ).start()

    def all_pieces(self):
        others = self.got.at[pl.ds(0, self.devices - 1)]
        return pltpu.make_async_remote_copy(
            src_ref=others,
            dst_ref=others,
            send_sem=self.sems.at[0],
            recv_sem=self.sems.at[1],
            device_id=self.ring.to_next,
            device_id_type=MESH,
        )

    def arrived(self):
        self.own().wait()
        self.all_pieces().wait_recv()

    def drain(self):
        self.all_pieces().wait_send()


class Unit:
    def __init__(self, ring, number, spot, sems):
        self.ring, self.number, self.spot = ring, number, spot
        self.send, self.ring_sem, self.seq_sem, self.core_sem = sems
        half = ring.count // 2
        self.reaches = ((half, ring.count - 1 - half), (ring.count - 1 - half, half))
        self.steps = half
        self.others = ring.count - 1

    def copy(self, spot, slot, sem, device):
        return pltpu.make_async_remote_copy(
            src_ref=spot,
            dst_ref=spot,
            send_sem=self.send.at[self.number, slot],
            recv_sem=sem,
            device_id=device,
            device_id_type=MESH,
        )

    def arrived(self, spot, sem):
        self.copy(spot, 0, sem, self.ring.to_next).wait_recv()

    def own(self):
        ring, n = self.ring, self.number
        for slot, third in ((0, ring.role), (1, 2)):
            spot = self.spot(third, ring.me)
            self.copy(spot, 2 * slot, self.ring_sem.at[n, slot, 0], ring.to_next).start()
            self.copy(spot, 2 * slot + 1, self.ring_sem.at[n, slot, self.others - 1], ring.to_prev).start()
        for k, third in enumerate((ring.role, 1 - ring.role, 2)):
            self.copy(self.spot(third, ring.me), 4 + k, self.core_sem.at[n, third, 0], ring.to_core).start()

    def relay(self, step):
        ring, n, others = self.ring, self.number, self.others
        for slot, third in ((0, ring.role), (1, 2)):
            for direction in (0, 1):
                reach = self.reaches[slot][direction]
                lane = step - 1 if direction == 0 else others - step
                spot = self.spot(third, ring.at_step(direction, step))

                def forward(slot=slot, direction=direction, lane=lane, spot=spot):
                    onward = self.ring_sem.at[n, slot, lane + 1 - 2 * direction]
                    target = (ring.to_next, ring.to_prev)[direction]
                    self.copy(spot, 7 + slot * others + lane, onward, target).start()

                def take(slot=slot, third=third, reach=reach, lane=lane, spot=spot, forward=forward):
                    self.arrived(spot, self.ring_sem.at[n, slot, lane])
                    when(step < reach, forward)
                    if slot == 0:
                        self.copy(spot, 7 + 2 * others + lane, self.seq_sem.at[n, lane], ring.to_seq).start()
                    core = self.core_sem.at[n, third, 1 + lane]
                    self.copy(spot, 7 + (3 + slot) * others + lane, core, ring.to_core).start()

                when(step <= reach, take)

    def relay_seq(self, step):
        ring, n, others = self.ring, self.number, self.others
        third = 1 - ring.role
        for direction in (0, 1):
            reach = self.reaches[0][direction]
            lane = step - 1 if direction == 0 else others - step
            spot = self.spot(third, ring.at_step(direction, step))

            def take(lane=lane, spot=spot):
                self.arrived(spot, self.seq_sem.at[n, lane])
                core = self.core_sem.at[n, third, 1 + lane]
                self.copy(spot, 7 + 5 * others + lane, core, ring.to_core).start()

            when(step <= reach, take)

    def collect(self):
        for third in range(3):
            for lane in range(self.others + 1):
                self.arrived(self.spot(third, self.ring.me), self.core_sem.at[self.number, third, lane])

    def drain(self):
        ring, others = self.ring, self.others

        def done(third, slot):
            self.copy(self.spot(third, ring.me), slot, self.seq_sem.at[self.number, 0], ring.to_next).wait_send()

        for slot, third in ((0, 0), (1, 2)):
            done(third, 2 * slot)
            done(third, 2 * slot + 1)
            for direction in (0, 1):
                reach = self.reaches[slot][direction]
                for step in range(1, reach + 1):
                    lane = step - 1 if direction == 0 else others - step
                    if step < reach:
                        done(third, 7 + slot * others + lane)
                    done(third, 7 + (3 + slot) * others + lane)
        for lane in range(others):
            done(0, 7 + 2 * others + lane)
            done(0, 7 + 5 * others + lane)
        for k, third in enumerate((0, 0, 2)):
            done(third, 4 + k)


def unit_sems(units, count):
    return [
        pltpu.SemaphoreType.DMA((units, 7 + 6 * (count - 1))),
        pltpu.SemaphoreType.DMA((units, 2, count - 1)),
        pltpu.SemaphoreType.DMA((units, count - 1)),
        pltpu.SemaphoreType.DMA((units, 3, count)),
    ]


def move_in(moves, sems):
    inward = [pltpu.make_async_copy(a, b, sems.at[0, k]) for k, (a, b, _) in enumerate(moves)]
    outward = [pltpu.make_async_copy(b, c, sems.at[1, k]) for k, (_, b, c) in enumerate(moves)]
    for copy in inward:
        copy.start()
    for first, second in zip(inward, outward):
        first.wait()
        second.start()
    return outward


def row_spot(landing, rows, start, size, third, owner):
    return landing.at[pl.ds(owner * rows + start + third * size, size), :]


def column_spot(landing, rows, width, last, third, owner):
    size = last if isinstance(third, int) and third == 2 else width
    start = third * width if isinstance(third, int) else pl.multiple_of(third * width, LANES)
    return landing.at[pl.ds(owner * rows, rows), pl.ds(start, size)]


def down_pieces(down_rows):
    return 3 if down_rows % 288 == 0 else 1


def unroll_gain(out, rows):
    values = rows[...].astype(F32)
    for k in range(values.shape[0]):
        out[:, k * LANES : (k + 1) * LANES] = values[k : k + 1, :]


def in_spot(landing, rows, part, half, third, owner):
    start = pl.multiple_of(third * part + half * (part // 2), LANES)
    return landing.at[pl.ds(owner * rows, rows), pl.ds(start, part // 2)]


def chunk_spot(landing, rows, size, chunk, third, owner):
    start = pl.multiple_of((chunk * 3 + third) * size, LANES)
    return landing.at[:, pl.ds(owner * rows, rows), pl.ds(start, size)]


class Plan:
    LINK, CORE, DELAY, COST = 37e3, 200e3, 1.7, 0.25
    WINDOWS = (4, 8, 1.5, 6, 1.5, 4, 1, 8, 1, 3, 2, 2)

    def __init__(self, units, sizes):
        self.units, self.sizes = units, sizes
        self.now = 0.0
        self.free = {"next": 0.0, "prev": 0.0, "seq": 0.0, "core": 0.0}
        self.steps = units[0].steps
        self.owned = 0
        self.arrival, self.core, self.left, self.collected = {}, {}, {}, set()
        self.list = []

    def send(self, link, size):
        if size:
            rate = self.CORE if link == "core" else self.LINK
            self.free[link] = max(self.free[link], self.now) + size / rate
        return self.free[link] + self.DELAY

    def run_own(self):
        u = self.owned
        self.owned += 1
        shared, common = self.sizes[u]
        self.list.append(self.units[u].own)
        self.now += self.COST
        size = shared + common
        self.arrival[(u, "ring", 1)] = max(self.send("next", size), self.send("prev", size))
        self.core[u] = self.send("core", 2 * shared + common)
        self.left[u] = 2 * self.steps

    def run(self, key):
        u, kind, step = key
        del self.arrival[key]
        shared, common = self.sizes[u]
        unit = self.units[u]
        self.left[u] -= 1
        self.now += self.COST
        if kind == "seq":
            self.list.append(functools.partial(unit.relay_seq, step))
            lanes = sum(step <= reach for reach in unit.reaches[0])
            self.core[u] = max(self.core[u], self.send("core", lanes * shared))
            return
        self.list.append(functools.partial(unit.relay, step))
        across = inward = 0
        onward = []
        for size, reaches, is_shared in ((shared, unit.reaches[0], True), (common, unit.reaches[1], False)):
            for link, reach in zip(("next", "prev"), reaches):
                if step <= reach:
                    inward += size
                    across += size if is_shared else 0
                if step < reach:
                    onward.append(self.send(link, size))
        if onward:
            self.arrival[(u, "ring", step + 1)] = max(onward)
        self.arrival[(u, "seq", step)] = self.send("seq", across)
        self.core[u] = max(self.core[u], self.send("core", inward))

    def ready(self):
        return [key for key, at in sorted(self.arrival.items()) if at <= self.now]

    def pump(self):
        while True:
            keys = self.ready()
            if keys:
                self.run(keys[0])
            elif (
                self.owned < len(self.units)
                and max(self.free["next"], self.free["prev"]) - self.now < self.WINDOWS[self.owned % 12]
            ):
                self.run_own()
            else:
                return

    def can_collect(self, u):
        return u < self.owned and self.left[u] == 0 and self.core[u] <= self.now

    def collect(self, u):
        if u not in self.collected:
            self.collected.add(u)
            self.list.append(self.units[u].collect)
            self.now += self.COST

    def need(self, numbers):
        for u in numbers:
            if u in self.collected:
                continue
            while not self.can_collect(u):
                self.pump()
                if self.can_collect(u):
                    break
                if u < self.owned and self.left[u] == 0:
                    self.now = max(self.now, self.core[u])
                elif self.arrival:
                    self.now = max(self.now, min(self.arrival.values()))
                else:
                    self.run_own()
            self.collect(u)

    def take(self):
        taken, self.list = self.list, []
        return taken

    def tick(self, duration):
        self.pump()
        taken = self.take()
        self.now += duration
        return taken


def run_tick(lists, tick):
    for k, actions in enumerate(lists):
        if not actions:
            continue

        @pl.when(tick == k)
        def _(actions=actions):
            for action in actions:
                action()


def rms_unit(rows):
    inverse = lax.rsqrt(jnp.mean(rows * rows, axis=-1, keepdims=True) + EPSILON)
    return inverse, rows * inverse


def rms_back(scaled, inverse, unit_rows):
    return inverse * (scaled - unit_rows * jnp.mean(scaled * unit_rows, axis=-1, keepdims=True))


ANYWHERE = pl.BlockSpec(memory_space=pl.ANY)
IN_VMEM = pl.BlockSpec(memory_space=pltpu.VMEM)


class Shares:
    def __init__(self, devices, features, hidden_size):
        self.devices = devices
        self.wide, self.narrow = hidden_size // LANES, features // LANES
        self.chunk = FF_CHUNK // LANES
        self.per_chunk = 3 * self.chunk
        third = 3 * self.per_chunk
        names = ("down_first", "gate_second", "up_second")

        def of_third(k):
            return [
                (name, (3 * k + c) * self.chunk + i) for c in range(3) for name in names for i in range(self.chunk)
            ]

        def all_of(name, count):
            return [(name, i) for i in range(count)]

        self.used = min(third, devices)
        self.pitch = third
        sets = [of_third(0), of_third(1)]
        self.spare = [tiles[self.used :] for tiles in sets]
        sets = [tiles[: self.used] for tiles in sets]
        narrow = self.narrow
        rest = of_third(2) + all_of("gate_first", narrow) + all_of("up_first", narrow)
        rest += all_of("down_second", narrow) + self.spare[0] + self.spare[1]
        self.rest_all = len(rest)
        self.per = max(1, len(rest) // devices)
        self.rest_used = min(len(rest), self.per * devices)
        self.left = len(rest) - self.rest_used
        sets.append(rest[: self.rest_used])
        sets.append(rest[self.rest_used :] + all_of("out_first", narrow) + all_of("out_second", narrow))
        sets.append(all_of("in_first", narrow) + all_of("in_second", 3 * narrow))
        self.sets = sets
        self.rest_start = 2 * self.pitch
        self.grads_width = (self.rest_start + self.rest_all) * LANES

    def is_first(self, number, tile):
        flags = [name.endswith("first") for name, _ in self.sets[number]]
        found, start = tile < 0, 0
        for k in range(1, len(flags) + 1):
            if k == len(flags) or flags[k] != flags[start]:
                if flags[start]:
                    found = found | ((tile >= start) & (tile < k))
                start = k
        return found

    def places(self):
        found = {}
        for number, tiles in enumerate(self.sets):
            for k, tile in enumerate(tiles):
                if number == 2:
                    found[tile] = (0, (2 + self.per) * (k // self.per) + 2 + k % self.per)
                else:
                    found[tile] = (0, (2 + self.per) * k + number) if number < 2 else (number - 2, k)
        return found


def column_tiles(source, start, count, used, d, devices):
    if used // count < devices:
        d = lax.rem(d, used // count)
    return source.at[:, pl.ds(pl.multiple_of((start + d * count) * LANES, LANES), count * LANES)]


class Sum:
    def __init__(self, ring, seq_size, number, landing, is_first, got, result, sems, unit_sems_refs):
        self.ring, self.seq_size, self.landing = ring, seq_size, landing
        self.is_first, self.got, self.result = is_first, got, result
        self.seq_sem, self.local_sem = sems
        self.place = landing.at[ring.me, ring.x]
        self.unit = Unit(ring, number, self.spot, unit_sems_refs)

    def spot(self, third, owner):
        size = 32 if isinstance(third, int) and third == 2 else 48
        return self.landing.at[owner, :, :, pl.ds(third * 48, size), :]

    def add(self, chosen):
        tiles = self.result.shape[0]
        for t in range(tiles):
            tile = dot_tn(chosen, self.got(t))
            self.result[t] = jnp.where(self.is_first(t), tile.T, tile).astype(BF16)
        store = pltpu.make_async_copy(self.result, self.place, self.local_sem.at[0])
        store.start()
        store.wait()
        for k in range(1, self.seq_size):
            self.across(k).start()

    def across(self, k):
        return pltpu.make_async_remote_copy(
            src_ref=self.place,
            dst_ref=self.place,
            send_sem=self.seq_sem.at[0, k],
            recv_sem=self.seq_sem.at[1, k],
            device_id={"seq": lax.rem(self.ring.x + k, self.seq_size)},
            device_id_type=MESH,
        )

    def crossed(self):
        for k in range(1, self.seq_size):
            self.across(k).wait_recv()

    def groups(self):
        unit = self.unit
        found = [[self.crossed, unit.own], [functools.partial(unit.relay, 1)]]
        for step in range(2, unit.steps + 1):
            found.append([functools.partial(unit.relay, step), functools.partial(unit.relay_seq, step - 1)])
        return found + [[functools.partial(unit.relay_seq, unit.steps)]]

    def drain(self):
        self.unit.drain()
        for k in range(1, self.seq_size):
            self.across(k).wait_send()


def share_out(groups, ticks):
    cuts = [len(groups) * k // ticks for k in range(ticks + 1)]
    return [sum(groups[cuts[k] : cuts[k + 1]], []) for k in range(ticks)]


def front_kernel(sizes, per_sequence, shares, *refs):
    (
        block_any, cotangent_any, ids, taps_in, gain_first_in, gain_second_in,
        in_first, in_second, out_first, out_second, gate_first, up_first, down_second,
        gate_second, up_second, down_first, in_own, out_own, gate_own, up_own, down_own,
    ) = refs[:21]
    (
        grad_second, grads, low_in, low_out, in_first_s, in_second_s, out_first_s, out_second_s, pick_t,
        block_out, after_out, mixed_out, conv_out, mixer_out, normed_out, in_all, out_all, gu_all, down_all,
        grad_mixer_out, got_front, got_rest, out_tiles, picks,
    ) = refs[21:45]
    sems, local_sem, load_sem, stage_sem, rim_sem, out_sem = refs[45:49], refs[49], refs[50], refs[51], refs[52], refs[53]
    exchange_sems = refs[54:58]
    held = refs[58:63]
    pick, taps, gain_first, gain_second, out_grads, block_in, cotangent, input_sem = refs[-8:]
    (
        total, wide, gate_w, up_w, down_w, normed, mixer, second, gate_up_first, first_down, second_gu, second_down,
        low_gu, grad_low_down, low_down, grad_low_gu, partial, rim_out, rim_in,
    ) = refs[63:-8]
    fsdp_size, seq_size = sizes
    ring = Ring(fsdp_size)
    rows, down_rows = gate_own.shape[0], down_own.shape[0]
    tokens, features = cotangent.shape
    hidden_size = gate_own.shape[1]
    chunks = hidden_size // FF_CHUNK
    sequences = tokens // per_sequence
    block = min(ROW_BLOCK, per_sequence)
    wide_block = min(WIDE_BLOCK, tokens)
    blocks, wide_blocks = tokens // block, tokens // wide_block
    slots = low_in.shape[1]
    mine = pl.ds(ring.me * rows, rows)
    moved = move_in(
        [
            (in_own, held[0], in_all.at[mine, :]),
            (out_own, held[1], out_all.at[mine, :]),
            (down_own, held[4], down_all.at[pl.ds(ring.me * down_rows, down_rows), :]),
            (gate_own, held[2], gu_all.at[0, mine, :]),
            (up_own, held[3], gu_all.at[1, mine, :]),
        ],
        local_sem,
    )
    stages = []
    for k in range(-(-hidden_size // features)):
        width = min(features, hidden_size - k * features)
        part, lanes = pl.ds(k * features, width), pl.ds(k * LANES, LANES)
        stages += [
            (gate_second.at[:, part], second.at[lanes, pl.ds(0, width)]),
            (up_second.at[:, part], normed.at[lanes, pl.ds(0, width)]),
            (down_first.at[part, :], mixer.at[pl.ds(0, width), lanes]),
        ]
    stages = [pltpu.make_async_copy(a, b, stage_sem.at[k]) for k, (a, b) in enumerate(stages)]
    stages.append(pltpu.make_async_copy(block_any, block_in, input_sem.at[0]))
    stages.append(pltpu.make_async_copy(cotangent_any, cotangent, input_sem.at[1]))
    for copy in stages:
        copy.start()
    devices = fsdp_size * seq_size
    ring.greet(seq_size, devices)

    part = in_all.shape[1] // 3
    out_x = 3 * features // 8
    unit_list, sizes_of = [], []

    def add_unit(spot, shared, common):
        unit_list.append(Unit(ring, len(unit_list), spot, sems))
        sizes_of.append((2 * shared, 2 * common))

    for k in range(2):
        add_unit(functools.partial(in_spot, in_all, rows, part, k), rows * part // 2, rows * part // 2)
    last_out = features - 2 * out_x
    add_unit(functools.partial(column_spot, out_all, rows, out_x, last_out), rows * out_x, rows * last_out)
    pieces = down_pieces(down_rows)
    for k in range(pieces):
        size = down_rows // pieces // 3
        add_unit(functools.partial(row_spot, down_all, down_rows, 3 * size * k, size), size * features, size * features)
    fixed = len(unit_list)
    comm_chunks = 2 * chunks // 3
    comm_size = hidden_size // comm_chunks // 3
    for k in range(comm_chunks):
        add_unit(functools.partial(chunk_spot, gu_all, rows, comm_size, k), 2 * rows * comm_size, 2 * rows * comm_size)
    plan = Plan(unit_list, sizes_of)

    def run_all(actions):
        for action in actions:
            action()

    for copy in moved:
        copy.wait()
    run_all(plan.tick(5.0))
    sequence_row = lax.broadcasted_iota(jnp.int32, (slots, LANES), 0)
    sequence_column = lax.broadcasted_iota(jnp.int32, (LANES, slots), 1)
    wanted_row, wanted_column = lax.rem(sequence_row, R), lax.rem(sequence_column, R)
    for k in range(sequences):
        base = ids[k // ids.shape[1], k % ids.shape[1]] * R
        wanted_row += jnp.where(sequence_row // R == k, base, 0)
        wanted_column += jnp.where(sequence_column // R == k, base, 0)
    pick_t[...] = (wanted_row == lax.broadcasted_iota(jnp.int32, (slots, LANES), 1)).astype(F32).astype(BF16)
    pick[...] = (wanted_column == lax.broadcasted_iota(jnp.int32, (LANES, slots), 0)).astype(F32).astype(BF16)
    taps[...] = taps_in[...].astype(F32)
    unroll_gain(gain_first, gain_first_in)
    unroll_gain(gain_second, gain_second_in)

    def rows_of(r, size=block):
        return pl.ds(pl.multiple_of(r * size, size), size)

    def masked(r, values, size=block):
        row = r * size + lax.broadcasted_iota(jnp.int32, (size, slots), 0)
        column = lax.broadcasted_iota(jnp.int32, (size, slots), 1)
        return jnp.where(row // per_sequence == column // R, ADAPTER_SCALE * values, 0.0).astype(BF16)

    for copy in stages:
        copy.wait()
    for k in range(-(-hidden_size // features)):
        width = min(features, hidden_size - k * features)
        at, lanes = slice(k * features, k * features + width), slice(k * LANES, (k + 1) * LANES)
        second_gu[0, :, at] = dot_nn(pick_t[...], second[lanes, :width]).astype(BF16)
        second_gu[1, :, at] = dot_nn(pick_t[...], normed[lanes, :width]).astype(BF16)
        first_down[at, :] = dot_nn(mixer[:width, lanes], pick[...]).astype(BF16)
    second_down[...] = dot_nn(pick_t[...], down_second[...]).astype(BF16)
    in_second_s[...] = dot_nn(pick_t[...], in_second[...]).astype(BF16)
    out_second_s[...] = dot_nn(pick_t[...], out_second[...]).astype(BF16)
    in_first_s[...] = dot_nn(in_first[...], pick[...]).astype(BF16)
    out_first_s[...] = dot_nn(out_first[...], pick[...]).astype(BF16)
    gate_up_first[0] = dot_nn(gate_first[...], pick[...]).astype(BF16)
    gate_up_first[1] = dot_nn(up_first[...], pick[...]).astype(BF16)
    lists = [plan.tick(0.9) for _ in range(blocks)]

    @pl.loop(0, blocks)
    def _(r):
        run_tick(lists, r)
        at = rows_of(r)
        normed_rows = (rms_unit(block_in[at, :].astype(F32))[1] * gain_first[...]).astype(BF16)
        normed[at, :] = normed_rows
        low_in[at, :] = masked(r, dot_nn(normed_rows, in_first_s[...]))
        grad_low_down[at, :] = masked(r, dot_nt(cotangent[at, :], second_down[...]))
        grad_second[at, :] = jnp.zeros((block, features), F32)

    low_down[...] = jnp.zeros_like(low_down)
    grad_low_gu[...] = jnp.zeros_like(grad_low_gu)
    plan.need((0, 1))
    run_all(plan.take())

    half = FF_CHUNK
    middle, last_part, conv_part = (slice(k * features, (k + 1) * features) for k in (1, 2, 3))
    in_loads = []
    for k in range(2):
        for part_number, buffer in ((0, gate_w), (1, up_w)):
            columns = pl.ds(part_number * features + k * half, half)
            in_loads.append(pltpu.make_async_copy(in_all.at[:, columns], buffer.at[k], load_sem.at[k, part_number]))
        place = in_all.at[pl.ds(k * half, half), pl.ds(2 * features, features)]
        in_loads.append(pltpu.make_async_copy(place, down_w.at[k], load_sem.at[k, 2]))
    for copy in in_loads:
        copy.start()
    run_all(plan.tick(2.0))
    for copy in in_loads:
        copy.wait()
    lists = [plan.tick(1.6) for _ in range(blocks)]

    @pl.loop(0, blocks)
    def _(r):
        run_tick(lists, r)
        at = rows_of(r)
        values, low = normed[at, :], low_in[at, :]
        for part_number, buffer in ((0, gate_w), (1, up_w)):
            for k in range(2):
                start = part_number * features + k * half
                columns = slice(start, start + half)
                wide[at, columns] = dot_nn(values, buffer[k]) + dot_nn(low, in_second_s[:, columns])
        wide[at, last_part] = (
            dot_nn(values[:, :half], down_w[0])
            + dot_nn(values[:, half:], down_w[1])
            + dot_nn(low, in_second_s[:, last_part])
        )

    plan.need((2,))
    run_all(plan.take())
    out_loads = [
        pltpu.make_async_copy(out_all.at[:, pl.ds(k * half, half)], gate_w.at[k], load_sem.at[k, 0]) for k in range(2)
    ]
    for copy in out_loads:
        copy.start()
    for k in range(sequences):
        at = slice((k + 1) * per_sequence - 8, (k + 1) * per_sequence)
        rim_out[k] = wide[at, :features] * wide[at, last_part]
    rim = pltpu.make_async_remote_copy(
        src_ref=rim_out,
        dst_ref=rim_in,
        send_sem=rim_sem.at[0],
        recv_sem=rim_sem.at[1],
        device_id={"seq": lax.rem(ring.x + 1, seq_size)},
        device_id_type=MESH,
    )
    rim.start()
    mixed_store = pltpu.make_async_copy(wide.at[:, pl.ds(0, 3 * features)], mixed_out, out_sem.at[0])
    mixed_store.start()
    normed_store = pltpu.make_async_copy(normed.at[pl.ds(0, tokens), :], normed_out, out_sem.at[1])
    normed_store.start()
    run_all(plan.tick(2.0))
    for copy in out_loads:
        copy.wait()
    rim.wait_recv()
    inner = (ring.x > 0).astype(F32)
    lists = [plan.tick(2.2) for _ in range(blocks)]

    @pl.loop(0, blocks)
    def _(r):
        run_tick(lists, r)
        at = rows_of(r)
        gated = wide[at, :features] * wide[at, last_part]
        before_at = pl.ds(pl.multiple_of(jnp.maximum(r * block - 8, 0), 8), 8)
        before = wide[before_at, :features] * wide[before_at, last_part]
        first = lax.rem(r * block, per_sequence) == 0
        before = jnp.where(first, rim_in[(r * block) // per_sequence] * inner, before)
        extended = jnp.concatenate([before, gated], axis=0)
        convolved = (
            taps[0:1, :] * extended[6 : block + 6] + taps[1:2, :] * extended[7 : block + 7] + taps[2:3, :] * gated
        )
        wide[at, conv_part] = convolved
        mixed = (wide[at, middle] * convolved).astype(BF16)
        mixer[at, :] = mixed
        low = masked(r, dot_nn(mixed, out_first_s[...]))
        low_out[at, :] = low
        branch = jnp.concatenate([dot_nn(mixed, gate_w[0]), dot_nn(mixed, gate_w[1])], axis=1)
        after = block_in[at, :].astype(F32) + (branch + dot_nn(low, out_second_s[...]))
        total[at, :] = after
        second_rows = (rms_unit(after)[1] * gain_second[...]).astype(BF16)
        second[at, :] = second_rows
        for k in range(2):
            low_gu[k, at, :] = masked(r, dot_nn(second_rows, gate_up_first[k]))

    stores = [
        pltpu.make_async_copy(wide.at[:, pl.ds(3 * features, features)], conv_out, out_sem.at[2]),
        pltpu.make_async_copy(mixer.at[pl.ds(0, tokens), :], mixer_out, out_sem.at[3]),
        pltpu.make_async_copy(total, after_out, out_sem.at[4]),
    ]
    for copy in stores:
        copy.start()
    plan.need(range(3, fixed))
    run_all(plan.take())

    def down_load(j, s):
        return pltpu.make_async_copy(down_all.at[rows_of(j, FF_CHUNK), :], down_w.at[s], load_sem.at[s, 2])

    def gu_loads(j, s):
        place = rows_of(j, FF_CHUNK)
        return (
            pltpu.make_async_copy(gu_all.at[0, :, place], gate_w.at[s], load_sem.at[s, 0]),
            pltpu.make_async_copy(gu_all.at[1, :, place], up_w.at[s], load_sem.at[s, 1]),
        )

    down_load(0, 0).start()
    mixed_store.wait()
    for copy in stores:
        copy.wait()
    lists = [plan.tick(1.7) for _ in range(chunks)]

    @pl.loop(0, chunks)
    def _(j):
        s = lax.rem(j, 2)

        @pl.when(j + 1 < chunks)
        def _():
            down_load(j + 1, 1 - s).start()

        down_load(j, s).wait()
        run_tick(lists, j)
        columns = rows_of(j, FF_CHUNK)

        @pl.loop(0, wide_blocks)
        def _(r):
            at = rows_of(r, wide_block)
            wide[at, columns] = dot_nt(cotangent[at, :], down_w[s]) + dot_nt(
                grad_low_down[at, :], first_down[columns, :]
            )

    def begin(j):
        for copy in (down_load(j, j % 2),) + gu_loads(j, j % 2):
            copy.start()

    def units_of(j):
        first, last = j * FF_CHUNK // (3 * comm_size), (j * FF_CHUNK + FF_CHUNK - 1) // (3 * comm_size)
        return range(fixed + first, fixed + last + 1)

    plan.need(units_of(0))
    plan.list.append(functools.partial(begin, 0))
    run_all(plan.tick(1.0))

    def tile_columns(start):
        return lambda d: column_tiles(grads, start, 1, shares.used, d, devices)

    sources = [tile_columns(k * shares.pitch) for k in range(2)]
    sources.append(
        lambda d: column_tiles(grads, shares.rest_start, shares.per, shares.rest_used, d, devices)
    )
    sources.append(lambda d: pick_t)
    places = (got_front.at[0], got_front.at[1], got_rest, picks)
    exchanges = [
        Exchange(ring, seq_size, devices, source, place, exchange_sems[k])
        for k, (source, place) in enumerate(zip(sources, places))
    ]
    spare_slot = chunks % 2
    back_loads = [
        pltpu.make_async_copy(out_all.at[:, pl.ds(k * half, half)], buffer.at[spare_slot], load_sem.at[2, k])
        for k, buffer in enumerate((gate_w, up_w))
    ]
    back_loads.append(pltpu.make_async_copy(after_out, wide.at[:, pl.ds(0, features)], load_sem.at[2, 2]))

    def load_back():
        for copy in back_loads:
            copy.start()

    lists, begun = [], 0
    for tick in range(chunks * wide_blocks):
        j = tick // wide_blocks
        plan.pump()
        if begun == j and j + 1 < chunks:
            possible = all(u in plan.collected or plan.can_collect(u) for u in units_of(j + 1))
            if possible or (tick + 1) % wide_blocks == 0:
                plan.need(units_of(j + 1))
                plan.list.append(functools.partial(begin, j + 1))
                begun += 1
        if tick == (chunks - 2) * wide_blocks:
            plan.list += [exchanges[0].start, exchanges[3].start]
        if tick == (chunks - 1) * wide_blocks:
            plan.list += [load_back, exchanges[1].start]
        lists.append(plan.tick(3.9))

    @pl.loop(0, chunks * wide_blocks)
    def _(tick):
        j, r = tick // wide_blocks, lax.rem(tick, wide_blocks)
        s = lax.rem(j, 2)
        columns = rows_of(j, FF_CHUNK)

        @pl.when(r == 0)
        def _():
            for copy in (down_load(j, s),) + gu_loads(j, s):
                copy.wait()
            partial[...] = jnp.zeros_like(partial)

        run_tick(lists, tick)
        at = rows_of(r, wide_block)
        values = second[at, :]
        lows = (grad_low_down[at, :], low_gu[0, at, :], low_gu[1, at, :])
        gate = dot_nn(values, gate_w[s]) + dot_nn(lows[1], second_gu[0, :, columns])
        up = dot_nn(values, up_w[s]) + dot_nn(lows[2], second_gu[1, :, columns])
        back = wide[at, columns]
        sigmoid = 1.0 / (1.0 + jnp.exp(-gate))
        active = gate * sigmoid
        hidden = (active * up).astype(BF16)
        grad_gate = (back * up * (sigmoid + active * (1.0 - sigmoid))).astype(BF16)
        grad_up = (back * active).astype(BF16)
        total[at, :] += dot_nn(hidden, down_w[s])
        grad_second[at, :] += dot_nt(grad_gate, gate_w[s]) + dot_nt(grad_up, up_w[s])
        low_down[at, :] += dot_nn(hidden, first_down[columns, :])
        grad_low_gu[0, at, :] += dot_nt(grad_gate, second_gu[0, :, columns])
        grad_low_gu[1, at, :] += dot_nt(grad_up, second_gu[1, :, columns])
        for k, right in enumerate((hidden, grad_gate, grad_up)):
            partial[k] += dot_tn(lows[k], right)

        @pl.when(r == wide_blocks - 1)
        def _():
            for k in range(3):
                start = (j // 3) * shares.pitch + lax.rem(j, 3) * shares.per_chunk + k * shares.chunk
                place = pl.ds(pl.multiple_of(start * LANES, LANES), FF_CHUNK)
                grads[:, place] = partial[k].astype(BF16)

    normed_store.wait()
    rest_tiles = shares.rest_start + 3 * shares.per_chunk
    base = rest_tiles * LANES

    @pl.loop(0, blocks)
    def _(r):
        at = rows_of(r)
        low = masked(r, low_down[at, :])
        grad_low_down[at, :] = low
        normed[at, :] = (total[at, :] + dot_nn(low, second_down[...])).astype(BF16)
        for k in range(2):
            back_low = masked(r, grad_low_gu[k, at, :])
            low_gu[k, at, :] = back_low
            grad_second[at, :] += dot_nt(back_low, gate_up_first[k])

    block_store = pltpu.make_async_copy(normed.at[pl.ds(0, tokens), :], block_out, out_sem.at[1])
    block_store.start()
    grads[:, base + 2 * features : base + 3 * features] = dot_tn(grad_low_down[...], cotangent[...]).astype(BF16)
    for k in range(2):
        columns = slice(base + k * features, base + (k + 1) * features)
        grads[:, columns] = dot_tn(low_gu[k], second[:tokens, :]).astype(BF16)
    start = base + 3 * features
    for k in range(2):
        width = len(shares.spare[k]) * LANES
        if width:
            spare = (k * shares.pitch + shares.used) * LANES
            grads[:, start : start + width] = grads[:, spare : spare + width]
            start += width
    exchanges[2].start()

    for copy in back_loads:
        copy.wait()
    out_grads[...] = jnp.zeros_like(out_grads)

    @pl.loop(0, blocks)
    def _(r):
        at = rows_of(r)
        inverse, unit_rows = rms_unit(wide[at, :features])
        gradient = cotangent[at, :].astype(F32) + rms_back(
            grad_second[at, :] * gain_second[...], inverse, unit_rows
        )
        grad_second[at, :] = gradient
        rounded = gradient.astype(BF16)
        back_low = masked(r, dot_nt(rounded, out_second_s[...]))
        total[at, :] = (
            dot_nt(rounded[:, :half], gate_w[spare_slot])
            + dot_nt(rounded[:, half:], up_w[spare_slot])
            + dot_nt(back_low, out_first_s[...])
        )
        out_grads[0] += dot_tn(back_low, mixer[at, :])
        out_grads[1] += dot_tn(low_out[at, :], rounded)

    mixer_store = pltpu.make_async_copy(total, grad_mixer_out, out_sem.at[0])
    mixer_store.start()
    if shares.left:
        start = (shares.rest_start + shares.rest_used) * LANES
        out_tiles[:, : shares.left * LANES] = grads[:, start : start + shares.left * LANES]
    for k in range(2):
        start = shares.left * LANES + k * features
        out_tiles[:, start : start + features] = out_grads[k].astype(BF16)
    for unit in unit_list[:fixed]:
        unit.drain()

    @pl.loop(0, comm_chunks)
    def _(k):
        Unit(ring, fixed + k, functools.partial(chunk_spot, gu_all, rows, comm_size, k), sems).drain()

    rim.wait_send()
    block_store.wait()
    mixer_store.wait()
    for member in exchanges:
        member.arrived()
    for member in exchanges:
        member.drain()


def front(sizes, per_sequence, shares, operands):
    fsdp_size, seq_size = sizes
    cotangent, ids = operands[1:3]
    own = operands[-5:]
    tokens, features = cotangent.shape
    hidden_size = own[2].shape[1]
    sequences = ids.shape[0] * ids.shape[1]
    slots = sequences * R
    units = 3 + down_pieces(own[4].shape[0]) + 2 * (hidden_size // FF_CHUNK) // 3
    tall = max(tokens, features)
    stages = 3 * -(-hidden_size // features)

    def shape(*dims, kind=BF16):
        return jax.ShapeDtypeStruct(dims, kind)

    return pl.pallas_call(
        functools.partial(front_kernel, sizes, per_sequence, shares),
        out_shape=(
            shape(tokens, features, kind=F32),
            shape(slots, shares.grads_width),
            shape(tokens, slots),
            shape(tokens, slots),
            shape(features, slots),
            shape(slots, 3 * features),
            shape(features, slots),
            shape(slots, features),
            shape(slots, LANES),
            shape(tokens, features),
            shape(tokens, features, kind=F32),
            shape(tokens, 3 * features, kind=F32),
            shape(tokens, features, kind=F32),
            shape(tokens, features),
            shape(tokens, features),
            shape(features, 3 * features),
            shape(features, features),
            shape(2, features, hidden_size),
            shape(hidden_size, features),
            shape(tokens, features, kind=F32),
            shape(2, shares.devices, slots, LANES),
            shape(shares.devices, slots, shares.per * LANES),
            shape(slots, (shares.left + 2 * shares.narrow) * LANES),
            shape(shares.devices, slots, LANES),
        ),
        in_specs=[ANYWHERE] * 2 + [pl.BlockSpec(memory_space=pltpu.SMEM)] + [IN_VMEM] * 10 + [ANYWHERE] * 8,
        out_specs=(IN_VMEM,) * 9 + (ANYWHERE,) * 13 + (IN_VMEM, ANYWHERE),
        scratch_shapes=unit_sems(units, fsdp_size // 2)
        + [
            pltpu.SemaphoreType.DMA((2, 5)),
            pltpu.SemaphoreType.DMA((3, 3)),
            pltpu.SemaphoreType.DMA((stages,)),
            pltpu.SemaphoreType.DMA((2,)),
            pltpu.SemaphoreType.DMA((5,)),
        ]
        + [pltpu.SemaphoreType.DMA((3,))] * 4
        + [pltpu.VMEM(member.shape, BF16) for member in own]
        + [
            pltpu.VMEM((tokens, features), F32),
            pltpu.VMEM((tokens, hidden_size), F32),
            pltpu.VMEM((2, features, FF_CHUNK), BF16),
            pltpu.VMEM((2, features, FF_CHUNK), BF16),
            pltpu.VMEM((2, FF_CHUNK, features), BF16),
            pltpu.VMEM((tall, features), BF16),
            pltpu.VMEM((tall, features), BF16),
            pltpu.VMEM((tall, features), BF16),
            pltpu.VMEM((2, features, slots), BF16),
            pltpu.VMEM((hidden_size, slots), BF16),
            pltpu.VMEM((2, slots, hidden_size), BF16),
            pltpu.VMEM((slots, features), BF16),
            pltpu.VMEM((2, tokens, slots), BF16),
            pltpu.VMEM((tokens, slots), BF16),
            pltpu.VMEM((tokens, slots), F32),
            pltpu.VMEM((2, tokens, slots), F32),
            pltpu.VMEM((3, slots, FF_CHUNK), F32),
            pltpu.VMEM((sequences, 8, features), F32),
            pltpu.VMEM((sequences, 8, features), F32),
            pltpu.VMEM((LANES, slots), BF16),
            pltpu.VMEM((3, features), F32),
            pltpu.VMEM((1, features), F32),
            pltpu.VMEM((1, features), F32),
            pltpu.VMEM((2, slots, features), F32),
            pltpu.VMEM((tokens, features), BF16),
            pltpu.VMEM((tokens, features), BF16),
            pltpu.SemaphoreType.DMA((2,)),
        ],
        compiler_params=pltpu.CompilerParams(
            collective_id=0, has_side_effects=True, vmem_limit_bytes=VMEM_LIMIT_FRONT
        ),
    )(*operands)


def mixer_back_kernel(sizes, per_sequence, shares, *refs):
    (
        grad_after_in, grad_mixer_in, block_in_in, mixed, conv, normed_in, weight_in, low_in, in_first, in_second,
        taps_in, gain_first_in, got_front, got_rest, out_tiles, picks,
    ) = refs[:16]
    grad_input = refs[16]
    landings = refs[17:20]
    units_refs = refs[20:24]
    exchange_sems, seq_sems, local_sems = refs[24:26], refs[26:29], refs[29:32]
    rim_sem, load_sem = refs[32:34]
    got_out, got_in, results = refs[34], refs[35], refs[36:39]
    (
        rim_out, rim_in, grad_after, mixed_s, conv_s, in_w, grad_mixer, grad_mixed,
        low_in_back, in_tiles, block_in, normed, taps, gain_first,
    ) = refs[39:]
    fsdp_size, seq_size = sizes
    devices = fsdp_size * seq_size
    ring = Ring(fsdp_size)
    me = ring.me * seq_size + ring.x
    tokens, features = grad_mixer.shape
    slots = low_in.shape[1]
    sequences = tokens // per_sequence
    block = min(ROW_BLOCK, per_sequence)
    loads = [
        pltpu.make_async_copy(a, b, load_sem.at[k])
        for k, (a, b) in enumerate(
            (
                (grad_mixer_in, grad_mixer),
                (mixed, mixed_s),
                (conv, conv_s),
                (normed_in, normed),
                (weight_in, in_w),
                (block_in_in, block_in),
                (grad_after_in, grad_after),
            )
        )
    ]
    for copy in loads[:3]:
        copy.start()
    ring.greet(seq_size, devices)
    out_exchange, in_exchange = (
        Exchange(
            ring, seq_size, devices,
            functools.partial(lambda source, d: column_tiles(source, 0, 1, source.shape[1] // LANES, d, devices), source),
            got, exchange_sems[k],
        )
        for k, (source, got) in enumerate(((out_tiles, got_out), (in_tiles, got_in)))
    )
    out_exchange.start()
    total_slots = devices * slots
    per = shares.per

    def front_got(t):
        if t < 2:
            return got_front[t].reshape(total_slots, LANES)
        return got_rest[:, :, (t - 2) * LANES : (t - 1) * LANES].reshape(total_slots, LANES)

    def front_first(t):
        return shares.is_first(t, me) if t < 2 else shares.is_first(2, me * per + t - 2)

    def one_got(got):
        return lambda t: got[...].reshape(total_slots, LANES)

    sums = [
        Sum(ring, seq_size, k, landings[k], is_first, got, results[k], (seq_sems[k], local_sems[k]), units_refs)
        for k, (got, is_first) in enumerate(
            (
                (front_got, front_first),
                (one_got(got_out), lambda t: shares.is_first(3, me)),
                (one_got(got_in), lambda t: shares.is_first(4, me)),
            )
        )
    ]
    chosen = picks[...].reshape(total_slots, LANES)
    sums[0].add(chosen)
    taps[...] = taps_in[...].astype(F32)
    unroll_gain(gain_first, gain_first_in)
    parts = tokens // block

    def add_out():
        out_exchange.arrived()
        sums[1].add(chosen)

    begin_all, *front_steps = sums[0].groups()
    out_steps, in_steps = sums[1].groups(), sums[2].groups()

    def rows_of(r):
        return pl.ds(pl.multiple_of(r * block, block), block)

    def masked(r, values):
        row = r * block + lax.broadcasted_iota(jnp.int32, (block, slots), 0)
        column = lax.broadcasted_iota(jnp.int32, (block, slots), 1)
        return jnp.where(row // per_sequence == column // R, ADAPTER_SCALE * values, 0.0).astype(BF16)

    for copy in loads[:3]:
        copy.wait()
    for copy in loads[3:]:
        copy.start()
    middle = slice(features, 2 * features)
    for k in range(sequences):
        at = slice(k * per_sequence, k * per_sequence + 8)
        rim_out[k] = grad_mixer[at, :] * mixed_s[at, middle]
    rim = pltpu.make_async_remote_copy(
        src_ref=rim_out,
        dst_ref=rim_in,
        send_sem=rim_sem.at[0],
        recv_sem=rim_sem.at[1],
        device_id={"seq": lax.rem(ring.x + seq_size - 1, seq_size)},
        device_id_type=MESH,
    )
    rim.start()
    rim.wait_recv()
    inner = (ring.x < seq_size - 1).astype(F32)

    @pl.loop(0, parts)
    def _(r):
        run_tick([[]] * (parts - 1) + [begin_all], r)
        at = rows_of(r)
        back = grad_mixer[at, :]
        through = back * mixed_s[at, middle]
        after_at = pl.ds(pl.multiple_of(jnp.minimum((r + 1) * block, tokens - 8), 8), 8)
        beyond = grad_mixer[after_at, :] * mixed_s[after_at, middle]
        last = lax.rem((r + 1) * block, per_sequence) == 0
        beyond = jnp.where(last, rim_in[(r * block) // per_sequence] * inner, beyond)
        extended = jnp.concatenate([through, beyond], axis=0)
        gated = (
            taps[2:3, :] * through + taps[1:2, :] * extended[1 : block + 1] + taps[0:1, :] * extended[2 : block + 2]
        )
        grad_mixed[at, :features] = (gated * mixed_s[at, 2 * features :]).astype(BF16)
        grad_mixed[at, middle] = (back * conv_s[at, :]).astype(BF16)
        grad_mixed[at, 2 * features :] = (gated * mixed_s[at, :features]).astype(BF16)
        low_in_back[at, :] = masked(r, dot_nt(grad_mixed[at, :], in_second[...]))

    for copy in loads[3:]:
        copy.wait()
    in_tiles[:, features : 4 * features] = dot_tn(low_in[...], grad_mixed[...]).astype(BF16)
    in_tiles[:, :features] = dot_tn(low_in_back[...], normed[...]).astype(BF16)
    in_exchange.start()

    def finish(r):
        at = rows_of(r)
        rows = block_in[at, :].astype(F32)
        inverse = lax.rsqrt(jnp.mean(rows * rows, axis=-1, keepdims=True) + EPSILON)
        unit_rows = rows * inverse
        gradient = dot_nt(grad_mixed[at, :], in_w[...]) + dot_nt(low_in_back[at, :], in_first[...])
        scaled = gradient * gain_first[...]
        grad_input[at, :] = (
            grad_after[at, :]
            + inverse * (scaled - unit_rows * jnp.mean(scaled * unit_rows, axis=-1, keepdims=True))
        ).astype(BF16)

    def add_last():
        in_exchange.arrived()
        sums[2].add(chosen)

    def step_of(steps, k):
        return steps[k] if 0 <= k < len(steps) else []

    rest = []
    for k in range(len(front_steps) + len(in_steps) + parts):
        actions = [add_last] if k == parts - 2 else []
        actions += step_of(in_steps, k - parts + 1) + step_of(front_steps, k)
        actions += [add_out] if k == 0 else []
        rest.append(actions + step_of(out_steps, k - 1))

    @pl.loop(0, parts)
    def _(r):
        run_tick(rest[:parts], r)
        finish(r)

    for actions in rest[parts:]:
        for action in actions:
            action()
    for member in sums:
        member.unit.collect()
    for member in sums:
        member.drain()
    out_exchange.drain()
    in_exchange.drain()
    rim.wait_send()


def mixer_back(sizes, per_sequence, shares, operands):
    fsdp_size, seq_size = sizes
    devices = fsdp_size * seq_size
    tokens, features = operands[0].shape
    slots = operands[7].shape[1]
    sequences = tokens // per_sequence
    tiles = (2 + shares.per, 1, 1)
    return pl.pallas_call(
        functools.partial(mixer_back_kernel, sizes, per_sequence, shares),
        out_shape=(jax.ShapeDtypeStruct((tokens, features), BF16),)
        + tuple(jax.ShapeDtypeStruct((fsdp_size, seq_size, count, LANES, LANES), BF16) for count in tiles),
        in_specs=[ANYWHERE] * 7 + [IN_VMEM] * 9,
        out_specs=(IN_VMEM,) + (ANYWHERE,) * 3,
        scratch_shapes=unit_sems(3, fsdp_size // 2)
        + [pltpu.SemaphoreType.DMA((3,))] * 2
        + [pltpu.SemaphoreType.DMA((2, seq_size))] * 3
        + [pltpu.SemaphoreType.DMA((1,))] * 3
        + [
            pltpu.SemaphoreType.DMA((2,)),
            pltpu.SemaphoreType.DMA((7,)),
            pltpu.VMEM((devices, slots, LANES), BF16),
            pltpu.VMEM((devices, slots, LANES), BF16),
        ]
        + [pltpu.VMEM((count, LANES, LANES), BF16) for count in tiles]
        + [
            pltpu.VMEM((sequences, 8, features), F32),
            pltpu.VMEM((sequences, 8, features), F32),
            pltpu.VMEM((tokens, features), F32),
            pltpu.VMEM((tokens, 3 * features), F32),
            pltpu.VMEM((tokens, features), F32),
            pltpu.VMEM((features, 3 * features), BF16),
            pltpu.VMEM((tokens, features), F32),
            pltpu.VMEM((tokens, 3 * features), BF16),
            pltpu.VMEM((tokens, slots), BF16),
            pltpu.VMEM((slots, 4 * shares.narrow * LANES), BF16),
            pltpu.VMEM((tokens, features), BF16),
            pltpu.VMEM((tokens, features), BF16),
            pltpu.VMEM((3, features), F32),
            pltpu.VMEM((1, features), F32),
        ],
        compiler_params=pltpu.CompilerParams(
            collective_id=2, has_side_effects=True, vmem_limit_bytes=VMEM_LIMIT_FRONT
        ),
    )(*operands)


def spread_kernel(layout, *refs):
    count = len(layout)
    landings, kept, outs, kept_outs = refs[:3], refs[3:5], refs[5 : 5 + count], refs[5 + count : 7 + count]
    sources, held = refs[7 + count : 10 + count], refs[10 + count : 12 + count]
    staged, load_sem, out_sem = refs[12 + count : 12 + 2 * count], refs[-2], refs[-1]
    loads = [pltpu.make_async_copy(a, b, load_sem.at[k]) for k, (a, b) in enumerate(zip(landings + kept, sources + held))]
    for copy in loads:
        copy.start()
    stores = [pltpu.make_async_copy(a, b, out_sem.at[count + k]) for k, (a, b) in enumerate(zip(held, kept_outs))]
    for copy in loads[:3]:
        copy.wait()
    for k, (out, (first, runs)) in enumerate(zip(staged, layout)):
        for source, start, stride, offset, length in runs:

            @pl.loop(0, length)
            def _(j, source=sources[source], start=start, stride=stride, offset=offset, out=out, first=first):
                at = pl.ds(pl.multiple_of((offset + j) * LANES, LANES), LANES)
                tile = source[start + j * stride].astype(F32)
                if first:
                    out[at, :] = tile
                else:
                    out[:, at] = tile

        stores.append(pltpu.make_async_copy(out, outs[k], out_sem.at[k]))
        stores[-1].start()
        if k == 1:
            for j in range(2):
                loads[3 + j].wait()
                stores[j].start()
    for copy in stores:
        copy.wait()


def spread(shares, landings, kept):
    wide, narrow = shares.wide, shares.narrow
    places = shares.places()
    layout, shapes = [], []
    for name, count in (
        ("in_first", narrow),
        ("in_second", 3 * narrow),
        ("out_first", narrow),
        ("out_second", narrow),
        ("gate_first", narrow),
        ("gate_second", wide),
        ("up_first", narrow),
        ("up_second", wide),
        ("down_first", wide),
        ("down_second", narrow),
    ):
        runs, k = [], 0
        while k < count:
            source, start = places[(name, k)]
            stride, length = 1, 1
            if k + 1 < count and places[(name, k + 1)][0] == source:
                stride = places[(name, k + 1)][1] - start
            while k + length < count and places[(name, k + length)] == (source, start + length * stride):
                length += 1
            runs.append((source, start, stride, k, length))
            k += length
        first = name.endswith("first")
        layout.append((first, tuple(runs)))
        shapes.append(jax.ShapeDtypeStruct((count * LANES, LANES) if first else (LANES, count * LANES), F32))
    landings = [landing.reshape(-1, LANES, LANES) for landing in landings]
    kept_shapes = [jax.ShapeDtypeStruct(member.shape, member.dtype) for member in kept]
    return pl.pallas_call(
        functools.partial(spread_kernel, tuple(layout)),
        out_shape=tuple(shapes + kept_shapes),
        in_specs=[ANYWHERE] * 5,
        out_specs=(ANYWHERE,) * (len(shapes) + 2),
        scratch_shapes=[pltpu.VMEM(member.shape, member.dtype) for member in (*landings, *kept, *shapes)]
        + [pltpu.SemaphoreType.DMA((5,)), pltpu.SemaphoreType.DMA((len(shapes) + 2,))],
        compiler_params=pltpu.CompilerParams(vmem_limit_bytes=VMEM_LIMIT),
    )(*landings, *kept)


def per_device(
    block_input,
    output_grad,
    adapter_ids,
    in_weight,
    out_weight,
    gate_weight,
    up_weight,
    down_weight,
    conv_weight,
    first_gain,
    second_gain,
    infirst_adapter,
    insecond_adapter,
    outfirst_adapter,
    outsecond_adapter,
    gatefirst_adapter,
    gatesecond_adapter,
    upfirst_adapter,
    upsecond_adapter,
    downfirst_adapter,
    downsecond_adapter,
):
    batches, seq_count, local_len, features = block_input.shape
    sequences = batches * seq_count
    tokens = sequences * local_len
    fsdp_size, seq_size = lax.axis_size("fsdp"), lax.axis_size("seq")
    hidden_size = gate_weight.shape[1]
    shares = Shares(fsdp_size * seq_size, features, hidden_size)
    gain_first, gain_second = (gain.reshape(-1, LANES) for gain in (first_gain, second_gain))
    cotangent = output_grad.reshape(tokens, features)
    block_in = block_input.reshape(tokens, features)
    (
        grad_after, _, low_in, _, in_first, in_second, _, _, _,
        block_output, _, mixed_in, conv_out, _, normed, weight_in, _, _, _,
        grad_mixer, got_front, got_rest, out_tiles, picks,
    ) = front(
        (fsdp_size, seq_size),
        local_len,
        shares,
        (
            block_in,
            cotangent,
            adapter_ids,
            conv_weight,
            gain_first,
            gain_second,
            infirst_adapter,
            insecond_adapter,
            outfirst_adapter,
            outsecond_adapter,
            gatefirst_adapter,
            upfirst_adapter,
            downsecond_adapter,
            gatesecond_adapter,
            upsecond_adapter,
            downfirst_adapter,
            in_weight,
            out_weight,
            gate_weight,
            up_weight,
            down_weight,
        ),
    )
    grad_input, *landings = mixer_back(
        (fsdp_size, seq_size),
        local_len,
        shares,
        (
            grad_after,
            grad_mixer,
            block_in,
            mixed_in,
            conv_out,
            normed,
            weight_in,
            low_in,
            in_first,
            in_second,
            conv_weight,
            gain_first,
            got_front,
            got_rest,
            out_tiles,
            picks,
        ),
    )
    *gradients, block_output, grad_input = spread(shares, landings, (block_output, grad_input))
    shape = block_input.shape
    return (block_output.reshape(shape), grad_input.reshape(shape)) + tuple(gradients)


def solution(mesh):
    return jax.shard_map(
        per_device,
        mesh=mesh,
        in_specs=(
            P(None, "fsdp", "seq", None),
            P(None, "fsdp", "seq", None),
            P(None, "fsdp"),
            P("fsdp", None),
            P("fsdp", None),
            P("fsdp", None),
            P("fsdp", None),
            P("fsdp", None),
            P(),
            P(),
            P(),
            P(),
            P(),
            P(),
            P(),
            P(),
            P(),
            P(),
            P(),
            P(),
            P(),
        ),
        out_specs=(
            P(None, "fsdp", "seq", None),
            P(None, "fsdp", "seq", None),
            P(),
            P(),
            P(),
            P(),
            P(),
            P(),
            P(),
            P(),
            P(),
            P(),
        ),
        check_vma=False,
    )
```

```python
import functools

import jax
import jax.numpy as jnp
from jax import lax
from jax.experimental import pallas as pl
from jax.experimental.pallas import tpu as pltpu
from jax.sharding import PartitionSpec as P

R = 16
LANES = 128
EPSILON = 1e-05
ADAPTER_SCALE = 0.5
MESH = pl.DeviceIdType.MESH
BF16 = jnp.bfloat16
F32 = jnp.float32
VMEM_LIMIT = 62 * 1024 * 1024
FF_CHUNK = 512
ROW_BLOCK = 256
WIDE_BLOCK = 512
VMEM_LIMIT_FRONT = 63 * 1024 * 1024


def dot_nn(left, right):
    return jnp.dot(left, right, preferred_element_type=F32)


def dot_nt(left, right):
    return lax.dot_general(left, right, (((1,), (1,)), ((), ())), preferred_element_type=F32)


def dot_tn(left, right):
    return lax.dot_general(left, right, (((0,), (0,)), ((), ())), preferred_element_type=F32)


def when(condition, action):
    if isinstance(condition, bool):
        if condition:
            action()
    else:
        pl.when(condition)(action)


class Ring:
    def __init__(self, fsdp_size):
        self.count = fsdp_size // 2
        self.me = lax.axis_index("fsdp")
        self.core = lax.rem(self.me, 2)
        chip = self.me // 2
        self.grid = fsdp_size == 16
        if self.grid:
            z, y = chip // 2, lax.rem(chip, 2)
            self.place = y * z + (1 - y) * (7 - z)
        else:
            self.place = chip
        x = lax.axis_index("seq")
        self.x = x
        self.role = lax.rem(x, 2)
        self.to_next = {"fsdp": self.device(lax.rem(self.place + 1, self.count))}
        self.to_prev = {"fsdp": self.device(lax.rem(self.place + self.count - 1, self.count))}
        self.to_core = {"fsdp": self.me + 1 - 2 * self.core}
        self.to_seq = {"seq": x + 1 - 2 * self.role}

    def device(self, place):
        if self.grid:
            y = 1 - place // 4
            z = y * place + (1 - y) * (7 - place)
            return (z * 2 + y) * 2 + self.core
        return place * 2 + self.core

    def at_step(self, direction, step):
        if direction == 0:
            return self.device(lax.rem(self.place + self.count - step, self.count))
        return self.device(lax.rem(self.place + step, self.count))

    def target(self, k, seq_size, devices):
        d = lax.rem(self.me * seq_size + self.x + k, devices)
        return d, {"fsdp": d // seq_size, "seq": lax.rem(d, seq_size)}

    def greet(self, seq_size, devices):
        barrier = pltpu.get_barrier_semaphore()

        @pl.loop(1, devices)
        def _(k):
            device = self.target(k, seq_size, devices)[1]
            pl.semaphore_signal(barrier, inc=1, device_id=device, device_id_type=MESH)

        pl.semaphore_wait(barrier, devices - 1)


class Exchange:
    def __init__(self, ring, seq_size, devices, source, got, sems):
        self.ring, self.seq_size, self.devices = ring, seq_size, devices
        self.source, self.got, self.sems = source, got, sems
        self.me = ring.me * seq_size + ring.x

    def own(self):
        return pltpu.make_async_copy(self.source(self.me), self.got.at[self.me], self.sems.at[2])

    def start(self):
        self.own().start()

        @pl.loop(1, self.devices)
        def _(k):
            d, device = self.ring.target(k, self.seq_size, self.devices)
            pltpu.make_async_remote_copy(
                src_ref=self.source(d),
                dst_ref=self.got.at[self.me],
                send_sem=self.sems.at[0],
                recv_sem=self.sems.at[1],
                device_id=device,
                device_id_type=MESH,
            ).start()

    def all_pieces(self):
        others = self.got.at[pl.ds(0, self.devices - 1)]
        return pltpu.make_async_remote_copy(
            src_ref=others,
            dst_ref=others,
            send_sem=self.sems.at[0],
            recv_sem=self.sems.at[1],
            device_id=self.ring.to_next,
            device_id_type=MESH,
        )

    def arrived(self):
        self.own().wait()
        self.all_pieces().wait_recv()

    def drain(self):
        self.all_pieces().wait_send()


class Unit:
    def __init__(self, ring, number, spot, sems):
        self.ring, self.number, self.spot = ring, number, spot
        self.send, self.ring_sem, self.seq_sem, self.core_sem = sems
        half = ring.count // 2
        self.reaches = ((half, ring.count - 1 - half), (ring.count - 1 - half, half))
        self.steps = half
        self.others = ring.count - 1

    def copy(self, spot, slot, sem, device):
        return pltpu.make_async_remote_copy(
            src_ref=spot,
            dst_ref=spot,
            send_sem=self.send.at[self.number, slot],
            recv_sem=sem,
            device_id=device,
            device_id_type=MESH,
        )

    def arrived(self, spot, sem):
        self.copy(spot, 0, sem, self.ring.to_next).wait_recv()

    def own(self):
        ring, n = self.ring, self.number
        for slot, third in ((0, ring.role), (1, 2)):
            spot = self.spot(third, ring.me)
            self.copy(spot, 2 * slot, self.ring_sem.at[n, slot, 0], ring.to_next).start()
            self.copy(spot, 2 * slot + 1, self.ring_sem.at[n, slot, self.others - 1], ring.to_prev).start()
        for k, third in enumerate((ring.role, 1 - ring.role, 2)):
            self.copy(self.spot(third, ring.me), 4 + k, self.core_sem.at[n, third, 0], ring.to_core).start()

    def relay(self, step):
        ring, n, others = self.ring, self.number, self.others
        for slot, third in ((0, ring.role), (1, 2)):
            for direction in (0, 1):
                reach = self.reaches[slot][direction]
                lane = step - 1 if direction == 0 else others - step
                spot = self.spot(third, ring.at_step(direction, step))

                def forward(slot=slot, direction=direction, lane=lane, spot=spot):
                    onward = self.ring_sem.at[n, slot, lane + 1 - 2 * direction]
                    target = (ring.to_next, ring.to_prev)[direction]
                    self.copy(spot, 7 + slot * others + lane, onward, target).start()

                def take(slot=slot, third=third, reach=reach, lane=lane, spot=spot, forward=forward):
                    self.arrived(spot, self.ring_sem.at[n, slot, lane])
                    when(step < reach, forward)
                    if slot == 0:
                        self.copy(spot, 7 + 2 * others + lane, self.seq_sem.at[n, lane], ring.to_seq).start()
                    core = self.core_sem.at[n, third, 1 + lane]
                    self.copy(spot, 7 + (3 + slot) * others + lane, core, ring.to_core).start()

                when(step <= reach, take)

    def relay_seq(self, step):
        ring, n, others = self.ring, self.number, self.others
        third = 1 - ring.role
        for direction in (0, 1):
            reach = self.reaches[0][direction]
            lane = step - 1 if direction == 0 else others - step
            spot = self.spot(third, ring.at_step(direction, step))

            def take(lane=lane, spot=spot):
                self.arrived(spot, self.seq_sem.at[n, lane])
                core = self.core_sem.at[n, third, 1 + lane]
                self.copy(spot, 7 + 5 * others + lane, core, ring.to_core).start()

            when(step <= reach, take)

    def collect(self):
        for third in range(3):
            for lane in range(self.others + 1):
                self.arrived(self.spot(third, self.ring.me), self.core_sem.at[self.number, third, lane])

    def drain(self):
        ring, others = self.ring, self.others

        def done(third, slot):
            self.copy(self.spot(third, ring.me), slot, self.seq_sem.at[self.number, 0], ring.to_next).wait_send()

        for slot, third in ((0, 0), (1, 2)):
            done(third, 2 * slot)
            done(third, 2 * slot + 1)
            for direction in (0, 1):
                reach = self.reaches[slot][direction]
                for step in range(1, reach + 1):
                    lane = step - 1 if direction == 0 else others - step
                    if step < reach:
                        done(third, 7 + slot * others + lane)
                    done(third, 7 + (3 + slot) * others + lane)
        for lane in range(others):
            done(0, 7 + 2 * others + lane)
            done(0, 7 + 5 * others + lane)
        for k, third in enumerate((0, 0, 2)):
            done(third, 4 + k)


def unit_sems(units, count):
    return [
        pltpu.SemaphoreType.DMA((units, 7 + 6 * (count - 1))),
        pltpu.SemaphoreType.DMA((units, 2, count - 1)),
        pltpu.SemaphoreType.DMA((units, count - 1)),
        pltpu.SemaphoreType.DMA((units, 3, count)),
    ]


def move_in(moves, sems):
    inward = [pltpu.make_async_copy(a, b, sems.at[0, k]) for k, (a, b, _) in enumerate(moves)]
    outward = [pltpu.make_async_copy(b, c, sems.at[1, k]) for k, (_, b, c) in enumerate(moves)]
    for copy in inward:
        copy.start()
    for first, second in zip(inward, outward):
        first.wait()
        second.start()
    return outward


def row_spot(landing, rows, start, size, third, owner):
    return landing.at[pl.ds(owner * rows + start + third * size, size), :]


def column_spot(landing, rows, width, last, third, owner):
    size = last if isinstance(third, int) and third == 2 else width
    start = third * width if isinstance(third, int) else pl.multiple_of(third * width, LANES)
    return landing.at[pl.ds(owner * rows, rows), pl.ds(start, size)]


def down_pieces(down_rows):
    return 3 if down_rows % 288 == 0 else 1


def unroll_gain(out, rows):
    values = rows[...].astype(F32)
    for k in range(values.shape[0]):
        out[:, k * LANES : (k + 1) * LANES] = values[k : k + 1, :]


def in_spot(landing, rows, part, half, third, owner):
    start = pl.multiple_of(third * part + half * (part // 2), LANES)
    return landing.at[pl.ds(owner * rows, rows), pl.ds(start, part // 2)]


def chunk_spot(landing, rows, size, chunk, third, owner):
    start = pl.multiple_of((chunk * 3 + third) * size, LANES)
    return landing.at[:, pl.ds(owner * rows, rows), pl.ds(start, size)]


class Plan:
    LINK, CORE, DELAY, COST = 41e3, 200e3, 2.0, 0.15
    WINDOWS = (2, 10, 5, 2, 1.5, 10, 2, 4, 1.5, 1.5, 1.5, 8)

    def __init__(self, units, sizes):
        self.units, self.sizes = units, sizes
        self.now = 0.0
        self.free = {"next": 0.0, "prev": 0.0, "seq": 0.0, "core": 0.0}
        self.steps = units[0].steps
        self.owned = 0
        self.arrival, self.core, self.left, self.collected = {}, {}, {}, set()
        self.list = []

    def send(self, link, size):
        if size:
            rate = self.CORE if link == "core" else self.LINK
            self.free[link] = max(self.free[link], self.now) + size / rate
        return self.free[link] + self.DELAY

    def run_own(self):
        u = self.owned
        self.owned += 1
        shared, common = self.sizes[u]
        self.list.append(self.units[u].own)
        self.now += self.COST
        size = shared + common
        self.arrival[(u, "ring", 1)] = max(self.send("next", size), self.send("prev", size))
        self.core[u] = self.send("core", 2 * shared + common)
        self.left[u] = 2 * self.steps

    def run(self, key):
        u, kind, step = key
        del self.arrival[key]
        shared, common = self.sizes[u]
        unit = self.units[u]
        self.left[u] -= 1
        self.now += self.COST
        if kind == "seq":
            self.list.append(functools.partial(unit.relay_seq, step))
            lanes = sum(step <= reach for reach in unit.reaches[0])
            self.core[u] = max(self.core[u], self.send("core", lanes * shared))
            return
        self.list.append(functools.partial(unit.relay, step))
        across = inward = 0
        onward = []
        for size, reaches, is_shared in ((shared, unit.reaches[0], True), (common, unit.reaches[1], False)):
            for link, reach in zip(("next", "prev"), reaches):
                if step <= reach:
                    inward += size
                    across += size if is_shared else 0
                if step < reach:
                    onward.append(self.send(link, size))
        if onward:
            self.arrival[(u, "ring", step + 1)] = max(onward)
        self.arrival[(u, "seq", step)] = self.send("seq", across)
        self.core[u] = max(self.core[u], self.send("core", inward))

    def ready(self):
        return [key for key, at in sorted(self.arrival.items()) if at <= self.now]

    def pump(self):
        while True:
            keys = self.ready()
            if keys:
                self.run(keys[0])
            elif (
                self.owned < len(self.units)
                and max(self.free["next"], self.free["prev"]) - self.now < self.WINDOWS[self.owned % 12]
            ):
                self.run_own()
            else:
                return

    def can_collect(self, u):
        return u < self.owned and self.left[u] == 0 and self.core[u] <= self.now

    def collect(self, u):
        if u not in self.collected:
            self.collected.add(u)
            self.list.append(self.units[u].collect)
            self.now += self.COST

    def need(self, numbers):
        for u in numbers:
            if u in self.collected:
                continue
            while not self.can_collect(u):
                self.pump()
                if self.can_collect(u):
                    break
                if u < self.owned and self.left[u] == 0:
                    self.now = max(self.now, self.core[u])
                elif self.arrival:
                    self.now = max(self.now, min(self.arrival.values()))
                else:
                    self.run_own()
            self.collect(u)

    def take(self):
        taken, self.list = self.list, []
        return taken

    def tick(self, duration):
        self.pump()
        taken = self.take()
        self.now += duration
        return taken


def run_tick(lists, tick):
    for k, actions in enumerate(lists):
        if not actions:
            continue

        @pl.when(tick == k)
        def _(actions=actions):
            for action in actions:
                action()


def rms_unit(rows):
    inverse = lax.rsqrt(jnp.mean(rows * rows, axis=-1, keepdims=True) + EPSILON)
    return inverse, rows * inverse


def rms_back(scaled, inverse, unit_rows):
    return inverse * (scaled - unit_rows * jnp.mean(scaled * unit_rows, axis=-1, keepdims=True))


ANYWHERE = pl.BlockSpec(memory_space=pl.ANY)
IN_VMEM = pl.BlockSpec(memory_space=pltpu.VMEM)


class Shares:
    def __init__(self, devices, features, hidden_size):
        self.devices = devices
        self.wide, self.narrow = hidden_size // LANES, features // LANES
        self.chunk = FF_CHUNK // LANES
        self.per_chunk = 3 * self.chunk
        third = 3 * self.per_chunk
        names = ("down_first", "gate_second", "up_second")

        def of_third(k):
            return [
                (name, (3 * k + c) * self.chunk + i) for c in range(3) for name in names for i in range(self.chunk)
            ]

        def all_of(name, count):
            return [(name, i) for i in range(count)]

        self.used = min(third, devices)
        self.pitch = third
        sets = [of_third(0), of_third(1)]
        self.spare = [tiles[self.used :] for tiles in sets]
        sets = [tiles[: self.used] for tiles in sets]
        narrow = self.narrow
        rest = of_third(2) + all_of("gate_first", narrow) + all_of("up_first", narrow)
        rest += all_of("down_second", narrow) + self.spare[0] + self.spare[1]
        self.rest_all = len(rest)
        self.per = max(1, len(rest) // devices)
        self.rest_used = min(len(rest), self.per * devices)
        self.left = len(rest) - self.rest_used
        sets.append(rest[: self.rest_used])
        sets.append(rest[self.rest_used :] + all_of("out_first", narrow) + all_of("out_second", narrow))
        sets.append(all_of("in_first", narrow) + all_of("in_second", 3 * narrow))
        self.sets = sets
        self.rest_start = 2 * self.pitch
        self.grads_width = (self.rest_start + self.rest_all) * LANES

    def is_first(self, number, tile):
        flags = [name.endswith("first") for name, _ in self.sets[number]]
        found, start = tile < 0, 0
        for k in range(1, len(flags) + 1):
            if k == len(flags) or flags[k] != flags[start]:
                if flags[start]:
                    found = found | ((tile >= start) & (tile < k))
                start = k
        return found

    def places(self):
        found = {}
        for number, tiles in enumerate(self.sets):
            for k, tile in enumerate(tiles):
                if number == 2:
                    found[tile] = (0, (2 + self.per) * (k % self.devices) + 2 + k // self.devices)
                else:
                    found[tile] = (0, (2 + self.per) * k + number) if number < 2 else (number - 2, k)
        return found


def column_tiles(source, start, count, used, d, devices):
    if used // count < devices:
        d = lax.rem(d, used // count)
    return source.at[:, pl.ds(pl.multiple_of((start + d * count) * LANES, LANES), count * LANES)]


class Sum:
    def __init__(self, ring, seq_size, number, landing, is_first, got, result, sems, unit_sems_refs):
        self.ring, self.seq_size, self.landing = ring, seq_size, landing
        self.is_first, self.got, self.result = is_first, got, result
        self.seq_sem, self.local_sem = sems
        self.place = landing.at[ring.me, ring.x]
        self.unit = Unit(ring, number, self.spot, unit_sems_refs)

    def spot(self, third, owner):
        size = 32 if isinstance(third, int) and third == 2 else 48
        return self.landing.at[owner, :, :, pl.ds(third * 48, size), :]

    def add(self, chosen):
        tiles = self.result.shape[0]
        for t in range(tiles):
            tile = dot_nn(chosen, self.got(t))
            self.result[t] = jnp.where(self.is_first(t), tile.T, tile).astype(BF16)
        store = pltpu.make_async_copy(self.result, self.place, self.local_sem.at[0])
        store.start()
        store.wait()
        for k in range(1, self.seq_size):
            self.across(k).start()

    def across(self, k):
        return pltpu.make_async_remote_copy(
            src_ref=self.place,
            dst_ref=self.place,
            send_sem=self.seq_sem.at[0, k],
            recv_sem=self.seq_sem.at[1, k],
            device_id={"seq": lax.rem(self.ring.x + k, self.seq_size)},
            device_id_type=MESH,
        )

    def crossed(self):
        for k in range(1, self.seq_size):
            self.across(k).wait_recv()

    def groups(self):
        unit = self.unit
        found = [[self.crossed, unit.own], [functools.partial(unit.relay, 1)]]
        for step in range(2, unit.steps + 1):
            found.append([functools.partial(unit.relay, step), functools.partial(unit.relay_seq, step - 1)])
        return found + [[functools.partial(unit.relay_seq, unit.steps)]]

    def drain(self):
        self.unit.drain()
        for k in range(1, self.seq_size):
            self.across(k).wait_send()


def share_out(groups, ticks):
    cuts = [len(groups) * k // ticks for k in range(ticks + 1)]
    return [sum(groups[cuts[k] : cuts[k + 1]], []) for k in range(ticks)]


def front_kernel(sizes, per_sequence, shares, *refs):
    (
        block_any, cotangent_any, ids, taps_in, gain_first_in, gain_second_in,
        in_first, in_second, out_first, out_second, gate_first, up_first, down_second,
        gate_second, up_second, down_first, in_own, out_own, gate_own, up_own, down_own,
    ) = refs[:21]
    (
        grad_second, grads, low_in, low_out, in_first_s, in_second_s, out_first_s, out_second_s, pick_t,
        block_out, after_out, mixed_out, conv_out, mixer_out, normed_out, in_all, out_all, gu_all, down_all,
        grad_mixer_out, got_front, got_rest, out_tiles, picks,
    ) = refs[21:45]
    sems, local_sem, load_sem, stage_sem, rim_sem, out_sem = refs[45:49], refs[49], refs[50], refs[51], refs[52], refs[53]
    exchange_sems = refs[54 : 57 + shares.per]
    held = refs[57 + shares.per : 62 + shares.per]
    pick, taps, gain_first, gain_second, out_grads, block_in, cotangent, input_sem = refs[-8:]
    (
        total, wide, gate_w, up_w, down_w, normed, mixer, second, gate_up_first, first_down, second_gu, second_down,
        low_gu, grad_low_down, low_down, grad_low_gu, partial, rim_out, rim_in,
    ) = refs[62 + shares.per : -8]
    fsdp_size, seq_size = sizes
    ring = Ring(fsdp_size)
    rows, down_rows = gate_own.shape[0], down_own.shape[0]
    tokens, features = cotangent.shape
    hidden_size = gate_own.shape[1]
    chunks = hidden_size // FF_CHUNK
    sequences = tokens // per_sequence
    block = min(ROW_BLOCK, per_sequence)
    wide_block = min(WIDE_BLOCK, tokens)
    blocks, wide_blocks = tokens // block, tokens // wide_block
    slots = low_in.shape[1]
    mine = pl.ds(ring.me * rows, rows)
    moved = move_in(
        [
            (in_own, held[0], in_all.at[mine, :]),
            (out_own, held[1], out_all.at[mine, :]),
            (down_own, held[4], down_all.at[pl.ds(ring.me * down_rows, down_rows), :]),
            (gate_own, held[2], gu_all.at[0, mine, :]),
            (up_own, held[3], gu_all.at[1, mine, :]),
        ],
        local_sem,
    )
    stages = []
    for k in range(-(-hidden_size // features)):
        width = min(features, hidden_size - k * features)
        part, lanes = pl.ds(k * features, width), pl.ds(k * LANES, LANES)
        stages += [
            (gate_second.at[:, part], second.at[lanes, pl.ds(0, width)]),
            (up_second.at[:, part], normed.at[lanes, pl.ds(0, width)]),
            (down_first.at[part, :], mixer.at[pl.ds(0, width), lanes]),
        ]
    stages = [pltpu.make_async_copy(a, b, stage_sem.at[k]) for k, (a, b) in enumerate(stages)]
    stages.append(pltpu.make_async_copy(block_any, block_in, input_sem.at[0]))
    stages.append(pltpu.make_async_copy(cotangent_any, cotangent, input_sem.at[1]))
    for copy in stages:
        copy.start()
    devices = fsdp_size * seq_size
    ring.greet(seq_size, devices)

    part = in_all.shape[1] // 3
    out_x = 3 * features // 8
    unit_list, sizes_of = [], []

    def add_unit(spot, shared, common):
        unit_list.append(Unit(ring, len(unit_list), spot, sems))
        sizes_of.append((2 * shared, 2 * common))

    for k in range(2):
        add_unit(functools.partial(in_spot, in_all, rows, part, k), rows * part // 2, rows * part // 2)
    last_out = features - 2 * out_x
    add_unit(functools.partial(column_spot, out_all, rows, out_x, last_out), rows * out_x, rows * last_out)
    pieces = down_pieces(down_rows)
    for k in range(pieces):
        size = down_rows // pieces // 3
        add_unit(functools.partial(row_spot, down_all, down_rows, 3 * size * k, size), size * features, size * features)
    fixed = len(unit_list)
    comm_chunks = 2 * chunks // 3
    comm_size = hidden_size // comm_chunks // 3
    for k in range(comm_chunks):
        add_unit(functools.partial(chunk_spot, gu_all, rows, comm_size, k), 2 * rows * comm_size, 2 * rows * comm_size)
    plan = Plan(unit_list, sizes_of)

    def run_all(actions):
        for action in actions:
            action()

    for copy in moved:
        copy.wait()
    run_all(plan.tick(5.0))
    sequence_row = lax.broadcasted_iota(jnp.int32, (slots, LANES), 0)
    sequence_column = lax.broadcasted_iota(jnp.int32, (LANES, slots), 1)
    wanted_row, wanted_column = lax.rem(sequence_row, R), lax.rem(sequence_column, R)
    for k in range(sequences):
        base = ids[k // ids.shape[1], k % ids.shape[1]] * R
        wanted_row += jnp.where(sequence_row // R == k, base, 0)
        wanted_column += jnp.where(sequence_column // R == k, base, 0)
    pick_t[...] = (wanted_row == lax.broadcasted_iota(jnp.int32, (slots, LANES), 1)).astype(F32).astype(BF16)
    pick[...] = (wanted_column == lax.broadcasted_iota(jnp.int32, (LANES, slots), 0)).astype(F32).astype(BF16)
    taps[...] = taps_in[...].astype(F32)
    unroll_gain(gain_first, gain_first_in)
    unroll_gain(gain_second, gain_second_in)

    def rows_of(r, size=block):
        return pl.ds(pl.multiple_of(r * size, size), size)

    def masked(r, values, size=block):
        row = r * size + lax.broadcasted_iota(jnp.int32, (size, slots), 0)
        column = lax.broadcasted_iota(jnp.int32, (size, slots), 1)
        return jnp.where(row // per_sequence == column // R, ADAPTER_SCALE * values, 0.0).astype(BF16)

    for copy in stages:
        copy.wait()
    for k in range(-(-hidden_size // features)):
        width = min(features, hidden_size - k * features)
        at, lanes = slice(k * features, k * features + width), slice(k * LANES, (k + 1) * LANES)
        second_gu[0, :, at] = dot_nn(pick_t[...], second[lanes, :width]).astype(BF16)
        second_gu[1, :, at] = dot_nn(pick_t[...], normed[lanes, :width]).astype(BF16)
        first_down[at, :] = dot_nn(mixer[:width, lanes], pick[...]).astype(BF16)
    second_down[...] = dot_nn(pick_t[...], down_second[...]).astype(BF16)
    in_second_s[...] = dot_nn(pick_t[...], in_second[...]).astype(BF16)
    out_second_s[...] = dot_nn(pick_t[...], out_second[...]).astype(BF16)
    in_first_s[...] = dot_nn(in_first[...], pick[...]).astype(BF16)
    out_first_s[...] = dot_nn(out_first[...], pick[...]).astype(BF16)
    gate_up_first[0] = dot_nn(gate_first[...], pick[...]).astype(BF16)
    gate_up_first[1] = dot_nn(up_first[...], pick[...]).astype(BF16)
    lists = [plan.tick(0.9) for _ in range(blocks)]

    @pl.loop(0, blocks)
    def _(r):
        run_tick(lists, r)
        at = rows_of(r)
        normed_rows = (rms_unit(block_in[at, :].astype(F32))[1] * gain_first[...]).astype(BF16)
        normed[at, :] = normed_rows
        low_in[at, :] = masked(r, dot_nn(normed_rows, in_first_s[...]))
        grad_low_down[at, :] = masked(r, dot_nt(cotangent[at, :], second_down[...]))
        grad_second[at, :] = jnp.zeros((block, features), F32)

    low_down[...] = jnp.zeros_like(low_down)
    grad_low_gu[...] = jnp.zeros_like(grad_low_gu)
    plan.need((0, 1))
    run_all(plan.take())

    half = FF_CHUNK
    middle, last_part, conv_part = (slice(k * features, (k + 1) * features) for k in (1, 2, 3))
    in_loads = []
    for k in range(2):
        for part_number, buffer in ((0, gate_w), (1, up_w)):
            columns = pl.ds(part_number * features + k * half, half)
            in_loads.append(pltpu.make_async_copy(in_all.at[:, columns], buffer.at[k], load_sem.at[k, part_number]))
        place = in_all.at[pl.ds(k * half, half), pl.ds(2 * features, features)]
        in_loads.append(pltpu.make_async_copy(place, down_w.at[k], load_sem.at[k, 2]))
    for copy in in_loads:
        copy.start()
    run_all(plan.tick(2.0))
    for copy in in_loads:
        copy.wait()
    lists = [plan.tick(1.6) for _ in range(blocks)]

    @pl.loop(0, blocks)
    def _(r):
        run_tick(lists, r)
        at = rows_of(r)
        values, low = normed[at, :], low_in[at, :]
        for part_number, buffer in ((0, gate_w), (1, up_w)):
            for k in range(2):
                start = part_number * features + k * half
                columns = slice(start, start + half)
                wide[at, columns] = dot_nn(values, buffer[k]) + dot_nn(low, in_second_s[:, columns])
        wide[at, last_part] = (
            dot_nn(values[:, :half], down_w[0])
            + dot_nn(values[:, half:], down_w[1])
            + dot_nn(low, in_second_s[:, last_part])
        )

    plan.need((2,))
    run_all(plan.take())
    out_loads = [
        pltpu.make_async_copy(out_all.at[:, pl.ds(k * half, half)], gate_w.at[k], load_sem.at[k, 0]) for k in range(2)
    ]
    for copy in out_loads:
        copy.start()
    for k in range(sequences):
        at = slice((k + 1) * per_sequence - 8, (k + 1) * per_sequence)
        rim_out[k] = wide[at, :features] * wide[at, last_part]
    rim = pltpu.make_async_remote_copy(
        src_ref=rim_out,
        dst_ref=rim_in,
        send_sem=rim_sem.at[0],
        recv_sem=rim_sem.at[1],
        device_id={"seq": lax.rem(ring.x + 1, seq_size)},
        device_id_type=MESH,
    )
    rim.start()
    mixed_store = pltpu.make_async_copy(wide.at[:, pl.ds(0, 3 * features)], mixed_out, out_sem.at[0])
    mixed_store.start()
    normed_store = pltpu.make_async_copy(normed.at[pl.ds(0, tokens), :], normed_out, out_sem.at[1])
    normed_store.start()
    run_all(plan.tick(2.0))
    for copy in out_loads:
        copy.wait()
    rim.wait_recv()
    inner = (ring.x > 0).astype(F32)
    lists = [plan.tick(2.2) for _ in range(blocks)]

    @pl.loop(0, blocks)
    def _(r):
        run_tick(lists, r)
        at = rows_of(r)
        gated = wide[at, :features] * wide[at, last_part]
        before_at = pl.ds(pl.multiple_of(jnp.maximum(r * block - 8, 0), 8), 8)
        before = wide[before_at, :features] * wide[before_at, last_part]
        first = lax.rem(r * block, per_sequence) == 0
        before = jnp.where(first, rim_in[(r * block) // per_sequence] * inner, before)
        extended = jnp.concatenate([before, gated], axis=0)
        convolved = (
            taps[0:1, :] * extended[6 : block + 6] + taps[1:2, :] * extended[7 : block + 7] + taps[2:3, :] * gated
        )
        wide[at, conv_part] = convolved
        mixed = (wide[at, middle] * convolved).astype(BF16)
        mixer[at, :] = mixed
        low = masked(r, dot_nn(mixed, out_first_s[...]))
        low_out[at, :] = low
        branch = jnp.concatenate([dot_nn(mixed, gate_w[0]), dot_nn(mixed, gate_w[1])], axis=1)
        after = block_in[at, :].astype(F32) + (branch + dot_nn(low, out_second_s[...]))
        total[at, :] = after
        second_rows = (rms_unit(after)[1] * gain_second[...]).astype(BF16)
        second[at, :] = second_rows
        for k in range(2):
            low_gu[k, at, :] = masked(r, dot_nn(second_rows, gate_up_first[k]))

    stores = [
        pltpu.make_async_copy(wide.at[:, pl.ds(3 * features, features)], conv_out, out_sem.at[2]),
        pltpu.make_async_copy(mixer.at[pl.ds(0, tokens), :], mixer_out, out_sem.at[3]),
        pltpu.make_async_copy(total, after_out, out_sem.at[4]),
    ]
    for copy in stores:
        copy.start()
    plan.need(range(3, fixed))
    run_all(plan.take())

    def down_load(j, s):
        return pltpu.make_async_copy(down_all.at[rows_of(j, FF_CHUNK), :], down_w.at[s], load_sem.at[s, 2])

    def gu_loads(j, s):
        place = rows_of(j, FF_CHUNK)
        return (
            pltpu.make_async_copy(gu_all.at[0, :, place], gate_w.at[s], load_sem.at[s, 0]),
            pltpu.make_async_copy(gu_all.at[1, :, place], up_w.at[s], load_sem.at[s, 1]),
        )

    down_load(0, 0).start()
    mixed_store.wait()
    for copy in stores:
        copy.wait()
    lists = [plan.tick(1.7) for _ in range(chunks)]

    @pl.loop(0, chunks)
    def _(j):
        s = lax.rem(j, 2)

        @pl.when(j + 1 < chunks)
        def _():
            down_load(j + 1, 1 - s).start()

        down_load(j, s).wait()
        run_tick(lists, j)
        columns = rows_of(j, FF_CHUNK)

        @pl.loop(0, wide_blocks)
        def _(r):
            at = rows_of(r, wide_block)
            wide[at, columns] = dot_nt(cotangent[at, :], down_w[s]) + dot_nt(
                grad_low_down[at, :], first_down[columns, :]
            )

    def begin(j):
        for copy in (down_load(j, j % 2),) + gu_loads(j, j % 2):
            copy.start()

    def units_of(j):
        first, last = j * FF_CHUNK // (3 * comm_size), (j * FF_CHUNK + FF_CHUNK - 1) // (3 * comm_size)
        return range(fixed + first, fixed + last + 1)

    plan.need(units_of(0))
    plan.list.append(functools.partial(begin, 0))
    run_all(plan.tick(1.0))

    def tile_columns(start):
        return lambda d: column_tiles(grads, start, 1, shares.used, d, devices)

    sources = [tile_columns(k * shares.pitch) for k in range(2)]
    for k in range(shares.per):
        sources.append(
            functools.partial(
                lambda k, d: column_tiles(
                    grads, shares.rest_start + k * devices, 1, min(devices, shares.rest_used), d, devices
                ),
                k,
            )
        )
    sources.append(lambda d: pick_t)
    places = [got_front.at[0], got_front.at[1]] + [got_rest.at[k] for k in range(shares.per)] + [picks]
    exchanges = [
        Exchange(ring, seq_size, devices, source, place, exchange_sems[k])
        for k, (source, place) in enumerate(zip(sources, places))
    ]
    spare_slot = chunks % 2
    back_loads = [
        pltpu.make_async_copy(out_all.at[:, pl.ds(k * half, half)], buffer.at[spare_slot], load_sem.at[2, k])
        for k, buffer in enumerate((gate_w, up_w))
    ]
    back_loads.append(pltpu.make_async_copy(after_out, wide.at[:, pl.ds(0, features)], load_sem.at[2, 2]))

    def load_back():
        for copy in back_loads:
            copy.start()

    lists, begun = [], 0
    for tick in range(chunks * wide_blocks):
        j = tick // wide_blocks
        plan.pump()
        if begun == j and j + 1 < chunks:
            possible = all(u in plan.collected or plan.can_collect(u) for u in units_of(j + 1))
            if possible or (tick + 1) % wide_blocks == 0:
                plan.need(units_of(j + 1))
                plan.list.append(functools.partial(begin, j + 1))
                begun += 1
        if tick == (chunks - 2) * wide_blocks:
            plan.list += [exchanges[0].start, exchanges[-1].start]
        if tick == (chunks - 1) * wide_blocks:
            plan.list += [load_back, exchanges[1].start]
        lists.append(plan.tick(3.9))

    @pl.loop(0, chunks * wide_blocks)
    def _(tick):
        j, r = tick // wide_blocks, lax.rem(tick, wide_blocks)
        s = lax.rem(j, 2)
        columns = rows_of(j, FF_CHUNK)

        @pl.when(r == 0)
        def _():
            for copy in (down_load(j, s),) + gu_loads(j, s):
                copy.wait()
            partial[...] = jnp.zeros_like(partial)

        run_tick(lists, tick)
        at = rows_of(r, wide_block)
        values = second[at, :]
        lows = (grad_low_down[at, :], low_gu[0, at, :], low_gu[1, at, :])
        gate = dot_nn(values, gate_w[s]) + dot_nn(lows[1], second_gu[0, :, columns])
        up = dot_nn(values, up_w[s]) + dot_nn(lows[2], second_gu[1, :, columns])
        back = wide[at, columns]
        sigmoid = 1.0 / (1.0 + jnp.exp(-gate))
        active = gate * sigmoid
        hidden = (active * up).astype(BF16)
        grad_gate = (back * up * (sigmoid + active * (1.0 - sigmoid))).astype(BF16)
        grad_up = (back * active).astype(BF16)
        total[at, :] += dot_nn(hidden, down_w[s])
        grad_second[at, :] += dot_nt(grad_gate, gate_w[s]) + dot_nt(grad_up, up_w[s])
        low_down[at, :] += dot_nn(hidden, first_down[columns, :])
        grad_low_gu[0, at, :] += dot_nt(grad_gate, second_gu[0, :, columns])
        grad_low_gu[1, at, :] += dot_nt(grad_up, second_gu[1, :, columns])
        for k, right in enumerate((hidden, grad_gate, grad_up)):
            partial[k] += dot_tn(lows[k], right)

        @pl.when(r == wide_blocks - 1)
        def _():
            for k in range(3):
                start = (j // 3) * shares.pitch + lax.rem(j, 3) * shares.per_chunk + k * shares.chunk
                place = pl.ds(pl.multiple_of(start * LANES, LANES), FF_CHUNK)
                grads[:, place] = partial[k].astype(BF16)

    normed_store.wait()
    ready = 1 if shares.per > 1 and devices <= 3 * shares.per_chunk else 0
    for member in exchanges[2 : 2 + ready]:
        member.start()
    rest_tiles = shares.rest_start + 3 * shares.per_chunk
    base = rest_tiles * LANES

    @pl.loop(0, blocks)
    def _(r):
        at = rows_of(r)
        low = masked(r, low_down[at, :])
        grad_low_down[at, :] = low
        normed[at, :] = (total[at, :] + dot_nn(low, second_down[...])).astype(BF16)
        for k in range(2):
            back_low = masked(r, grad_low_gu[k, at, :])
            low_gu[k, at, :] = back_low
            grad_second[at, :] += dot_nt(back_low, gate_up_first[k])

    block_store = pltpu.make_async_copy(normed.at[pl.ds(0, tokens), :], block_out, out_sem.at[1])
    block_store.start()
    grads[:, base + 2 * features : base + 3 * features] = dot_tn(grad_low_down[...], cotangent[...]).astype(BF16)
    for k in range(2):
        columns = slice(base + k * features, base + (k + 1) * features)
        grads[:, columns] = dot_tn(low_gu[k], second[:tokens, :]).astype(BF16)
    start = base + 3 * features
    for k in range(2):
        width = len(shares.spare[k]) * LANES
        if width:
            spare = (k * shares.pitch + shares.used) * LANES
            grads[:, start : start + width] = grads[:, spare : spare + width]
            start += width
    for member in exchanges[2 + ready : 2 + shares.per]:
        member.start()

    for copy in back_loads:
        copy.wait()
    out_grads[...] = jnp.zeros_like(out_grads)

    @pl.loop(0, blocks)
    def _(r):
        at = rows_of(r)
        inverse, unit_rows = rms_unit(wide[at, :features])
        gradient = cotangent[at, :].astype(F32) + rms_back(
            grad_second[at, :] * gain_second[...], inverse, unit_rows
        )
        grad_second[at, :] = gradient
        rounded = gradient.astype(BF16)
        back_low = masked(r, dot_nt(rounded, out_second_s[...]))
        total[at, :] = (
            dot_nt(rounded[:, :half], gate_w[spare_slot])
            + dot_nt(rounded[:, half:], up_w[spare_slot])
            + dot_nt(back_low, out_first_s[...])
        )
        out_grads[0] += dot_tn(back_low, mixer[at, :])
        out_grads[1] += dot_tn(low_out[at, :], rounded)

    mixer_store = pltpu.make_async_copy(total, grad_mixer_out, out_sem.at[0])
    mixer_store.start()
    if shares.left:
        start = (shares.rest_start + shares.rest_used) * LANES
        out_tiles[:, : shares.left * LANES] = grads[:, start : start + shares.left * LANES]
    for k in range(2):
        start = shares.left * LANES + k * features
        out_tiles[:, start : start + features] = out_grads[k].astype(BF16)
    for unit in unit_list[:fixed]:
        unit.drain()

    @pl.loop(0, comm_chunks)
    def _(k):
        Unit(ring, fixed + k, functools.partial(chunk_spot, gu_all, rows, comm_size, k), sems).drain()

    rim.wait_send()
    block_store.wait()
    mixer_store.wait()
    for member in exchanges:
        member.arrived()
    for member in exchanges:
        member.drain()


def front(sizes, per_sequence, shares, operands):
    fsdp_size, seq_size = sizes
    cotangent, ids = operands[1:3]
    own = operands[-5:]
    tokens, features = cotangent.shape
    hidden_size = own[2].shape[1]
    sequences = ids.shape[0] * ids.shape[1]
    slots = sequences * R
    units = 3 + down_pieces(own[4].shape[0]) + 2 * (hidden_size // FF_CHUNK) // 3
    tall = max(tokens, features)
    stages = 3 * -(-hidden_size // features)

    def shape(*dims, kind=BF16):
        return jax.ShapeDtypeStruct(dims, kind)

    return pl.pallas_call(
        functools.partial(front_kernel, sizes, per_sequence, shares),
        out_shape=(
            shape(tokens, features, kind=F32),
            shape(slots, shares.grads_width),
            shape(tokens, slots),
            shape(tokens, slots),
            shape(features, slots),
            shape(slots, 3 * features),
            shape(features, slots),
            shape(slots, features),
            shape(slots, LANES),
            shape(tokens, features),
            shape(tokens, features, kind=F32),
            shape(tokens, 3 * features, kind=F32),
            shape(tokens, features, kind=F32),
            shape(tokens, features),
            shape(tokens, features),
            shape(features, 3 * features),
            shape(features, features),
            shape(2, features, hidden_size),
            shape(hidden_size, features),
            shape(tokens, features, kind=F32),
            shape(2, shares.devices, slots, LANES),
            shape(shares.per, shares.devices, slots, LANES),
            shape(slots, (shares.left + 2 * shares.narrow) * LANES),
            shape(shares.devices, slots, LANES),
        ),
        in_specs=[ANYWHERE] * 2 + [pl.BlockSpec(memory_space=pltpu.SMEM)] + [IN_VMEM] * 10 + [ANYWHERE] * 8,
        out_specs=(IN_VMEM,) * 9 + (ANYWHERE,) * 13 + (IN_VMEM, ANYWHERE),
        scratch_shapes=unit_sems(units, fsdp_size // 2)
        + [
            pltpu.SemaphoreType.DMA((2, 5)),
            pltpu.SemaphoreType.DMA((3, 3)),
            pltpu.SemaphoreType.DMA((stages,)),
            pltpu.SemaphoreType.DMA((2,)),
            pltpu.SemaphoreType.DMA((5,)),
        ]
        + [pltpu.SemaphoreType.DMA((3,))] * (3 + shares.per)
        + [pltpu.VMEM(member.shape, BF16) for member in own]
        + [
            pltpu.VMEM((tokens, features), F32),
            pltpu.VMEM((tokens, hidden_size), F32),
            pltpu.VMEM((2, features, FF_CHUNK), BF16),
            pltpu.VMEM((2, features, FF_CHUNK), BF16),
            pltpu.VMEM((2, FF_CHUNK, features), BF16),
            pltpu.VMEM((tall, features), BF16),
            pltpu.VMEM((tall, features), BF16),
            pltpu.VMEM((tall, features), BF16),
            pltpu.VMEM((2, features, slots), BF16),
            pltpu.VMEM((hidden_size, slots), BF16),
            pltpu.VMEM((2, slots, hidden_size), BF16),
            pltpu.VMEM((slots, features), BF16),
            pltpu.VMEM((2, tokens, slots), BF16),
            pltpu.VMEM((tokens, slots), BF16),
            pltpu.VMEM((tokens, slots), F32),
            pltpu.VMEM((2, tokens, slots), F32),
            pltpu.VMEM((3, slots, FF_CHUNK), F32),
            pltpu.VMEM((sequences, 8, features), F32),
            pltpu.VMEM((sequences, 8, features), F32),
            pltpu.VMEM((LANES, slots), BF16),
            pltpu.VMEM((3, features), F32),
            pltpu.VMEM((1, features), F32),
            pltpu.VMEM((1, features), F32),
            pltpu.VMEM((2, slots, features), F32),
            pltpu.VMEM((tokens, features), BF16),
            pltpu.VMEM((tokens, features), BF16),
            pltpu.SemaphoreType.DMA((2,)),
        ],
        compiler_params=pltpu.CompilerParams(
            collective_id=0, has_side_effects=True, vmem_limit_bytes=VMEM_LIMIT_FRONT
        ),
    )(*operands)


def mixer_back_kernel(sizes, per_sequence, shares, *refs):
    (
        grad_after_in, grad_mixer_in, block_in_in, mixed, conv, normed_in, weight_in, low_in, in_first, in_second,
        taps_in, gain_first_in, got_front, got_rest, out_tiles, picks,
    ) = refs[:16]
    grad_input = refs[16]
    landings = refs[17:20]
    units_refs = refs[20:24]
    exchange_sems, seq_sems, local_sems = refs[24:26], refs[26:29], refs[29:32]
    rim_sem, load_sem = refs[32:34]
    got_out, got_in, results = refs[34], refs[35], refs[36:39]
    (
        rim_out, rim_in, grad_after, mixed_s, conv_s, in_w, grad_mixer, grad_mixed,
        low_in_back, in_tiles, block_in, normed, taps, gain_first, chosen_t,
    ) = refs[39:]
    fsdp_size, seq_size = sizes
    devices = fsdp_size * seq_size
    ring = Ring(fsdp_size)
    me = ring.me * seq_size + ring.x
    tokens, features = grad_mixer.shape
    slots = low_in.shape[1]
    sequences = tokens // per_sequence
    block = min(ROW_BLOCK, per_sequence)
    loads = [
        pltpu.make_async_copy(a, b, load_sem.at[k])
        for k, (a, b) in enumerate(
            (
                (grad_mixer_in, grad_mixer),
                (mixed, mixed_s),
                (conv, conv_s),
                (normed_in, normed),
                (weight_in, in_w),
                (block_in_in, block_in),
                (grad_after_in, grad_after),
            )
        )
    ]
    for copy in loads[:3]:
        copy.start()
    ring.greet(seq_size, devices)
    out_exchange, in_exchange = (
        Exchange(
            ring, seq_size, devices,
            functools.partial(lambda source, d: column_tiles(source, 0, 1, source.shape[1] // LANES, d, devices), source),
            got, exchange_sems[k],
        )
        for k, (source, got) in enumerate(((out_tiles, got_out), (in_tiles, got_in)))
    )
    out_exchange.start()
    total_slots = devices * slots

    def front_got(t):
        if t < 2:
            return got_front[t].reshape(total_slots, LANES)
        return got_rest[t - 2].reshape(total_slots, LANES)

    def front_first(t):
        return shares.is_first(t, me) if t < 2 else shares.is_first(2, me + (t - 2) * devices)

    def one_got(got):
        return lambda t: got[...].reshape(total_slots, LANES)

    sums = [
        Sum(ring, seq_size, k, landings[k], is_first, got, results[k], (seq_sems[k], local_sems[k]), units_refs)
        for k, (got, is_first) in enumerate(
            (
                (front_got, front_first),
                (one_got(got_out), lambda t: shares.is_first(3, me)),
                (one_got(got_in), lambda t: shares.is_first(4, me)),
            )
        )
    ]
    chosen_t[...] = picks[...].reshape(total_slots, LANES).astype(F32).T.astype(BF16)
    chosen = chosen_t[...]
    sums[0].add(chosen)
    taps[...] = taps_in[...].astype(F32)
    unroll_gain(gain_first, gain_first_in)
    parts = tokens // block

    def add_out():
        out_exchange.arrived()
        sums[1].add(chosen_t[...])

    begin_all, *front_steps = sums[0].groups()
    out_steps, in_steps = sums[1].groups(), sums[2].groups()

    def rows_of(r):
        return pl.ds(pl.multiple_of(r * block, block), block)

    def masked(r, values):
        row = r * block + lax.broadcasted_iota(jnp.int32, (block, slots), 0)
        column = lax.broadcasted_iota(jnp.int32, (block, slots), 1)
        return jnp.where(row // per_sequence == column // R, ADAPTER_SCALE * values, 0.0).astype(BF16)

    for copy in loads[:3]:
        copy.wait()
    for copy in loads[3:]:
        copy.start()
    middle = slice(features, 2 * features)
    for k in range(sequences):
        at = slice(k * per_sequence, k * per_sequence + 8)
        rim_out[k] = grad_mixer[at, :] * mixed_s[at, middle]
    rim = pltpu.make_async_remote_copy(
        src_ref=rim_out,
        dst_ref=rim_in,
        send_sem=rim_sem.at[0],
        recv_sem=rim_sem.at[1],
        device_id={"seq": lax.rem(ring.x + seq_size - 1, seq_size)},
        device_id_type=MESH,
    )
    rim.start()
    rim.wait_recv()
    inner = (ring.x < seq_size - 1).astype(F32)

    @pl.loop(0, parts)
    def _(r):
        run_tick([[]] * (parts - 1) + [begin_all], r)
        at = rows_of(r)
        back = grad_mixer[at, :]
        through = back * mixed_s[at, middle]
        after_at = pl.ds(pl.multiple_of(jnp.minimum((r + 1) * block, tokens - 8), 8), 8)
        beyond = grad_mixer[after_at, :] * mixed_s[after_at, middle]
        last = lax.rem((r + 1) * block, per_sequence) == 0
        beyond = jnp.where(last, rim_in[(r * block) // per_sequence] * inner, beyond)
        extended = jnp.concatenate([through, beyond], axis=0)
        gated = (
            taps[2:3, :] * through + taps[1:2, :] * extended[1 : block + 1] + taps[0:1, :] * extended[2 : block + 2]
        )
        grad_mixed[at, :features] = (gated * mixed_s[at, 2 * features :]).astype(BF16)
        grad_mixed[at, middle] = (back * conv_s[at, :]).astype(BF16)
        grad_mixed[at, 2 * features :] = (gated * mixed_s[at, :features]).astype(BF16)
        low_in_back[at, :] = masked(r, dot_nt(grad_mixed[at, :], in_second[...]))

    for copy in loads[3:]:
        copy.wait()
    in_tiles[:, features : 4 * features] = dot_tn(low_in[...], grad_mixed[...]).astype(BF16)
    in_tiles[:, :features] = dot_tn(low_in_back[...], normed[...]).astype(BF16)
    in_exchange.start()

    def finish(r):
        at = rows_of(r)
        rows = block_in[at, :].astype(F32)
        inverse = lax.rsqrt(jnp.mean(rows * rows, axis=-1, keepdims=True) + EPSILON)
        unit_rows = rows * inverse
        gradient = dot_nt(grad_mixed[at, :], in_w[...]) + dot_nt(low_in_back[at, :], in_first[...])
        scaled = gradient * gain_first[...]
        grad_input[at, :] = (
            grad_after[at, :]
            + inverse * (scaled - unit_rows * jnp.mean(scaled * unit_rows, axis=-1, keepdims=True))
        ).astype(BF16)

    def add_last():
        in_exchange.arrived()
        sums[2].add(chosen_t[...])

    def step_of(steps, k):
        return steps[k] if 0 <= k < len(steps) else []

    rest = []
    for k in range(len(front_steps) + len(in_steps) + parts):
        actions = [add_last] if k == parts - 2 else []
        actions += step_of(in_steps, k - parts + 1) + step_of(front_steps, k)
        actions += [add_out] if k == 0 else []
        rest.append(actions + step_of(out_steps, k - 1))

    @pl.loop(0, parts)
    def _(r):
        run_tick(rest[:parts], r)
        finish(r)

    for actions in rest[parts:]:
        for action in actions:
            action()
    for member in sums:
        member.unit.collect()
    for member in sums:
        member.drain()
    out_exchange.drain()
    in_exchange.drain()
    rim.wait_send()


def mixer_back(sizes, per_sequence, shares, operands):
    fsdp_size, seq_size = sizes
    devices = fsdp_size * seq_size
    tokens, features = operands[0].shape
    slots = operands[7].shape[1]
    sequences = tokens // per_sequence
    tiles = (2 + shares.per, 1, 1)
    return pl.pallas_call(
        functools.partial(mixer_back_kernel, sizes, per_sequence, shares),
        out_shape=(jax.ShapeDtypeStruct((tokens, features), BF16),)
        + tuple(jax.ShapeDtypeStruct((fsdp_size, seq_size, count, LANES, LANES), BF16) for count in tiles),
        in_specs=[ANYWHERE] * 7 + [IN_VMEM] * 9,
        out_specs=(IN_VMEM,) + (ANYWHERE,) * 3,
        scratch_shapes=unit_sems(3, fsdp_size // 2)
        + [pltpu.SemaphoreType.DMA((3,))] * 2
        + [pltpu.SemaphoreType.DMA((2, seq_size))] * 3
        + [pltpu.SemaphoreType.DMA((1,))] * 3
        + [
            pltpu.SemaphoreType.DMA((2,)),
            pltpu.SemaphoreType.DMA((7,)),
            pltpu.VMEM((devices, slots, LANES), BF16),
            pltpu.VMEM((devices, slots, LANES), BF16),
        ]
        + [pltpu.VMEM((count, LANES, LANES), BF16) for count in tiles]
        + [
            pltpu.VMEM((sequences, 8, features), F32),
            pltpu.VMEM((sequences, 8, features), F32),
            pltpu.VMEM((tokens, features), F32),
            pltpu.VMEM((tokens, 3 * features), F32),
            pltpu.VMEM((tokens, features), F32),
            pltpu.VMEM((features, 3 * features), BF16),
            pltpu.VMEM((tokens, features), F32),
            pltpu.VMEM((tokens, 3 * features), BF16),
            pltpu.VMEM((tokens, slots), BF16),
            pltpu.VMEM((slots, 4 * shares.narrow * LANES), BF16),
            pltpu.VMEM((tokens, features), BF16),
            pltpu.VMEM((tokens, features), BF16),
            pltpu.VMEM((3, features), F32),
            pltpu.VMEM((1, features), F32),
            pltpu.VMEM((LANES, devices * slots), BF16),
        ],
        compiler_params=pltpu.CompilerParams(
            collective_id=2, has_side_effects=True, vmem_limit_bytes=VMEM_LIMIT_FRONT
        ),
    )(*operands)


def spread_kernel(layout, *refs):
    count = len(layout)
    landings, kept, outs, kept_outs = refs[:3], refs[3:5], refs[5 : 5 + count], refs[5 + count : 7 + count]
    sources, held = refs[7 + count : 10 + count], refs[10 + count : 12 + count]
    staged, load_sem, out_sem = refs[12 + count : 12 + 2 * count], refs[-2], refs[-1]
    loads = [pltpu.make_async_copy(a, b, load_sem.at[k]) for k, (a, b) in enumerate(zip(landings + kept, sources + held))]
    for copy in loads:
        copy.start()
    stores = [pltpu.make_async_copy(a, b, out_sem.at[count + k]) for k, (a, b) in enumerate(zip(held, kept_outs))]
    for copy in loads[:3]:
        copy.wait()
    for k, (out, (first, runs)) in enumerate(zip(staged, layout)):
        for source, start, stride, offset, length in runs:

            @pl.loop(0, length)
            def _(j, source=sources[source], start=start, stride=stride, offset=offset, out=out, first=first):
                at = pl.ds(pl.multiple_of((offset + j) * LANES, LANES), LANES)
                tile = source[start + j * stride].astype(F32)
                if first:
                    out[at, :] = tile
                else:
                    out[:, at] = tile

        stores.append(pltpu.make_async_copy(out, outs[k], out_sem.at[k]))
        stores[-1].start()
        if k == 1:
            for j in range(2):
                loads[3 + j].wait()
                stores[j].start()
    for copy in stores:
        copy.wait()


def spread(shares, landings, kept):
    wide, narrow = shares.wide, shares.narrow
    places = shares.places()
    layout, shapes = [], []
    for name, count in (
        ("in_first", narrow),
        ("in_second", 3 * narrow),
        ("out_first", narrow),
        ("out_second", narrow),
        ("gate_first", narrow),
        ("gate_second", wide),
        ("up_first", narrow),
        ("up_second", wide),
        ("down_first", wide),
        ("down_second", narrow),
    ):
        runs, k = [], 0
        while k < count:
            source, start = places[(name, k)]
            stride, length = 1, 1
            if k + 1 < count and places[(name, k + 1)][0] == source:
                stride = places[(name, k + 1)][1] - start
            while k + length < count and places[(name, k + length)] == (source, start + length * stride):
                length += 1
            runs.append((source, start, stride, k, length))
            k += length
        first = name.endswith("first")
        layout.append((first, tuple(runs)))
        shapes.append(jax.ShapeDtypeStruct((count * LANES, LANES) if first else (LANES, count * LANES), F32))
    landings = [landing.reshape(-1, LANES, LANES) for landing in landings]
    kept_shapes = [jax.ShapeDtypeStruct(member.shape, member.dtype) for member in kept]
    return pl.pallas_call(
        functools.partial(spread_kernel, tuple(layout)),
        out_shape=tuple(shapes + kept_shapes),
        in_specs=[ANYWHERE] * 5,
        out_specs=(ANYWHERE,) * (len(shapes) + 2),
        scratch_shapes=[pltpu.VMEM(member.shape, member.dtype) for member in (*landings, *kept, *shapes)]
        + [pltpu.SemaphoreType.DMA((5,)), pltpu.SemaphoreType.DMA((len(shapes) + 2,))],
        compiler_params=pltpu.CompilerParams(vmem_limit_bytes=VMEM_LIMIT),
    )(*landings, *kept)


def per_device(
    block_input,
    output_grad,
    adapter_ids,
    in_weight,
    out_weight,
    gate_weight,
    up_weight,
    down_weight,
    conv_weight,
    first_gain,
    second_gain,
    infirst_adapter,
    insecond_adapter,
    outfirst_adapter,
    outsecond_adapter,
    gatefirst_adapter,
    gatesecond_adapter,
    upfirst_adapter,
    upsecond_adapter,
    downfirst_adapter,
    downsecond_adapter,
):
    batches, seq_count, local_len, features = block_input.shape
    sequences = batches * seq_count
    tokens = sequences * local_len
    fsdp_size, seq_size = lax.axis_size("fsdp"), lax.axis_size("seq")
    hidden_size = gate_weight.shape[1]
    shares = Shares(fsdp_size * seq_size, features, hidden_size)
    gain_first, gain_second = (gain.reshape(-1, LANES) for gain in (first_gain, second_gain))
    cotangent = output_grad.reshape(tokens, features)
    block_in = block_input.reshape(tokens, features)
    (
        grad_after, _, low_in, _, in_first, in_second, _, _, _,
        block_output, _, mixed_in, conv_out, _, normed, weight_in, _, _, _,
        grad_mixer, got_front, got_rest, out_tiles, picks,
    ) = front(
        (fsdp_size, seq_size),
        local_len,
        shares,
        (
            block_in,
            cotangent,
            adapter_ids,
            conv_weight,
            gain_first,
            gain_second,
            infirst_adapter,
            insecond_adapter,
            outfirst_adapter,
            outsecond_adapter,
            gatefirst_adapter,
            upfirst_adapter,
            downsecond_adapter,
            gatesecond_adapter,
            upsecond_adapter,
            downfirst_adapter,
            in_weight,
            out_weight,
            gate_weight,
            up_weight,
            down_weight,
        ),
    )
    grad_input, *landings = mixer_back(
        (fsdp_size, seq_size),
        local_len,
        shares,
        (
            grad_after,
            grad_mixer,
            block_in,
            mixed_in,
            conv_out,
            normed,
            weight_in,
            low_in,
            in_first,
            in_second,
            conv_weight,
            gain_first,
            got_front,
            got_rest,
            out_tiles,
            picks,
        ),
    )
    *gradients, block_output, grad_input = spread(shares, landings, (block_output, grad_input))
    shape = block_input.shape
    return (block_output.reshape(shape), grad_input.reshape(shape)) + tuple(gradients)


def solution(mesh):
    return jax.shard_map(
        per_device,
        mesh=mesh,
        in_specs=(
            P(None, "fsdp", "seq", None),
            P(None, "fsdp", "seq", None),
            P(None, "fsdp"),
            P("fsdp", None),
            P("fsdp", None),
            P("fsdp", None),
            P("fsdp", None),
            P("fsdp", None),
            P(),
            P(),
            P(),
            P(),
            P(),
            P(),
            P(),
            P(),
            P(),
            P(),
            P(),
            P(),
            P(),
        ),
        out_specs=(
            P(None, "fsdp", "seq", None),
            P(None, "fsdp", "seq", None),
            P(),
            P(),
            P(),
            P(),
            P(),
            P(),
            P(),
            P(),
            P(),
            P(),
        ),
        check_vma=False,
    )
```

```python
import functools

import jax
import jax.numpy as jnp
from jax import lax
from jax.experimental import pallas as pl
from jax.experimental.pallas import tpu as pltpu
from jax.sharding import PartitionSpec as P

R = 16
LANES = 128
EPSILON = 1e-05
ADAPTER_SCALE = 0.5
MESH = pl.DeviceIdType.MESH
BF16 = jnp.bfloat16
F32 = jnp.float32
VMEM_LIMIT = 62 * 1024 * 1024
FF_CHUNK = 512
ROW_BLOCK = 256
WIDE_BLOCK = 512
VMEM_LIMIT_FRONT = 63 * 1024 * 1024


def dot_nn(left, right):
    return jnp.dot(left, right, preferred_element_type=F32)


def dot_nt(left, right):
    return lax.dot_general(left, right, (((1,), (1,)), ((), ())), preferred_element_type=F32)


def dot_tn(left, right):
    return lax.dot_general(left, right, (((0,), (0,)), ((), ())), preferred_element_type=F32)


def when(condition, action):
    if isinstance(condition, bool):
        if condition:
            action()
    else:
        pl.when(condition)(action)


class Ring:
    def __init__(self, fsdp_size):
        self.count = fsdp_size // 2
        self.me = lax.axis_index("fsdp")
        self.core = lax.rem(self.me, 2)
        chip = self.me // 2
        self.grid = fsdp_size == 16
        if self.grid:
            z, y = chip // 2, lax.rem(chip, 2)
            self.place = y * z + (1 - y) * (7 - z)
        else:
            self.place = chip
        x = lax.axis_index("seq")
        self.x = x
        self.role = lax.rem(x, 2)
        self.to_next = {"fsdp": self.device(lax.rem(self.place + 1, self.count))}
        self.to_prev = {"fsdp": self.device(lax.rem(self.place + self.count - 1, self.count))}
        self.to_core = {"fsdp": self.me + 1 - 2 * self.core}
        self.to_seq = {"seq": x + 1 - 2 * self.role}

    def device(self, place):
        if self.grid:
            y = 1 - place // 4
            z = y * place + (1 - y) * (7 - place)
            return (z * 2 + y) * 2 + self.core
        return place * 2 + self.core

    def at_step(self, direction, step):
        if direction == 0:
            return self.device(lax.rem(self.place + self.count - step, self.count))
        return self.device(lax.rem(self.place + step, self.count))

    def target(self, k, seq_size, devices):
        d = lax.rem(self.me * seq_size + self.x + k, devices)
        return d, {"fsdp": d // seq_size, "seq": lax.rem(d, seq_size)}

    def greet(self, seq_size, devices):
        barrier = pltpu.get_barrier_semaphore()

        @pl.loop(1, devices)
        def _(k):
            device = self.target(k, seq_size, devices)[1]
            pl.semaphore_signal(barrier, inc=1, device_id=device, device_id_type=MESH)

        pl.semaphore_wait(barrier, devices - 1)


class Exchange:
    def __init__(self, ring, seq_size, devices, source, got, sems):
        self.ring, self.seq_size, self.devices = ring, seq_size, devices
        self.source, self.got, self.sems = source, got, sems
        self.me = ring.me * seq_size + ring.x

    def own(self):
        return pltpu.make_async_copy(self.source(self.me), self.got.at[self.me], self.sems.at[2])

    def start(self):
        self.own().start()

        @pl.loop(1, self.devices)
        def _(k):
            d, device = self.ring.target(k, self.seq_size, self.devices)
            pltpu.make_async_remote_copy(
                src_ref=self.source(d),
                dst_ref=self.got.at[self.me],
                send_sem=self.sems.at[0],
                recv_sem=self.sems.at[1],
                device_id=device,
                device_id_type=MESH,
            ).start()

    def all_pieces(self):
        others = self.got.at[pl.ds(0, self.devices - 1)]
        return pltpu.make_async_remote_copy(
            src_ref=others,
            dst_ref=others,
            send_sem=self.sems.at[0],
            recv_sem=self.sems.at[1],
            device_id=self.ring.to_next,
            device_id_type=MESH,
        )

    def arrived(self):
        self.own().wait()
        self.all_pieces().wait_recv()

    def drain(self):
        self.all_pieces().wait_send()


class Unit:
    def __init__(self, ring, number, spot, sems):
        self.ring, self.number, self.spot = ring, number, spot
        self.send, self.ring_sem, self.seq_sem, self.core_sem = sems
        half = ring.count // 2
        self.reaches = ((half, ring.count - 1 - half), (ring.count - 1 - half, half))
        self.steps = half
        self.others = ring.count - 1

    def copy(self, spot, slot, sem, device):
        return pltpu.make_async_remote_copy(
            src_ref=spot,
            dst_ref=spot,
            send_sem=self.send.at[self.number, slot],
            recv_sem=sem,
            device_id=device,
            device_id_type=MESH,
        )

    def arrived(self, spot, sem):
        self.copy(spot, 0, sem, self.ring.to_next).wait_recv()

    def own(self):
        ring, n = self.ring, self.number
        for slot, third in ((0, ring.role), (1, 2)):
            spot = self.spot(third, ring.me)
            self.copy(spot, 2 * slot, self.ring_sem.at[n, slot, 0], ring.to_next).start()
            self.copy(spot, 2 * slot + 1, self.ring_sem.at[n, slot, self.others - 1], ring.to_prev).start()
        for k, third in enumerate((ring.role, 1 - ring.role, 2)):
            self.copy(self.spot(third, ring.me), 4 + k, self.core_sem.at[n, third, 0], ring.to_core).start()

    def relay(self, step):
        ring, n, others = self.ring, self.number, self.others
        for slot, third in ((0, ring.role), (1, 2)):
            for direction in (0, 1):
                reach = self.reaches[slot][direction]
                lane = step - 1 if direction == 0 else others - step
                spot = self.spot(third, ring.at_step(direction, step))

                def forward(slot=slot, direction=direction, lane=lane, spot=spot):
                    onward = self.ring_sem.at[n, slot, lane + 1 - 2 * direction]
                    target = (ring.to_next, ring.to_prev)[direction]
                    self.copy(spot, 7 + slot * others + lane, onward, target).start()

                def take(slot=slot, third=third, reach=reach, lane=lane, spot=spot, forward=forward):
                    self.arrived(spot, self.ring_sem.at[n, slot, lane])
                    when(step < reach, forward)
                    if slot == 0:
                        self.copy(spot, 7 + 2 * others + lane, self.seq_sem.at[n, lane], ring.to_seq).start()
                    core = self.core_sem.at[n, third, 1 + lane]
                    self.copy(spot, 7 + (3 + slot) * others + lane, core, ring.to_core).start()

                when(step <= reach, take)

    def relay_seq(self, step):
        ring, n, others = self.ring, self.number, self.others
        third = 1 - ring.role
        for direction in (0, 1):
            reach = self.reaches[0][direction]
            lane = step - 1 if direction == 0 else others - step
            spot = self.spot(third, ring.at_step(direction, step))

            def take(lane=lane, spot=spot):
                self.arrived(spot, self.seq_sem.at[n, lane])
                core = self.core_sem.at[n, third, 1 + lane]
                self.copy(spot, 7 + 5 * others + lane, core, ring.to_core).start()

            when(step <= reach, take)

    def collect(self):
        for third in range(3):
            for lane in range(self.others + 1):
                self.arrived(self.spot(third, self.ring.me), self.core_sem.at[self.number, third, lane])

    def drain(self):
        ring, others = self.ring, self.others

        def done(third, slot):
            self.copy(self.spot(third, ring.me), slot, self.seq_sem.at[self.number, 0], ring.to_next).wait_send()

        for slot, third in ((0, 0), (1, 2)):
            done(third, 2 * slot)
            done(third, 2 * slot + 1)
            for direction in (0, 1):
                reach = self.reaches[slot][direction]
                for step in range(1, reach + 1):
                    lane = step - 1 if direction == 0 else others - step
                    if step < reach:
                        done(third, 7 + slot * others + lane)
                    done(third, 7 + (3 + slot) * others + lane)
        for lane in range(others):
            done(0, 7 + 2 * others + lane)
            done(0, 7 + 5 * others + lane)
        for k, third in enumerate((0, 0, 2)):
            done(third, 4 + k)


def unit_sems(units, count):
    return [
        pltpu.SemaphoreType.DMA((units, 7 + 6 * (count - 1))),
        pltpu.SemaphoreType.DMA((units, 2, count - 1)),
        pltpu.SemaphoreType.DMA((units, count - 1)),
        pltpu.SemaphoreType.DMA((units, 3, count)),
    ]


def move_in(moves, sems):
    inward = [pltpu.make_async_copy(a, b, sems.at[0, k]) for k, (a, b, _) in enumerate(moves)]
    outward = [pltpu.make_async_copy(b, c, sems.at[1, k]) for k, (_, b, c) in enumerate(moves)]
    for copy in inward:
        copy.start()
    for first, second in zip(inward, outward):
        first.wait()
        second.start()
    return outward


def row_spot(landing, rows, start, size, third, owner):
    return landing.at[pl.ds(owner * rows + start + third * size, size), :]


def column_spot(landing, rows, width, last, third, owner):
    size = last if isinstance(third, int) and third == 2 else width
    start = third * width if isinstance(third, int) else pl.multiple_of(third * width, LANES)
    return landing.at[pl.ds(owner * rows, rows), pl.ds(start, size)]


def down_pieces(down_rows):
    return 3 if down_rows % 288 == 0 else 1


def unroll_gain(out, rows):
    values = rows[...].astype(F32)
    for k in range(values.shape[0]):
        out[:, k * LANES : (k + 1) * LANES] = values[k : k + 1, :]


def in_spot(landing, rows, part, half, third, owner):
    start = pl.multiple_of(third * part + half * (part // 2), LANES)
    return landing.at[pl.ds(owner * rows, rows), pl.ds(start, part // 2)]


def chunk_spot(landing, rows, size, chunk, third, owner):
    start = pl.multiple_of((chunk * 3 + third) * size, LANES)
    return landing.at[:, pl.ds(owner * rows, rows), pl.ds(start, size)]


class Plan:
    LINK, CORE, DELAY, COST = 41e3, 200e3, 2.0, 0.15
    WINDOWS = (2, 10, 5, 2, 1.5, 10, 2, 4, 1.5, 1.5, 1.5, 8)

    def __init__(self, units, sizes):
        self.units, self.sizes = units, sizes
        self.now = 0.0
        self.free = {"next": 0.0, "prev": 0.0, "seq": 0.0, "core": 0.0}
        self.steps = units[0].steps
        self.owned = 0
        self.arrival, self.core, self.left, self.collected = {}, {}, {}, set()
        self.list = []

    def send(self, link, size):
        if size:
            rate = self.CORE if link == "core" else self.LINK
            self.free[link] = max(self.free[link], self.now) + size / rate
        return self.free[link] + self.DELAY

    def run_own(self):
        u = self.owned
        self.owned += 1
        shared, common = self.sizes[u]
        self.list.append(self.units[u].own)
        self.now += self.COST
        size = shared + common
        self.arrival[(u, "ring", 1)] = max(self.send("next", size), self.send("prev", size))
        self.core[u] = self.send("core", 2 * shared + common)
        self.left[u] = 2 * self.steps

    def run(self, key):
        u, kind, step = key
        del self.arrival[key]
        shared, common = self.sizes[u]
        unit = self.units[u]
        self.left[u] -= 1
        self.now += self.COST
        if kind == "seq":
            self.list.append(functools.partial(unit.relay_seq, step))
            lanes = sum(step <= reach for reach in unit.reaches[0])
            self.core[u] = max(self.core[u], self.send("core", lanes * shared))
            return
        self.list.append(functools.partial(unit.relay, step))
        across = inward = 0
        onward = []
        for size, reaches, is_shared in ((shared, unit.reaches[0], True), (common, unit.reaches[1], False)):
            for link, reach in zip(("next", "prev"), reaches):
                if step <= reach:
                    inward += size
                    across += size if is_shared else 0
                if step < reach:
                    onward.append(self.send(link, size))
        if onward:
            self.arrival[(u, "ring", step + 1)] = max(onward)
        self.arrival[(u, "seq", step)] = self.send("seq", across)
        self.core[u] = max(self.core[u], self.send("core", inward))

    def ready(self):
        return [key for key, at in sorted(self.arrival.items()) if at <= self.now]

    def pump(self):
        while True:
            keys = self.ready()
            if keys:
                self.run(keys[0])
            elif (
                self.owned < len(self.units)
                and max(self.free["next"], self.free["prev"]) - self.now < self.WINDOWS[self.owned % 12]
            ):
                self.run_own()
            else:
                return

    def can_collect(self, u):
        return u < self.owned and self.left[u] == 0 and self.core[u] <= self.now

    def collect(self, u):
        if u not in self.collected:
            self.collected.add(u)
            self.list.append(self.units[u].collect)
            self.now += self.COST

    def need(self, numbers):
        for u in numbers:
            if u in self.collected:
                continue
            while not self.can_collect(u):
                self.pump()
                if self.can_collect(u):
                    break
                if u < self.owned and self.left[u] == 0:
                    self.now = max(self.now, self.core[u])
                elif self.arrival:
                    self.now = max(self.now, min(self.arrival.values()))
                else:
                    self.run_own()
            self.collect(u)

    def take(self):
        taken, self.list = self.list, []
        return taken

    def tick(self, duration):
        self.pump()
        taken = self.take()
        self.now += duration
        return taken


def run_tick(lists, tick):
    for k, actions in enumerate(lists):
        if not actions:
            continue

        @pl.when(tick == k)
        def _(actions=actions):
            for action in actions:
                action()


def rms_unit(rows):
    inverse = lax.rsqrt(jnp.mean(rows * rows, axis=-1, keepdims=True) + EPSILON)
    return inverse, rows * inverse


def rms_back(scaled, inverse, unit_rows):
    return inverse * (scaled - unit_rows * jnp.mean(scaled * unit_rows, axis=-1, keepdims=True))


ANYWHERE = pl.BlockSpec(memory_space=pl.ANY)
IN_VMEM = pl.BlockSpec(memory_space=pltpu.VMEM)


class Shares:
    def __init__(self, devices, features, hidden_size):
        self.devices = devices
        self.wide, self.narrow = hidden_size // LANES, features // LANES
        self.chunk = FF_CHUNK // LANES
        self.per_chunk = 3 * self.chunk
        third = 3 * self.per_chunk
        names = ("down_first", "gate_second", "up_second")

        def of_third(k):
            return [
                (name, (3 * k + c) * self.chunk + i) for c in range(3) for name in names for i in range(self.chunk)
            ]

        def all_of(name, count):
            return [(name, i) for i in range(count)]

        self.used = min(third, devices)
        self.pitch = third
        sets = [of_third(0), of_third(1)]
        self.spare = [tiles[self.used :] for tiles in sets]
        sets = [tiles[: self.used] for tiles in sets]
        narrow = self.narrow
        rest = of_third(2) + all_of("gate_first", narrow) + all_of("up_first", narrow)
        rest += all_of("down_second", narrow) + self.spare[0] + self.spare[1]
        self.rest_all = len(rest)
        self.per = max(1, len(rest) // devices)
        self.rest_used = min(len(rest), self.per * devices)
        self.left = len(rest) - self.rest_used
        sets.append(rest[: self.rest_used])
        sets.append(rest[self.rest_used :] + all_of("out_first", narrow) + all_of("out_second", narrow))
        sets.append(all_of("in_first", narrow) + all_of("in_second", 3 * narrow))
        self.sets = sets
        self.rest_start = 2 * self.pitch
        self.grads_width = (self.rest_start + self.rest_all) * LANES

    def is_first(self, number, tile):
        flags = [name.endswith("first") for name, _ in self.sets[number]]
        found, start = tile < 0, 0
        for k in range(1, len(flags) + 1):
            if k == len(flags) or flags[k] != flags[start]:
                if flags[start]:
                    found = found | ((tile >= start) & (tile < k))
                start = k
        return found

    def places(self):
        found = {}
        for number, tiles in enumerate(self.sets):
            for k, tile in enumerate(tiles):
                if number == 2:
                    found[tile] = (0, (2 + self.per) * (k % self.devices) + 2 + k // self.devices)
                else:
                    found[tile] = (0, (2 + self.per) * k + number) if number < 2 else (number - 2, k)
        return found


def column_tiles(source, start, count, used, d, devices):
    if used // count < devices:
        d = lax.rem(d, used // count)
    return source.at[:, pl.ds(pl.multiple_of((start + d * count) * LANES, LANES), count * LANES)]


class Sum:
    def __init__(self, ring, seq_size, number, landing, is_first, got, result, sems, unit_sems_refs):
        self.ring, self.seq_size, self.landing = ring, seq_size, landing
        self.is_first, self.got, self.result = is_first, got, result
        self.seq_sem, self.local_sem = sems
        self.place = landing.at[ring.me, ring.x]
        self.unit = Unit(ring, number, self.spot, unit_sems_refs)

    def spot(self, third, owner):
        size = 32 if isinstance(third, int) and third == 2 else 48
        return self.landing.at[owner, :, :, pl.ds(third * 48, size), :]

    def add(self, chosen):
        tiles = self.result.shape[0]
        for t in range(tiles):
            tile = dot_nn(chosen, self.got(t))
            self.result[t] = jnp.where(self.is_first(t), tile.T, tile).astype(BF16)
        store = pltpu.make_async_copy(self.result, self.place, self.local_sem.at[0])
        store.start()
        store.wait()
        for k in range(1, self.seq_size):
            self.across(k).start()

    def across(self, k):
        return pltpu.make_async_remote_copy(
            src_ref=self.place,
            dst_ref=self.place,
            send_sem=self.seq_sem.at[0, k],
            recv_sem=self.seq_sem.at[1, k],
            device_id={"seq": lax.rem(self.ring.x + k, self.seq_size)},
            device_id_type=MESH,
        )

    def crossed(self):
        for k in range(1, self.seq_size):
            self.across(k).wait_recv()

    def groups(self):
        unit = self.unit
        found = [[self.crossed, unit.own], [functools.partial(unit.relay, 1)]]
        for step in range(2, unit.steps + 1):
            found.append([functools.partial(unit.relay, step), functools.partial(unit.relay_seq, step - 1)])
        return found + [[functools.partial(unit.relay_seq, unit.steps)]]

    def drain(self):
        self.unit.drain()
        for k in range(1, self.seq_size):
            self.across(k).wait_send()


def share_out(groups, ticks):
    cuts = [len(groups) * k // ticks for k in range(ticks + 1)]
    return [sum(groups[cuts[k] : cuts[k + 1]], []) for k in range(ticks)]


def front_kernel(sizes, per_sequence, shares, *refs):
    (
        block_any, cotangent_any, ids, taps_in, gain_first_in, gain_second_in,
        in_first, in_second, out_first, out_second, gate_first, up_first, down_second,
        gate_second, up_second, down_first, in_own, out_own, gate_own, up_own, down_own,
    ) = refs[:21]
    (
        grad_second, grads, low_in, low_out, in_first_s, in_second_s, out_first_s, out_second_s, pick_t,
        block_out, after_out, mixed_out, conv_out, mixer_out, normed_out, in_all, out_all, gu_all, down_all,
        grad_mixer_out, got_front, got_rest, out_tiles, picks,
    ) = refs[21:45]
    sems, local_sem, load_sem, stage_sem, rim_sem, out_sem = refs[45:49], refs[49], refs[50], refs[51], refs[52], refs[53]
    exchange_sems = refs[54 : 57 + shares.per]
    held = refs[57 + shares.per : 62 + shares.per]
    pick, taps, gain_first, gain_second, out_grads, block_in, cotangent, input_sem = refs[-8:]
    (
        total, wide, gate_w, up_w, down_w, normed, mixer, second, gate_up_first, first_down, second_gu, second_down,
        low_gu, grad_low_down, low_down, grad_low_gu, partial, rim_out, rim_in,
    ) = refs[62 + shares.per : -8]
    fsdp_size, seq_size = sizes
    ring = Ring(fsdp_size)
    rows, down_rows = gate_own.shape[0], down_own.shape[0]
    tokens, features = cotangent.shape
    hidden_size = gate_own.shape[1]
    chunks = hidden_size // FF_CHUNK
    sequences = tokens // per_sequence
    block = min(ROW_BLOCK, per_sequence)
    wide_block = min(WIDE_BLOCK, tokens)
    blocks, wide_blocks = tokens // block, tokens // wide_block
    slots = low_in.shape[1]
    mine = pl.ds(ring.me * rows, rows)
    moved = move_in(
        [
            (in_own, held[0], in_all.at[mine, :]),
            (out_own, held[1], out_all.at[mine, :]),
            (down_own, held[4], down_all.at[pl.ds(ring.me * down_rows, down_rows), :]),
            (gate_own, held[2], gu_all.at[0, mine, :]),
            (up_own, held[3], gu_all.at[1, mine, :]),
        ],
        local_sem,
    )
    stages = []
    for k in range(-(-hidden_size // features)):
        width = min(features, hidden_size - k * features)
        part, lanes = pl.ds(k * features, width), pl.ds(k * LANES, LANES)
        stages += [
            (gate_second.at[:, part], second.at[lanes, pl.ds(0, width)]),
            (up_second.at[:, part], normed.at[lanes, pl.ds(0, width)]),
            (down_first.at[part, :], mixer.at[pl.ds(0, width), lanes]),
        ]
    stages = [pltpu.make_async_copy(a, b, stage_sem.at[k]) for k, (a, b) in enumerate(stages)]
    stages.append(pltpu.make_async_copy(block_any, block_in, input_sem.at[0]))
    stages.append(pltpu.make_async_copy(cotangent_any, cotangent, input_sem.at[1]))
    for copy in stages:
        copy.start()
    devices = fsdp_size * seq_size
    ring.greet(seq_size, devices)

    part = in_all.shape[1] // 3
    out_x = 3 * features // 8
    unit_list, sizes_of = [], []

    def add_unit(spot, shared, common):
        unit_list.append(Unit(ring, len(unit_list), spot, sems))
        sizes_of.append((2 * shared, 2 * common))

    for k in range(2):
        add_unit(functools.partial(in_spot, in_all, rows, part, k), rows * part // 2, rows * part // 2)
    last_out = features - 2 * out_x
    add_unit(functools.partial(column_spot, out_all, rows, out_x, last_out), rows * out_x, rows * last_out)
    pieces = down_pieces(down_rows)
    for k in range(pieces):
        size = down_rows // pieces // 3
        add_unit(functools.partial(row_spot, down_all, down_rows, 3 * size * k, size), size * features, size * features)
    fixed = len(unit_list)
    comm_chunks = 2 * chunks // 3
    comm_size = hidden_size // comm_chunks // 3
    for k in range(comm_chunks):
        add_unit(functools.partial(chunk_spot, gu_all, rows, comm_size, k), 2 * rows * comm_size, 2 * rows * comm_size)
    plan = Plan(unit_list, sizes_of)

    def run_all(actions):
        for action in actions:
            action()

    for copy in moved:
        copy.wait()
    run_all(plan.tick(5.0))
    sequence_row = lax.broadcasted_iota(jnp.int32, (slots, LANES), 0)
    sequence_column = lax.broadcasted_iota(jnp.int32, (LANES, slots), 1)
    wanted_row, wanted_column = lax.rem(sequence_row, R), lax.rem(sequence_column, R)
    for k in range(sequences):
        base = ids[k % ids.shape[0], k // ids.shape[0]] * R
        wanted_row += jnp.where(sequence_row // R == k, base, 0)
        wanted_column += jnp.where(sequence_column // R == k, base, 0)
    pick_t[...] = (wanted_row == lax.broadcasted_iota(jnp.int32, (slots, LANES), 1)).astype(F32).astype(BF16)
    pick[...] = (wanted_column == lax.broadcasted_iota(jnp.int32, (LANES, slots), 0)).astype(F32).astype(BF16)
    taps[...] = taps_in[...].astype(F32)
    unroll_gain(gain_first, gain_first_in)
    unroll_gain(gain_second, gain_second_in)

    def rows_of(r, size=block):
        return pl.ds(pl.multiple_of(r * size, size), size)

    def masked(r, values, size=block):
        row = r * size + lax.broadcasted_iota(jnp.int32, (size, slots), 0)
        column = lax.broadcasted_iota(jnp.int32, (size, slots), 1)
        return jnp.where(row // per_sequence == column // R, ADAPTER_SCALE * values, 0.0).astype(BF16)

    for copy in stages:
        copy.wait()
    for k in range(-(-hidden_size // features)):
        width = min(features, hidden_size - k * features)
        at, lanes = slice(k * features, k * features + width), slice(k * LANES, (k + 1) * LANES)
        second_gu[0, :, at] = dot_nn(pick_t[...], second[lanes, :width]).astype(BF16)
        second_gu[1, :, at] = dot_nn(pick_t[...], normed[lanes, :width]).astype(BF16)
        first_down[at, :] = dot_nn(mixer[:width, lanes], pick[...]).astype(BF16)
    second_down[...] = dot_nn(pick_t[...], down_second[...]).astype(BF16)
    in_second_s[...] = dot_nn(pick_t[...], in_second[...]).astype(BF16)
    out_second_s[...] = dot_nn(pick_t[...], out_second[...]).astype(BF16)
    in_first_s[...] = dot_nn(in_first[...], pick[...]).astype(BF16)
    out_first_s[...] = dot_nn(out_first[...], pick[...]).astype(BF16)
    gate_up_first[0] = dot_nn(gate_first[...], pick[...]).astype(BF16)
    gate_up_first[1] = dot_nn(up_first[...], pick[...]).astype(BF16)
    lists = [plan.tick(0.9) for _ in range(blocks)]

    @pl.loop(0, blocks)
    def _(r):
        run_tick(lists, r)
        at = rows_of(r)
        normed_rows = (rms_unit(block_in[at, :].astype(F32))[1] * gain_first[...]).astype(BF16)
        normed[at, :] = normed_rows
        low_in[at, :] = masked(r, dot_nn(normed_rows, in_first_s[...]))
        grad_low_down[at, :] = masked(r, dot_nt(cotangent[at, :], second_down[...]))
        grad_second[at, :] = jnp.zeros((block, features), F32)

    low_down[...] = jnp.zeros_like(low_down)
    grad_low_gu[...] = jnp.zeros_like(grad_low_gu)
    plan.need((0, 1))
    run_all(plan.take())

    half = FF_CHUNK
    middle, last_part, conv_part = (slice(k * features, (k + 1) * features) for k in (1, 2, 3))
    in_loads = []
    for k in range(2):
        for part_number, buffer in ((0, gate_w), (1, up_w)):
            columns = pl.ds(part_number * features + k * half, half)
            in_loads.append(pltpu.make_async_copy(in_all.at[:, columns], buffer.at[k], load_sem.at[k, part_number]))
        place = in_all.at[pl.ds(k * half, half), pl.ds(2 * features, features)]
        in_loads.append(pltpu.make_async_copy(place, down_w.at[k], load_sem.at[k, 2]))
    for copy in in_loads:
        copy.start()
    run_all(plan.tick(2.0))
    for copy in in_loads:
        copy.wait()
    lists = [plan.tick(1.6) for _ in range(blocks)]

    @pl.loop(0, blocks)
    def _(r):
        run_tick(lists, r)
        at = rows_of(r)
        values, low = normed[at, :], low_in[at, :]
        for part_number, buffer in ((0, gate_w), (1, up_w)):
            for k in range(2):
                start = part_number * features + k * half
                columns = slice(start, start + half)
                wide[at, columns] = dot_nn(values, buffer[k]) + dot_nn(low, in_second_s[:, columns])
        wide[at, last_part] = (
            dot_nn(values[:, :half], down_w[0])
            + dot_nn(values[:, half:], down_w[1])
            + dot_nn(low, in_second_s[:, last_part])
        )

    plan.need((2,))
    run_all(plan.take())
    out_loads = [
        pltpu.make_async_copy(out_all.at[:, pl.ds(k * half, half)], gate_w.at[k], load_sem.at[k, 0]) for k in range(2)
    ]
    for copy in out_loads:
        copy.start()
    for k in range(sequences):
        at = slice((k + 1) * per_sequence - 8, (k + 1) * per_sequence)
        rim_out[k] = wide[at, :features] * wide[at, last_part]
    rim = pltpu.make_async_remote_copy(
        src_ref=rim_out,
        dst_ref=rim_in,
        send_sem=rim_sem.at[0],
        recv_sem=rim_sem.at[1],
        device_id={"seq": lax.rem(ring.x + 1, seq_size)},
        device_id_type=MESH,
    )
    rim.start()
    mixed_store = pltpu.make_async_copy(wide.at[:, pl.ds(0, 3 * features)], mixed_out, out_sem.at[0])
    mixed_store.start()
    normed_store = pltpu.make_async_copy(normed.at[pl.ds(0, tokens), :], normed_out, out_sem.at[1])
    normed_store.start()
    run_all(plan.tick(2.0))
    for copy in out_loads:
        copy.wait()
    rim.wait_recv()
    inner = (ring.x > 0).astype(F32)
    lists = [plan.tick(2.2) for _ in range(blocks)]

    @pl.loop(0, blocks)
    def _(r):
        run_tick(lists, r)
        at = rows_of(r)
        gated = wide[at, :features] * wide[at, last_part]
        before_at = pl.ds(pl.multiple_of(jnp.maximum(r * block - 8, 0), 8), 8)
        before = wide[before_at, :features] * wide[before_at, last_part]
        first = lax.rem(r * block, per_sequence) == 0
        before = jnp.where(first, rim_in[(r * block) // per_sequence] * inner, before)
        extended = jnp.concatenate([before, gated], axis=0)
        convolved = (
            taps[0:1, :] * extended[6 : block + 6] + taps[1:2, :] * extended[7 : block + 7] + taps[2:3, :] * gated
        )
        wide[at, conv_part] = convolved
        mixed = (wide[at, middle] * convolved).astype(BF16)
        mixer[at, :] = mixed
        low = masked(r, dot_nn(mixed, out_first_s[...]))
        low_out[at, :] = low
        branch = jnp.concatenate([dot_nn(mixed, gate_w[0]), dot_nn(mixed, gate_w[1])], axis=1)
        after = block_in[at, :].astype(F32) + (branch + dot_nn(low, out_second_s[...]))
        total[at, :] = after
        second_rows = (rms_unit(after)[1] * gain_second[...]).astype(BF16)
        second[at, :] = second_rows
        for k in range(2):
            low_gu[k, at, :] = masked(r, dot_nn(second_rows, gate_up_first[k]))

    stores = [
        pltpu.make_async_copy(wide.at[:, pl.ds(3 * features, features)], conv_out, out_sem.at[2]),
        pltpu.make_async_copy(mixer.at[pl.ds(0, tokens), :], mixer_out, out_sem.at[3]),
        pltpu.make_async_copy(total, after_out, out_sem.at[4]),
    ]
    for copy in stores:
        copy.start()
    plan.need(range(3, fixed))
    run_all(plan.take())

    def down_load(j, s):
        return pltpu.make_async_copy(down_all.at[rows_of(j, FF_CHUNK), :], down_w.at[s], load_sem.at[s, 2])

    def gu_loads(j, s):
        place = rows_of(j, FF_CHUNK)
        return (
            pltpu.make_async_copy(gu_all.at[0, :, place], gate_w.at[s], load_sem.at[s, 0]),
            pltpu.make_async_copy(gu_all.at[1, :, place], up_w.at[s], load_sem.at[s, 1]),
        )

    down_load(0, 0).start()
    mixed_store.wait()
    for copy in stores:
        copy.wait()
    lists = [plan.tick(1.7) for _ in range(chunks)]

    @pl.loop(0, chunks)
    def _(j):
        s = lax.rem(j, 2)

        @pl.when(j + 1 < chunks)
        def _():
            down_load(j + 1, 1 - s).start()

        down_load(j, s).wait()
        run_tick(lists, j)
        columns = rows_of(j, FF_CHUNK)

        @pl.loop(0, wide_blocks)
        def _(r):
            at = rows_of(r, wide_block)
            wide[at, columns] = dot_nt(cotangent[at, :], down_w[s]) + dot_nt(
                grad_low_down[at, :], first_down[columns, :]
            )

    def begin(j):
        for copy in (down_load(j, j % 2),) + gu_loads(j, j % 2):
            copy.start()

    def units_of(j):
        first, last = j * FF_CHUNK // (3 * comm_size), (j * FF_CHUNK + FF_CHUNK - 1) // (3 * comm_size)
        return range(fixed + first, fixed + last + 1)

    plan.need(units_of(0))
    plan.list.append(functools.partial(begin, 0))
    run_all(plan.tick(1.0))

    def tile_columns(start):
        return lambda d: column_tiles(grads, start, 1, shares.used, d, devices)

    sources = [tile_columns(k * shares.pitch) for k in range(2)]
    for k in range(shares.per):
        sources.append(
            functools.partial(
                lambda k, d: column_tiles(
                    grads, shares.rest_start + k * devices, 1, min(devices, shares.rest_used), d, devices
                ),
                k,
            )
        )
    sources.append(lambda d: pick_t)
    places = [got_front.at[0], got_front.at[1]] + [got_rest.at[k] for k in range(shares.per)] + [picks]
    exchanges = [
        Exchange(ring, seq_size, devices, source, place, exchange_sems[k])
        for k, (source, place) in enumerate(zip(sources, places))
    ]
    spare_slot = chunks % 2
    back_loads = [
        pltpu.make_async_copy(out_all.at[:, pl.ds(k * half, half)], buffer.at[spare_slot], load_sem.at[2, k])
        for k, buffer in enumerate((gate_w, up_w))
    ]
    back_loads.append(pltpu.make_async_copy(after_out, wide.at[:, pl.ds(0, features)], load_sem.at[2, 2]))

    def load_back():
        for copy in back_loads:
            copy.start()

    lists, begun = [], 0
    for tick in range(chunks * wide_blocks):
        j = tick // wide_blocks
        plan.pump()
        if begun == j and j + 1 < chunks:
            possible = all(u in plan.collected or plan.can_collect(u) for u in units_of(j + 1))
            if possible or (tick + 1) % wide_blocks == 0:
                plan.need(units_of(j + 1))
                plan.list.append(functools.partial(begin, j + 1))
                begun += 1
        if tick == (chunks - 2) * wide_blocks:
            plan.list += [exchanges[0].start, exchanges[-1].start]
        if tick == (chunks - 1) * wide_blocks:
            plan.list += [load_back, exchanges[1].start]
        lists.append(plan.tick(3.9))

    @pl.loop(0, chunks * wide_blocks)
    def _(tick):
        j, r = tick // wide_blocks, lax.rem(tick, wide_blocks)
        s = lax.rem(j, 2)
        columns = rows_of(j, FF_CHUNK)

        @pl.when(r == 0)
        def _():
            for copy in (down_load(j, s),) + gu_loads(j, s):
                copy.wait()
            partial[...] = jnp.zeros_like(partial)

        run_tick(lists, tick)
        at = rows_of(r, wide_block)
        values = second[at, :]
        lows = (grad_low_down[at, :], low_gu[0, at, :], low_gu[1, at, :])
        gate = dot_nn(values, gate_w[s]) + dot_nn(lows[1], second_gu[0, :, columns])
        up = dot_nn(values, up_w[s]) + dot_nn(lows[2], second_gu[1, :, columns])
        back = wide[at, columns]
        sigmoid = 1.0 / (1.0 + jnp.exp(-gate))
        active = gate * sigmoid
        hidden = (active * up).astype(BF16)
        grad_gate = (back * up * (sigmoid + active * (1.0 - sigmoid))).astype(BF16)
        grad_up = (back * active).astype(BF16)
        total[at, :] += dot_nn(hidden, down_w[s])
        grad_second[at, :] += dot_nt(grad_gate, gate_w[s]) + dot_nt(grad_up, up_w[s])
        low_down[at, :] += dot_nn(hidden, first_down[columns, :])
        grad_low_gu[0, at, :] += dot_nt(grad_gate, second_gu[0, :, columns])
        grad_low_gu[1, at, :] += dot_nt(grad_up, second_gu[1, :, columns])
        for k, right in enumerate((hidden, grad_gate, grad_up)):
            partial[k] += dot_tn(lows[k], right)

        @pl.when(r == wide_blocks - 1)
        def _():
            for k in range(3):
                start = (j // 3) * shares.pitch + lax.rem(j, 3) * shares.per_chunk + k * shares.chunk
                place = pl.ds(pl.multiple_of(start * LANES, LANES), FF_CHUNK)
                grads[:, place] = partial[k].astype(BF16)

    normed_store.wait()
    ready = 1 if shares.per > 1 and devices <= 3 * shares.per_chunk else 0
    for member in exchanges[2 : 2 + ready]:
        member.start()
    rest_tiles = shares.rest_start + 3 * shares.per_chunk
    base = rest_tiles * LANES

    @pl.loop(0, blocks)
    def _(r):
        at = rows_of(r)
        low = masked(r, low_down[at, :])
        grad_low_down[at, :] = low
        normed[at, :] = (total[at, :] + dot_nn(low, second_down[...])).astype(BF16)
        for k in range(2):
            back_low = masked(r, grad_low_gu[k, at, :])
            low_gu[k, at, :] = back_low
            grad_second[at, :] += dot_nt(back_low, gate_up_first[k])

    block_store = pltpu.make_async_copy(normed.at[pl.ds(0, tokens), :], block_out, out_sem.at[1])
    block_store.start()
    grads[:, base + 2 * features : base + 3 * features] = dot_tn(grad_low_down[...], cotangent[...]).astype(BF16)
    for k in range(2):
        columns = slice(base + k * features, base + (k + 1) * features)
        grads[:, columns] = dot_tn(low_gu[k], second[:tokens, :]).astype(BF16)
    start = base + 3 * features
    for k in range(2):
        width = len(shares.spare[k]) * LANES
        if width:
            spare = (k * shares.pitch + shares.used) * LANES
            grads[:, start : start + width] = grads[:, spare : spare + width]
            start += width
    for member in exchanges[2 + ready : 2 + shares.per]:
        member.start()

    for copy in back_loads:
        copy.wait()
    out_grads[...] = jnp.zeros_like(out_grads)

    @pl.loop(0, blocks)
    def _(r):
        at = rows_of(r)
        inverse, unit_rows = rms_unit(wide[at, :features])
        gradient = cotangent[at, :].astype(F32) + rms_back(
            grad_second[at, :] * gain_second[...], inverse, unit_rows
        )
        grad_second[at, :] = gradient
        rounded = gradient.astype(BF16)
        back_low = masked(r, dot_nt(rounded, out_second_s[...]))
        total[at, :] = (
            dot_nt(rounded[:, :half], gate_w[spare_slot])
            + dot_nt(rounded[:, half:], up_w[spare_slot])
            + dot_nt(back_low, out_first_s[...])
        )
        out_grads[0] += dot_tn(back_low, mixer[at, :])
        out_grads[1] += dot_tn(low_out[at, :], rounded)

    mixer_store = pltpu.make_async_copy(total, grad_mixer_out, out_sem.at[0])
    mixer_store.start()
    if shares.left:
        start = (shares.rest_start + shares.rest_used) * LANES
        out_tiles[:, : shares.left * LANES] = grads[:, start : start + shares.left * LANES]
    for k in range(2):
        start = shares.left * LANES + k * features
        out_tiles[:, start : start + features] = out_grads[k].astype(BF16)
    for unit in unit_list[:fixed]:
        unit.drain()

    @pl.loop(0, comm_chunks)
    def _(k):
        Unit(ring, fixed + k, functools.partial(chunk_spot, gu_all, rows, comm_size, k), sems).drain()

    rim.wait_send()
    block_store.wait()
    mixer_store.wait()
    for member in exchanges:
        member.arrived()
    for member in exchanges:
        member.drain()


def front(sizes, per_sequence, shares, operands):
    fsdp_size, seq_size = sizes
    cotangent, ids = operands[1:3]
    own = operands[-5:]
    tokens, features = cotangent.shape
    hidden_size = own[2].shape[1]
    sequences = ids.shape[0] * ids.shape[1]
    slots = sequences * R
    units = 3 + down_pieces(own[4].shape[0]) + 2 * (hidden_size // FF_CHUNK) // 3
    tall = max(tokens, features)
    stages = 3 * -(-hidden_size // features)

    def shape(*dims, kind=BF16):
        return jax.ShapeDtypeStruct(dims, kind)

    return pl.pallas_call(
        functools.partial(front_kernel, sizes, per_sequence, shares),
        out_shape=(
            shape(tokens, features, kind=F32),
            shape(slots, shares.grads_width),
            shape(tokens, slots),
            shape(tokens, slots),
            shape(features, slots),
            shape(slots, 3 * features),
            shape(features, slots),
            shape(slots, features),
            shape(slots, LANES),
            shape(tokens, features),
            shape(tokens, features, kind=F32),
            shape(tokens, 3 * features, kind=F32),
            shape(tokens, features, kind=F32),
            shape(tokens, features),
            shape(tokens, features),
            shape(features, 3 * features),
            shape(features, features),
            shape(2, features, hidden_size),
            shape(hidden_size, features),
            shape(tokens, features, kind=F32),
            shape(2, shares.devices, slots, LANES),
            shape(shares.per, shares.devices, slots, LANES),
            shape(slots, (shares.left + 2 * shares.narrow) * LANES),
            shape(shares.devices, slots, LANES),
        ),
        in_specs=[ANYWHERE] * 2 + [pl.BlockSpec(memory_space=pltpu.SMEM)] + [IN_VMEM] * 10 + [ANYWHERE] * 8,
        out_specs=(IN_VMEM,) * 9 + (ANYWHERE,) * 13 + (IN_VMEM, ANYWHERE),
        scratch_shapes=unit_sems(units, fsdp_size // 2)
        + [
            pltpu.SemaphoreType.DMA((2, 5)),
            pltpu.SemaphoreType.DMA((3, 3)),
            pltpu.SemaphoreType.DMA((stages,)),
            pltpu.SemaphoreType.DMA((2,)),
            pltpu.SemaphoreType.DMA((5,)),
        ]
        + [pltpu.SemaphoreType.DMA((3,))] * (3 + shares.per)
        + [pltpu.VMEM(member.shape, BF16) for member in own]
        + [
            pltpu.VMEM((tokens, features), F32),
            pltpu.VMEM((tokens, hidden_size), F32),
            pltpu.VMEM((2, features, FF_CHUNK), BF16),
            pltpu.VMEM((2, features, FF_CHUNK), BF16),
            pltpu.VMEM((2, FF_CHUNK, features), BF16),
            pltpu.VMEM((tall, features), BF16),
            pltpu.VMEM((tall, features), BF16),
            pltpu.VMEM((tall, features), BF16),
            pltpu.VMEM((2, features, slots), BF16),
            pltpu.VMEM((hidden_size, slots), BF16),
            pltpu.VMEM((2, slots, hidden_size), BF16),
            pltpu.VMEM((slots, features), BF16),
            pltpu.VMEM((2, tokens, slots), BF16),
            pltpu.VMEM((tokens, slots), BF16),
            pltpu.VMEM((tokens, slots), F32),
            pltpu.VMEM((2, tokens, slots), F32),
            pltpu.VMEM((3, slots, FF_CHUNK), F32),
            pltpu.VMEM((sequences, 8, features), F32),
            pltpu.VMEM((sequences, 8, features), F32),
            pltpu.VMEM((LANES, slots), BF16),
            pltpu.VMEM((3, features), F32),
            pltpu.VMEM((1, features), F32),
            pltpu.VMEM((1, features), F32),
            pltpu.VMEM((2, slots, features), F32),
            pltpu.VMEM((tokens, features), BF16),
            pltpu.VMEM((tokens, features), BF16),
            pltpu.SemaphoreType.DMA((2,)),
        ],
        compiler_params=pltpu.CompilerParams(
            collective_id=0, has_side_effects=True, vmem_limit_bytes=VMEM_LIMIT_FRONT
        ),
    )(*operands)


def mixer_back_kernel(sizes, per_sequence, shares, *refs):
    (
        grad_after_in, grad_mixer_in, block_in_in, mixed, conv, normed_in, weight_in, low_in, in_first, in_second,
        taps_in, gain_first_in, got_front, got_rest, out_tiles, picks,
    ) = refs[:16]
    grad_input = refs[16]
    landings = refs[17:20]
    units_refs = refs[20:24]
    exchange_sems, seq_sems, local_sems = refs[24:26], refs[26:29], refs[29:32]
    rim_sem, load_sem = refs[32:34]
    got_out, got_in, results = refs[34], refs[35], refs[36:39]
    (
        rim_out, rim_in, grad_after, mixed_s, conv_s, in_w, grad_mixer, grad_mixed,
        low_in_back, in_tiles, block_in, normed, taps, gain_first, chosen_t,
    ) = refs[39:]
    fsdp_size, seq_size = sizes
    devices = fsdp_size * seq_size
    ring = Ring(fsdp_size)
    me = ring.me * seq_size + ring.x
    tokens, features = grad_mixer.shape
    slots = low_in.shape[1]
    sequences = tokens // per_sequence
    block = min(ROW_BLOCK, per_sequence)
    loads = [
        pltpu.make_async_copy(a, b, load_sem.at[k])
        for k, (a, b) in enumerate(
            (
                (grad_mixer_in, grad_mixer),
                (mixed, mixed_s),
                (conv, conv_s),
                (normed_in, normed),
                (weight_in, in_w),
                (block_in_in, block_in),
                (grad_after_in, grad_after),
            )
        )
    ]
    for copy in loads[:3]:
        copy.start()
    ring.greet(seq_size, devices)
    out_exchange, in_exchange = (
        Exchange(
            ring, seq_size, devices,
            functools.partial(lambda source, d: column_tiles(source, 0, 1, source.shape[1] // LANES, d, devices), source),
            got, exchange_sems[k],
        )
        for k, (source, got) in enumerate(((out_tiles, got_out), (in_tiles, got_in)))
    )
    out_exchange.start()
    total_slots = devices * slots

    def front_got(t):
        if t < 2:
            return got_front[t].reshape(total_slots, LANES)
        return got_rest[t - 2].reshape(total_slots, LANES)

    def front_first(t):
        return shares.is_first(t, me) if t < 2 else shares.is_first(2, me + (t - 2) * devices)

    def one_got(got):
        return lambda t: got[...].reshape(total_slots, LANES)

    sums = [
        Sum(ring, seq_size, k, landings[k], is_first, got, results[k], (seq_sems[k], local_sems[k]), units_refs)
        for k, (got, is_first) in enumerate(
            (
                (front_got, front_first),
                (one_got(got_out), lambda t: shares.is_first(3, me)),
                (one_got(got_in), lambda t: shares.is_first(4, me)),
            )
        )
    ]
    chosen_t[...] = picks[...].reshape(total_slots, LANES).astype(F32).T.astype(BF16)
    chosen = chosen_t[...]
    sums[0].add(chosen)
    taps[...] = taps_in[...].astype(F32)
    unroll_gain(gain_first, gain_first_in)
    parts = tokens // block

    def add_out():
        out_exchange.arrived()
        sums[1].add(chosen_t[...])

    begin_all, *front_steps = sums[0].groups()
    out_steps, in_steps = sums[1].groups(), sums[2].groups()

    def rows_of(r):
        return pl.ds(pl.multiple_of(r * block, block), block)

    def masked(r, values):
        row = r * block + lax.broadcasted_iota(jnp.int32, (block, slots), 0)
        column = lax.broadcasted_iota(jnp.int32, (block, slots), 1)
        return jnp.where(row // per_sequence == column // R, ADAPTER_SCALE * values, 0.0).astype(BF16)

    for copy in loads[:3]:
        copy.wait()
    for copy in loads[3:]:
        copy.start()
    middle = slice(features, 2 * features)
    for k in range(sequences):
        at = slice(k * per_sequence, k * per_sequence + 8)
        rim_out[k] = grad_mixer[at, :] * mixed_s[at, middle]
    rim = pltpu.make_async_remote_copy(
        src_ref=rim_out,
        dst_ref=rim_in,
        send_sem=rim_sem.at[0],
        recv_sem=rim_sem.at[1],
        device_id={"seq": lax.rem(ring.x + seq_size - 1, seq_size)},
        device_id_type=MESH,
    )
    rim.start()
    rim.wait_recv()
    inner = (ring.x < seq_size - 1).astype(F32)

    @pl.loop(0, parts)
    def _(r):
        run_tick([[]] * (parts - 1) + [begin_all], r)
        at = rows_of(r)
        back = grad_mixer[at, :]
        through = back * mixed_s[at, middle]
        after_at = pl.ds(pl.multiple_of(jnp.minimum((r + 1) * block, tokens - 8), 8), 8)
        beyond = grad_mixer[after_at, :] * mixed_s[after_at, middle]
        last = lax.rem((r + 1) * block, per_sequence) == 0
        beyond = jnp.where(last, rim_in[(r * block) // per_sequence] * inner, beyond)
        extended = jnp.concatenate([through, beyond], axis=0)
        gated = (
            taps[2:3, :] * through + taps[1:2, :] * extended[1 : block + 1] + taps[0:1, :] * extended[2 : block + 2]
        )
        grad_mixed[at, :features] = (gated * mixed_s[at, 2 * features :]).astype(BF16)
        grad_mixed[at, middle] = (back * conv_s[at, :]).astype(BF16)
        grad_mixed[at, 2 * features :] = (gated * mixed_s[at, :features]).astype(BF16)
        low_in_back[at, :] = masked(r, dot_nt(grad_mixed[at, :], in_second[...]))

    for copy in loads[3:]:
        copy.wait()
    in_tiles[:, features : 4 * features] = dot_tn(low_in[...], grad_mixed[...]).astype(BF16)
    in_tiles[:, :features] = dot_tn(low_in_back[...], normed[...]).astype(BF16)
    in_exchange.start()

    def finish(r):
        at = rows_of(r)
        rows = block_in[at, :].astype(F32)
        inverse = lax.rsqrt(jnp.mean(rows * rows, axis=-1, keepdims=True) + EPSILON)
        unit_rows = rows * inverse
        gradient = dot_nt(grad_mixed[at, :], in_w[...]) + dot_nt(low_in_back[at, :], in_first[...])
        scaled = gradient * gain_first[...]
        grad_input[at, :] = (
            grad_after[at, :]
            + inverse * (scaled - unit_rows * jnp.mean(scaled * unit_rows, axis=-1, keepdims=True))
        ).astype(BF16)

    def add_last():
        in_exchange.arrived()
        sums[2].add(chosen_t[...])

    def step_of(steps, k):
        return steps[k] if 0 <= k < len(steps) else []

    rest = []
    for k in range(len(front_steps) + len(in_steps) + parts):
        actions = [add_last] if k == parts - 2 else []
        actions += step_of(in_steps, k - parts + 1) + step_of(front_steps, k)
        actions += [add_out] if k == 0 else []
        rest.append(actions + step_of(out_steps, k - 1))

    @pl.loop(0, parts)
    def _(r):
        run_tick(rest[:parts], r)
        finish(r)

    for actions in rest[parts:]:
        for action in actions:
            action()
    for member in sums:
        member.unit.collect()
    for member in sums:
        member.drain()
    out_exchange.drain()
    in_exchange.drain()
    rim.wait_send()


def mixer_back(sizes, per_sequence, shares, operands):
    fsdp_size, seq_size = sizes
    devices = fsdp_size * seq_size
    tokens, features = operands[0].shape
    slots = operands[7].shape[1]
    sequences = tokens // per_sequence
    tiles = (2 + shares.per, 1, 1)
    return pl.pallas_call(
        functools.partial(mixer_back_kernel, sizes, per_sequence, shares),
        out_shape=(jax.ShapeDtypeStruct((tokens, features), BF16),)
        + tuple(jax.ShapeDtypeStruct((fsdp_size, seq_size, count, LANES, LANES), BF16) for count in tiles),
        in_specs=[ANYWHERE] * 7 + [IN_VMEM] * 9,
        out_specs=(IN_VMEM,) + (ANYWHERE,) * 3,
        scratch_shapes=unit_sems(3, fsdp_size // 2)
        + [pltpu.SemaphoreType.DMA((3,))] * 2
        + [pltpu.SemaphoreType.DMA((2, seq_size))] * 3
        + [pltpu.SemaphoreType.DMA((1,))] * 3
        + [
            pltpu.SemaphoreType.DMA((2,)),
            pltpu.SemaphoreType.DMA((7,)),
            pltpu.VMEM((devices, slots, LANES), BF16),
            pltpu.VMEM((devices, slots, LANES), BF16),
        ]
        + [pltpu.VMEM((count, LANES, LANES), BF16) for count in tiles]
        + [
            pltpu.VMEM((sequences, 8, features), F32),
            pltpu.VMEM((sequences, 8, features), F32),
            pltpu.VMEM((tokens, features), F32),
            pltpu.VMEM((tokens, 3 * features), F32),
            pltpu.VMEM((tokens, features), F32),
            pltpu.VMEM((features, 3 * features), BF16),
            pltpu.VMEM((tokens, features), F32),
            pltpu.VMEM((tokens, 3 * features), BF16),
            pltpu.VMEM((tokens, slots), BF16),
            pltpu.VMEM((slots, 4 * shares.narrow * LANES), BF16),
            pltpu.VMEM((tokens, features), BF16),
            pltpu.VMEM((tokens, features), BF16),
            pltpu.VMEM((3, features), F32),
            pltpu.VMEM((1, features), F32),
            pltpu.VMEM((LANES, devices * slots), BF16),
        ],
        compiler_params=pltpu.CompilerParams(
            collective_id=2, has_side_effects=True, vmem_limit_bytes=VMEM_LIMIT_FRONT
        ),
    )(*operands)


def spread_kernel(layout, *refs):
    count = len(layout)
    landings, kept, outs, kept_outs = refs[:3], refs[3:5], refs[5 : 5 + count], refs[5 + count : 7 + count]
    sources, held = refs[7 + count : 10 + count], refs[10 + count : 12 + count]
    staged, load_sem, out_sem = refs[12 + count : 12 + 2 * count], refs[-2], refs[-1]
    loads = [pltpu.make_async_copy(a, b, load_sem.at[k]) for k, (a, b) in enumerate(zip(landings + kept, sources + held))]
    for copy in loads:
        copy.start()
    stores = [pltpu.make_async_copy(a, b, out_sem.at[count + k]) for k, (a, b) in enumerate(zip(held, kept_outs))]
    for copy in loads[:3]:
        copy.wait()
    for k, (out, (first, runs)) in enumerate(zip(staged, layout)):
        for source, start, stride, offset, length in runs:

            @pl.loop(0, length)
            def _(j, source=sources[source], start=start, stride=stride, offset=offset, out=out, first=first):
                at = pl.ds(pl.multiple_of((offset + j) * LANES, LANES), LANES)
                tile = source[start + j * stride].astype(F32)
                if first:
                    out[at, :] = tile
                else:
                    out[:, at] = tile

        stores.append(pltpu.make_async_copy(out, outs[k], out_sem.at[k]))
        stores[-1].start()
        if k == 1:
            for j in range(2):
                loads[3 + j].wait()
                stores[j].start()
    for copy in stores:
        copy.wait()


def spread(shares, landings, kept):
    wide, narrow = shares.wide, shares.narrow
    places = shares.places()
    layout, shapes = [], []
    for name, count in (
        ("in_first", narrow),
        ("in_second", 3 * narrow),
        ("out_first", narrow),
        ("out_second", narrow),
        ("gate_first", narrow),
        ("gate_second", wide),
        ("up_first", narrow),
        ("up_second", wide),
        ("down_first", wide),
        ("down_second", narrow),
    ):
        runs, k = [], 0
        while k < count:
            source, start = places[(name, k)]
            stride, length = 1, 1
            if k + 1 < count and places[(name, k + 1)][0] == source:
                stride = places[(name, k + 1)][1] - start
            while k + length < count and places[(name, k + length)] == (source, start + length * stride):
                length += 1
            runs.append((source, start, stride, k, length))
            k += length
        first = name.endswith("first")
        layout.append((first, tuple(runs)))
        shapes.append(jax.ShapeDtypeStruct((count * LANES, LANES) if first else (LANES, count * LANES), F32))
    landings = [landing.reshape(-1, LANES, LANES) for landing in landings]
    kept_shapes = [jax.ShapeDtypeStruct(member.shape, member.dtype) for member in kept]
    return pl.pallas_call(
        functools.partial(spread_kernel, tuple(layout)),
        out_shape=tuple(shapes + kept_shapes),
        in_specs=[ANYWHERE] * 5,
        out_specs=(ANYWHERE,) * (len(shapes) + 2),
        scratch_shapes=[pltpu.VMEM(member.shape, member.dtype) for member in (*landings, *kept, *shapes)]
        + [pltpu.SemaphoreType.DMA((5,)), pltpu.SemaphoreType.DMA((len(shapes) + 2,))],
        compiler_params=pltpu.CompilerParams(vmem_limit_bytes=VMEM_LIMIT),
    )(*landings, *kept)


def per_device(
    block_input,
    output_grad,
    adapter_ids,
    in_weight,
    out_weight,
    gate_weight,
    up_weight,
    down_weight,
    conv_weight,
    first_gain,
    second_gain,
    infirst_adapter,
    insecond_adapter,
    outfirst_adapter,
    outsecond_adapter,
    gatefirst_adapter,
    gatesecond_adapter,
    upfirst_adapter,
    upsecond_adapter,
    downfirst_adapter,
    downsecond_adapter,
):
    batches, seq_count, local_len, features = block_input.shape
    sequences = batches * seq_count
    tokens = sequences * local_len
    fsdp_size, seq_size = lax.axis_size("fsdp"), lax.axis_size("seq")
    hidden_size = gate_weight.shape[1]
    shares = Shares(fsdp_size * seq_size, features, hidden_size)
    gain_first, gain_second = (gain.reshape(-1, LANES) for gain in (first_gain, second_gain))
    cotangent = output_grad.reshape(tokens, features)
    block_in = block_input.reshape(tokens, features)
    (
        grad_after, _, low_in, _, in_first, in_second, _, _, _,
        block_output, _, mixed_in, conv_out, _, normed, weight_in, _, _, _,
        grad_mixer, got_front, got_rest, out_tiles, picks,
    ) = front(
        (fsdp_size, seq_size),
        local_len,
        shares,
        (
            block_in,
            cotangent,
            adapter_ids.T,
            conv_weight,
            gain_first,
            gain_second,
            infirst_adapter,
            insecond_adapter,
            outfirst_adapter,
            outsecond_adapter,
            gatefirst_adapter,
            upfirst_adapter,
            downsecond_adapter,
            gatesecond_adapter,
            upsecond_adapter,
            downfirst_adapter,
            in_weight,
            out_weight,
            gate_weight,
            up_weight,
            down_weight,
        ),
    )
    grad_input, *landings = mixer_back(
        (fsdp_size, seq_size),
        local_len,
        shares,
        (
            grad_after,
            grad_mixer,
            block_in,
            mixed_in,
            conv_out,
            normed,
            weight_in,
            low_in,
            in_first,
            in_second,
            conv_weight,
            gain_first,
            got_front,
            got_rest,
            out_tiles,
            picks,
        ),
    )
    *gradients, block_output, grad_input = spread(shares, landings, (block_output, grad_input))
    shape = block_input.shape
    return (block_output.reshape(shape), grad_input.reshape(shape)) + tuple(gradients)


def solution(mesh):
    return jax.shard_map(
        per_device,
        mesh=mesh,
        in_specs=(
            P(None, "fsdp", "seq", None),
            P(None, "fsdp", "seq", None),
            P(None, "fsdp"),
            P("fsdp", None),
            P("fsdp", None),
            P("fsdp", None),
            P("fsdp", None),
            P("fsdp", None),
            P(),
            P(),
            P(),
            P(),
            P(),
            P(),
            P(),
            P(),
            P(),
            P(),
            P(),
            P(),
            P(),
        ),
        out_specs=(
            P(None, "fsdp", "seq", None),
            P(None, "fsdp", "seq", None),
            P(),
            P(),
            P(),
            P(),
            P(),
            P(),
            P(),
            P(),
            P(),
            P(),
        ),
        check_vma=False,
    )
```
